256 devices in a mesh: gx: 8 (over x, core), gy: 4 (over y), gz: 8 (over z).
Axes of the slice: x: 4, y: 4, z: 8, core: 2. Of those that a mesh axis runs over, the one named last changes fastest.
Arguments:
- right_side: float32 [192, 128, 1024], P('gx', 'gy', 'gz'), may hold values from -6 to 6
- conductance: float32 [192, 128, 1024], P('gx', 'gy', 'gz'), may hold values from 0.05 to 10
- absorption: float32 [192, 128, 1024], P('gx', 'gy', 'gz'), may hold values from 0.002 to 0.02
- block_agg: int32 [96, 64, 512], P('gx', 'gy', 'gz'), may hold values from 0 to 127, as said below
Outputs:
- solution: float32 [192, 128, 1024], P('gx', 'gy', 'gz')
The draws below stay inside these ranges and needn't reach their ends.
Inputs may be any that keep to these rules, and one draw needn't show every extreme that they name: `block_agg`: aggregates never leave their brick; in every brick each number 0 to 127 names at least one block.
All inputs are finite; a program needn't handle non-finite values.
Results may differ from the reference program's by a relative error of at most 0.0003.
Values sent between devices are 32-bit elements; how exact they have to be, the bound alone decides.
A program may use at most 128 MiB of HBM per device.

```python
import math
import jax
import jax.numpy as jnp

CX = 24
CY = 32
CZ = 128
RXY = 4
RZ = 8
AGG = 128
PRE = 2
POST = 4
KC = 8
NX = 192
NY = 128
NZ = 1024
N_GX = 8
N_GY = 4
N_GZ = 8


def draw_block_agg(key, part):
    span_y = CY // 2
    span_z = CZ // 2
    bands_z = RXY * RZ
    jitter = jax.random.randint(key, (2, NX // 2, NY // 2, NZ // 2), -1, 2, dtype=jnp.int32)
    local_x = (jnp.arange(NX // 2, dtype=jnp.int32) % (CX // 2))[:, None, None]
    local_y = (jnp.arange(NY // 2, dtype=jnp.int32) % span_y)[None, :, None]
    local_z = (jnp.arange(NZ // 2, dtype=jnp.int32) % span_z)[None, None, :]
    keep_plane = (local_x == 0).astype(jnp.int32)
    shift_y = jitter[0] * (1 - keep_plane)
    shift_z = jitter[1] * (1 - keep_plane)
    region_y = jnp.clip(local_y + shift_y, 0, span_y - 1) * RXY // span_y
    region_z = jnp.clip(local_z + shift_z, 0, span_z - 1) * bands_z // span_z
    return (region_y * bands_z + region_z).astype(jnp.int32)


def draw_conductance(key, part):
    key_lines = jax.random.fold_in(key, 11)
    key_fibre = jax.random.fold_in(key, 12)
    key_matrix = jax.random.fold_in(key, 13)
    lines = jax.random.randint(key_lines, (1, NY, NZ), 0, 10, dtype=jnp.int32) < 3
    fibre = jnp.exp(jax.random.uniform(key_fibre, (NX, NY, NZ), jnp.float32, math.log(2.0), math.log(10.0)))
    matrix = jnp.exp(jax.random.uniform(key_matrix, (NX, NY, NZ), jnp.float32, math.log(0.05), math.log(0.2)))
    return jnp.clip(jnp.where(lines, fibre, matrix), 0.05, 10.0).astype(jnp.float32)


def level_of(own_key, dims, split, least, high):
    loudness = 1.0
    for position, shards_of in split:
        draws = jax.random.uniform(jax.random.fold_in(jax.random.fold_in(own_key, 6), position), (shards_of,), jnp.float32, least / len(split), high / len(split))
        loudness = loudness * jnp.repeat(jnp.exp(draws), dims[position] // shards_of).reshape((-1,) + (1,) * (len(dims) - 1 - position))
    return loudness


def gaussian(own_key, extent, scale, limit, shards=(), kind=jnp.bfloat16):
    values = scale * jax.random.normal(own_key, extent, jnp.float32)
    if shards:
        values = values * level_of(own_key, extent, shards, -0.22, 0.18)
    return jnp.clip(values, -limit, limit).astype(kind)


def setup_inputs(seed: int = 0) -> dict:
    keys = jax.random.split(jax.random.key(seed), 5)
    right_side = gaussian(keys[0], (NX, NY, NZ), 1.0, 6.0, ((0, 8), (1, 4), (2, 8)), jnp.float32)
    conductance = draw_conductance(jax.random.fold_in(keys[4], 71), 0)
    absorption = jnp.clip(jnp.exp(math.log(0.02) - 2.30258502 * jax.random.uniform(keys[2], (NX, NY, NZ), jnp.float32) ** level_of(keys[2], (NX, NY, NZ), ((0, 8), (1, 4), (2, 8)), -0.2, 0.2)), 0.002, 0.02)
    block_agg = draw_block_agg(jax.random.fold_in(keys[4], 71), 0)
    return dict(right_side=right_side, conductance=conductance, absorption=absorption, block_agg=block_agg)


OMEGA_FINE = 0.8
OMEGA_COARSE = 0.7


def harmonic(one_side, other_side):
    return 2.0 * (one_side * other_side) / (one_side + other_side)


def block_sum(values):
    size_a, size_b, size_c = values.shape
    return values.reshape(size_a // 2, 2, size_b // 2, 2, size_c // 2, 2).sum(axis=(1, 3, 5))


def upsample(values):
    size_a, size_b, size_c = values.shape
    spread = jnp.broadcast_to(values[:, None, :, None, :, None], (size_a, 2, size_b, 2, size_c, 2))
    return spread.reshape(2 * size_a, 2 * size_b, 2 * size_c)


def neighbour_sum(values, face_x, face_y, face_z):
    padded = jnp.pad(values, 1)
    beside = face_x[1:] * padded[2:, 1:-1, 1:-1] + face_x[:-1] * padded[:-2, 1:-1, 1:-1]
    beside = beside + face_y[:, 1:] * padded[1:-1, 2:, 1:-1] + face_y[:, :-1] * padded[1:-1, :-2, 1:-1]
    beside = beside + face_z[:, :, 1:] * padded[1:-1, 1:-1, 2:] + face_z[:, :, :-1] * padded[1:-1, 1:-1, :-2]
    return beside


def reference(right_side, conductance, absorption, block_agg):
    pad_x = jnp.pad(conductance, ((1, 1), (0, 0), (0, 0)))
    pad_y = jnp.pad(conductance, ((0, 0), (1, 1), (0, 0)))
    pad_z = jnp.pad(conductance, ((0, 0), (0, 0), (1, 1)))
    face_x = harmonic(pad_x[:-1], pad_x[1:])
    face_y = harmonic(pad_y[:, :-1], pad_y[:, 1:])
    face_z = harmonic(pad_z[:, :, :-1], pad_z[:, :, 1:])
    cell_diag = absorption + face_x[:-1] + face_x[1:] + face_y[:, :-1] + face_y[:, 1:] + face_z[:, :, :-1] + face_z[:, :, 1:]

    def fine_apply(values):
        return cell_diag * values - neighbour_sum(values, face_x, face_y, face_z)

    def smooth(values, sweeps):
        for repeat_no in range(sweeps):
            values = values + OMEGA_FINE * (right_side - fine_apply(values)) / cell_diag
        return values

    presmoothed = smooth(jnp.zeros_like(right_side), PRE)
    residual = right_side - fine_apply(presmoothed)

    blocks_x, blocks_y, blocks_z = block_agg.shape
    brick_x = jnp.arange(blocks_x, dtype=jnp.int32) // (CX // 2)
    brick_y = jnp.arange(blocks_y, dtype=jnp.int32) // (CY // 2)
    brick_z = jnp.arange(blocks_z, dtype=jnp.int32) // (CZ // 2)
    brick_ids = (brick_x[:, None, None] * N_GY + brick_y[None, :, None]) * N_GZ + brick_z[None, None, :]
    global_ids = (brick_ids * AGG + block_agg).astype(jnp.int32)
    coarse_count = AGG * N_GX * N_GY * N_GZ

    def aggregate_sum(values, labels):
        return jax.ops.segment_sum(values.reshape(-1), labels.reshape(-1), num_segments=coarse_count)

    block_x = face_x[0::2].reshape(blocks_x + 1, blocks_y, 2, blocks_z, 2).sum(axis=(2, 4))
    block_y = face_y[:, 0::2].reshape(blocks_x, 2, blocks_y + 1, blocks_z, 2).sum(axis=(1, 4))
    block_z = face_z[:, :, 0::2].reshape(blocks_x, 2, blocks_y, 2, blocks_z + 1).sum(axis=(1, 3))
    block_absorb = block_sum(absorption)
    block_diag = block_absorb + block_x[:-1] + block_x[1:] + block_y[:, :-1] + block_y[:, 1:] + block_z[:, :, :-1] + block_z[:, :, 1:]

    coarse_diag = aggregate_sum(block_absorb, global_ids)
    pairs = [(global_ids[:-1], global_ids[1:], block_x[1:-1]),
             (global_ids[:, :-1], global_ids[:, 1:], block_y[:, 1:-1]),
             (global_ids[:, :, :-1], global_ids[:, :, 1:], block_z[:, :, 1:-1])]
    for low_ids, high_ids, cut_weights in pairs:
        crossing = jnp.where(low_ids != high_ids, cut_weights, 0.0)
        coarse_diag = coarse_diag + aggregate_sum(crossing, low_ids) + aggregate_sum(crossing, high_ids)

    def coarse_apply(coarse_vec):
        block_vec = coarse_vec[global_ids]
        applied = block_diag * block_vec - neighbour_sum(block_vec, block_x, block_y, block_z)
        return aggregate_sum(applied, global_ids)

    coarse_rhs = aggregate_sum(block_sum(residual), global_ids)
    correction = jnp.zeros((coarse_count,), jnp.float32)
    for turn_no in range(KC):
        correction = correction + OMEGA_COARSE * (coarse_rhs - coarse_apply(correction)) / coarse_diag
    corrected = presmoothed + upsample(correction[global_ids])
    return smooth(corrected, POST)
```

```python
import jax
import jax.numpy as jnp
from jax import lax
from jax.experimental import pallas as pl
from jax.experimental.pallas import tpu as pltpu
from jax.sharding import PartitionSpec as P

AGG = 128
POST = 4
KC = 8
OMEGA_FINE = 0.8
OMEGA_COARSE = 0.7
CX, CY, CZ = 24, 32, 128
BX = CX // 2
TOP = 8
END = TOP + CY
AXES = ("gx", "gy", "gz")
F32 = jnp.float32
BF16 = jnp.bfloat16
NT = (((1,), (1,)), ((), ()))


def harmonic(one_side, other_side):
    summed = one_side + other_side
    return 2.0 * (one_side * other_side) / summed


def safe_harmonic(one_side, other_side):
    summed = one_side + other_side
    return 2.0 * (one_side * other_side) / jnp.where(summed > 0.0, summed, 1.0)


def lanes_of(shape):
    return lax.broadcasted_iota(jnp.int32, shape, 1)


def rows_of(shape):
    return lax.broadcasted_iota(jnp.int32, shape, 0)


def lane_roll(values, shift):
    return pltpu.roll(values, shift % CZ if isinstance(shift, int) else shift, 1)


def row_roll(values, shift):
    return pltpu.roll(values, shift % values.shape[0], 0)


def pack(low, high, plane, x):
    lane = lanes_of((8, CZ))
    for g in range(4):
        k = 4 * x + g
        piece = plane[8 * g : 8 * g + 8]
        low = jnp.where(lane == k, lane_roll(piece, k), low)
        high = jnp.where(lane == k, lane_roll(piece, k + 1), high)
    return low, high


def unpack_low(packed, x):
    return jnp.concatenate([lane_roll(packed, lax.rem(CZ - (4 * x + g), CZ)) for g in range(4)], axis=0)


def unpack_high(packed, x):
    return jnp.concatenate([lane_roll(packed, CZ - 1 - (4 * x + g)) for g in range(4)], axis=0)


def quad_sum(values):
    pair = values + row_roll(values, -1)
    return pair + lane_roll(pair, -1)


def squeeze_cells(values):
    even = (lanes_of(values.shape) & 1) == 0
    return jnp.where(even, values, lane_roll(row_roll(values, -2), 1))


def split(values):
    high = values.astype(BF16).astype(F32)
    return high, values - high


def spread_row(row):
    return jnp.broadcast_to(row, (16, CZ)).astype(BF16)


def kernel(
    b_hbm, k_hbm, a_hbm, l_hbm, out_hbm,
    bv, av, kp, lv, v, gw, c0, dg, lc, el, ew,
    kzs, kzh, lxh, lys, lyh, lzs, lzh, zs, zh,
    wxf, wyf, fzf, xs, ys, acc, mf, mm, cs, ch,
    local_sem, send_sem, recv_sem,
):
    pos = [lax.axis_index(a) for a in AXES]
    size = [lax.axis_size(a) for a in AXES]
    has = []
    dev = []
    for axis in range(3):
        has.append(pos[axis] > 0)
        dev.append({AXES[axis]: pos[axis] - 1})
        has.append(pos[axis] < size[axis] - 1)
        dev.append({AXES[axis]: pos[axis] + 1})

    def exchange_of(kind, slot):
        if kind == "k":
            src = [kp.at[1, TOP:END], kp.at[CX, TOP:END], kp.at[1 : CX + 1, TOP : TOP + 1],
                   kp.at[1 : CX + 1, END - 1 : END], kzs.at[0], kzs.at[1]]
            dst = [kp.at[0, TOP:END], kp.at[CX + 1, TOP:END], kp.at[1 : CX + 1, TOP - 1 : TOP],
                   kp.at[1 : CX + 1, END : END + 1], kzh.at[0], kzh.at[1]]
            sem = 0
        elif kind == "l":
            src = [lc.at[0, TOP:END], lc.at[BX - 1, TOP:END], lys.at[0], lys.at[1], lzs.at[0], lzs.at[1]]
            dst = [lxh.at[0], lxh.at[1], lyh.at[0], lyh.at[1], lzh.at[0], lzh.at[1]]
            sem = 1
        elif kind == "v":
            src = [v.at[slot, 1, TOP:END], v.at[slot, CX, TOP:END], v.at[slot, 1 : CX + 1, TOP : TOP + 1],
                   v.at[slot, 1 : CX + 1, END - 1 : END], zs.at[slot, 0], zs.at[slot, 1]]
            dst = [v.at[slot, 0, TOP:END], v.at[slot, CX + 1, TOP:END], v.at[slot, 1 : CX + 1, TOP - 1 : TOP],
                   v.at[slot, 1 : CX + 1, END : END + 1], zh.at[slot, 0], zh.at[slot, 1]]
            sem = 2 + slot
        else:
            src = [cs.at[slot]] * 6
            dst = [ch.at[slot, d] for d in range(6)]
            sem = 4 + slot
        return src, dst, sem

    def copy_to(kind, slot, d):
        src, dst, sem = exchange_of(kind, slot)
        return pltpu.make_async_remote_copy(
            src[d], dst[d ^ 1], send_sem.at[sem, d], recv_sem.at[sem, d ^ 1],
            device_id=dev[d], device_id_type=pl.DeviceIdType.MESH)

    def copy_from(kind, slot, d):
        src, dst, sem = exchange_of(kind, slot)
        return pltpu.make_async_remote_copy(
            src[d], dst[d], send_sem.at[sem, d], recv_sem.at[sem, d],
            device_id=dev[d], device_id_type=pl.DeviceIdType.MESH)

    def start(kind, slot=0, sides=range(6)):
        for d in sides:
            @pl.when(has[d])
            def _():
                copy_to(kind, slot, d).start()

    def finish(kind, slot=0):
        for d in range(6):
            @pl.when(has[d])
            def _():
                copy_from(kind, slot, d).wait_recv()
        for d in range(6):
            @pl.when(has[d])
            def _():
                copy_to(kind, slot, d).wait_send()

    load_k = pltpu.make_async_copy(k_hbm, kp.at[1 : CX + 1, TOP:END], local_sem.at[0])
    load_l = pltpu.make_async_copy(l_hbm, lv, local_sem.at[1])
    load_a = pltpu.make_async_copy(a_hbm, av, local_sem.at[2])
    load_b = pltpu.make_async_copy(b_hbm, bv, local_sem.at[3])
    load_k.start()
    load_l.start()
    load_a.start()
    load_b.start()

    zero_plane = jnp.zeros((CY, CZ), F32)
    zero_tile = jnp.zeros((8, CZ), F32)
    for edge in (0, CX + 1):
        kp[edge, TOP:END] = zero_plane
        v[0, edge, TOP:END] = zero_plane
        v[1, edge, TOP:END] = zero_plane
    for side in range(2):
        lxh[side] = zero_plane
        lyh[side] = jnp.zeros((16, CZ), F32)
        lys[side] = jnp.zeros((16, CZ), F32)
        wyf[side] = jnp.zeros((16, CZ), F32)
        kzh[side] = zero_tile
        lzh[side] = zero_tile
        for slot in range(2):
            zh[slot, side] = zero_tile
    for slot in range(2):
        for d in range(6):
            ch[slot, d] = zero_tile

    def clear_rows(x, carry):
        for edge in (TOP - 8, END):
            kp[x + 1, edge : edge + 8] = zero_tile
            v[0, x + 1, edge : edge + 8] = zero_tile
            v[1, x + 1, edge : edge + 8] = zero_tile
        return carry

    lax.fori_loop(0, CX, clear_rows, 0)

    barrier = pltpu.get_barrier_semaphore()
    count = jnp.int32(0)
    for d in range(6):
        @pl.when(has[d])
        def _():
            pl.semaphore_signal(barrier, inc=1, device_id=dev[d], device_id_type=pl.DeviceIdType.MESH)
        count = count + has[d].astype(jnp.int32)
    pl.semaphore_wait(barrier, count)

    load_k.wait()
    start("k", 0, range(4))

    def pack_k(x, carry):
        return pack(*carry, kp[x + 1, TOP:END], x)

    kz_low, kz_high = lax.fori_loop(0, CX, pack_k, (zero_tile, zero_tile))
    kzs[0] = kz_low
    kzs[1] = kz_high
    start("k", 0, (4, 5))

    load_l.wait()
    labels = lv[...].reshape(BX * 16, 64).astype(F32).astype(BF16)
    widen = jnp.where(lanes_of((64, CZ)) // 2 == rows_of((64, CZ)), 1.0, 0.0).astype(BF16)
    wide = jnp.dot(labels, widen, preferred_element_type=F32).astype(BF16)
    tall_shape = (BX * CY, BX * 16)
    heighten = jnp.where(rows_of(tall_shape) // 2 == lanes_of(tall_shape), 1.0, 0.0).astype(BF16)
    cells = jnp.dot(heighten, wide, preferred_element_type=F32)
    for x in range(BX):
        lc[x, TOP:END] = cells[x * CY : (x + 1) * CY]
        lc[x, END : END + 8] = zero_tile
        lys[0, x : x + 1] = cells[x * CY : x * CY + 1]
        lys[1, x : x + 1] = cells[x * CY + CY - 1 : x * CY + CY]

    def pack_l(block, carry):
        plane = lc[block, TOP:END]
        return pack(*pack(*carry, plane, 2 * block), plane, 2 * block + 1)

    lz_low, lz_high = lax.fori_loop(0, BX, pack_l, (zero_tile, zero_tile))
    lzs[0] = lz_low
    lzs[1] = lz_high
    start("l")

    load_a.wait()
    load_b.wait()
    finish("k")

    lane = lanes_of((CY, CZ))
    row = rows_of((CY, CZ))
    fzf[0] = safe_harmonic(kzs[0], kzh[0])
    fzf[1] = safe_harmonic(kzs[1], kzh[1])

    def coefficients(x, fx_low):
        centre = kp[x + 1, TOP:END]
        fx_high = harmonic(centre, kp[x + 2, TOP:END])
        fy_low = harmonic(kp[x + 1, TOP - 1 : END - 1], centre)
        last = harmonic(centre[CY - 8 :], kp[x + 1, END - 7 : END + 1])
        last = jnp.concatenate([last] * 4, axis=0)
        fy_high = jnp.where(row == CY - 1, last, row_roll(fy_low, -1))
        fz_low = harmonic(lane_roll(centre, 1), centre)
        fz_low = jnp.where(lane == 0, unpack_low(fzf[0], x), fz_low)
        fz_high = jnp.where(lane == CZ - 1, unpack_high(fzf[1], x), lane_roll(fz_low, -1))
        diag = av[x] + fx_low + fx_high + fy_low + fy_high + fz_low + fz_high
        scale = OMEGA_FINE / diag
        for n, face in enumerate((fx_low, fx_high, fy_low, fy_high, fz_low, fz_high)):
            gw[n, x] = scale * face
        first = scale * bv[x]
        c0[x] = first
        dg[x] = diag
        v[0, x + 1, TOP:END] = first
        return first, fx_high, fy_low, fy_high, fz_high

    def block_step(block, carry):
        fx_low, low, high = carry
        x = 2 * block
        first_0, fx_mid, fy_low_0, fy_high_0, fz_high_0 = coefficients(x, fx_low)
        low, high = pack(low, high, first_0, x)
        first_1, fx_high, fy_low_1, fy_high_1, fz_high_1 = coefficients(x + 1, fx_mid)
        low, high = pack(low, high, first_1, x + 1)
        wx = quad_sum(fx_high)
        wy = fy_high_0 + fy_high_1
        wy = row_roll(wy + lane_roll(wy, -1), -1)
        wz = fz_high_0 + fz_high_1
        wz = lane_roll(wz + row_roll(wz, -1), -1)
        wa = 0.5 * quad_sum(av[x] + av[x + 1])
        wy_low = (fy_low_0 + fy_low_1)[0:1]
        wyf[0, pl.ds(block, 1)] = wy_low + lane_roll(wy_low, -1)
        wyf[1, pl.ds(block, 1)] = wy[CY - 2 : CY - 1]
        own = lc[block, TOP:END]
        lx = lc[jnp.minimum(block + 1, BX - 1), TOP:END]
        ly = lc[block, TOP + 2 : END + 2]
        lz = lane_roll(own, -2)
        lx = jnp.where(lx == own, -1.0, lx)
        ly = jnp.where((ly == own) | (row >= CY - 2), -1.0, ly)
        lz = jnp.where((lz == own) | (lane >= CZ - 2), -1.0, lz)
        same = ly == lx
        wx = wx + jnp.where(same, wy, 0.0)
        ly = jnp.where(same, -1.0, ly)
        same = lz == lx
        wx = wx + jnp.where(same, wz, 0.0)
        lz = jnp.where(same, -1.0, lz)
        same = lz == ly
        wy = wy + jnp.where(same, wz, 0.0)
        lz = jnp.where(same, -1.0, lz)
        for n, field in enumerate((own, lx, ly, lz)):
            el[n, block] = squeeze_cells(field)
        for n, field in enumerate((wa, wx, wy, wz)):
            ew[n, block] = squeeze_cells(field)
        return fx_high, low, high

    fx_first = harmonic(kp[0, TOP:END], kp[1, TOP:END])
    wxf[0] = quad_sum(fx_first)
    fx_last, z_low, z_high = lax.fori_loop(0, BX, block_step, (fx_first, zero_tile, zero_tile))
    wxf[1] = quad_sum(fx_last)
    zs[0, 0] = z_low
    zs[0, 1] = z_high
    start("v", 0)

    number = rows_of((16, CZ)).astype(F32)
    numbers = [(number + 16.0 * q).astype(BF16) for q in range(8)]
    one = jnp.ones((16, CZ), BF16)
    zero = jnp.zeros((16, CZ), BF16)

    def place(at, lhs_label, pairs):
        lhs_label = spread_row(lhs_label)
        spread = []
        for label, weight in pairs:
            high, low = split(weight)
            spread.append((spread_row(label), spread_row(high), spread_row(low)))
        for q in range(8):
            xs[16 * q : 16 * q + 16, at : at + CZ] = jnp.where(lhs_label == numbers[q], one, zero)
            y_high = zero
            y_low = zero
            for label, high, low in spread:
                hit = label == numbers[q]
                y_high = jnp.where(hit, high, y_high)
                y_low = jnp.where(hit, low, y_low)
            ys[16 * q : 16 * q + 16, at : at + CZ] = y_high
            ys[AGG + 16 * q : AGG + 16 * q + 16, at : at + CZ] = y_low

    acc[...] = jnp.zeros((AGG, 2 * AGG), F32)

    def own_step(block, carry):
        for m in range(8):
            rows = slice(4 * m, 4 * m + 1)
            pairs = [(el[n, block, rows], ew[n, block, rows]) for n in range(4)]
            place(m * CZ, pairs[0][0], pairs)
        acc[...] += lax.dot_general(xs[...], ys[...], NT, preferred_element_type=F32)
        return carry

    lax.fori_loop(0, BX, own_step, 0)
    half = acc[:, :AGG] + acc[:, AGG:]
    mf[0:AGG] = half + half.T

    def neighbours(slot, x):
        centre = v[slot, x + 1, TOP:END]
        z_low = jnp.where(lane == 0, unpack_low(zh[slot, 0], x), lane_roll(centre, 1))
        z_high = jnp.where(lane == CZ - 1, unpack_high(zh[slot, 1], x), lane_roll(centre, -1))
        total = c0[x]
        total = total + gw[0, x] * v[slot, x, TOP:END] + gw[1, x] * v[slot, x + 2, TOP:END]
        total = total + gw[2, x] * v[slot, x + 1, TOP - 1 : END - 1]
        total = total + gw[3, x] * v[slot, x + 1, TOP + 1 : END + 1]
        total = total + gw[4, x] * z_low + gw[5, x] * z_high
        return centre, total

    def sweep(slot, other):
        def step(x, carry):
            centre, total = neighbours(slot, x)
            new = total + (1.0 - OMEGA_FINE) * centre
            v[other, x + 1, TOP:END] = new
            return pack(*carry, new, x)

        low, high = lax.fori_loop(0, CX, step, (zero_tile, zero_tile))
        zs[other, 0] = low
        zs[other, 1] = high

    finish("v", 0)
    sweep(0, 1)
    start("v", 1)

    finish("l")

    def face(d, peer, own, weight, rows):
        for n, r in enumerate(rows):
            at = slice(r, r + 1)
            place(n * CZ, peer[at], [(own[at], weight[at])])
        depth = len(rows) * CZ
        tile = lax.dot_general(xs[:, :depth], ys[:, :depth], NT, preferred_element_type=F32)
        mf[AGG * (d + 1) : AGG * (d + 2)] = tile[:, :AGG] + tile[:, AGG:]

    def pair_rows(values):
        even = (lanes_of(values.shape) & 1) == 0
        return jnp.where(even, values, lane_roll(row_roll(values, -1), 1))

    def pair_packed(values):
        even = (lanes_of(values.shape) & 4) == 0
        return jnp.where(even, values, lane_roll(row_roll(values, -2), 4))

    for side in range(2):
        face(side, squeeze_cells(lxh[side]), squeeze_cells(lc[side * (BX - 1), TOP:END]),
             squeeze_cells(wxf[side]), range(0, CY, 4))
        face(2 + side, pair_rows(lyh[side]), pair_rows(lys[side]), pair_rows(wyf[side]), range(0, BX, 2))
        wz = fzf[side] + lane_roll(fzf[side], -4)
        wz = pair_packed(wz + row_roll(wz, -1))
        wz = jnp.where(lanes_of((8, CZ)) < 4 * CX, wz, 0.0)
        face(4 + side, pair_packed(lzh[side]), pair_packed(lzs[side]), wz, (0, 4))

    def add_rows(block, total):
        return total + mf[pl.ds(pl.multiple_of(8 * block, 8), 8), :]

    coarse_diag = jnp.sum(lax.fori_loop(0, 7 * AGG // 8, add_rows, zero_tile), axis=0, keepdims=True)
    coarse_scale = OMEGA_COARSE / coarse_diag
    square = (AGG, AGG)
    mf[0:AGG] = jnp.where(rows_of(square) == lanes_of(square), 0.0, mf[0:AGG])
    for t in range(7):
        high, low = split(mf[AGG * t : AGG * (t + 1)])
        mm[AGG * t : AGG * (t + 1), :AGG] = high.astype(BF16)
        mm[AGG * t : AGG * (t + 1), AGG:] = low.astype(BF16)

    finish("v", 1)

    def residual_step(block, carry):
        total = zero_plane
        for x in (2 * block, 2 * block + 1):
            centre, image = neighbours(1, x)
            total = total + dg[x] * (image * (1.0 / OMEGA_FINE) - centre)
        ew[0, block] = squeeze_cells(quad_sum(total))
        return carry

    lax.fori_loop(0, BX, residual_step, 0)
    wanted = rows_of((AGG, CZ)).astype(F32)

    def restrict_step(block, sums):
        for m in range(8):
            rows = slice(4 * m, 4 * m + 1)
            label = jnp.broadcast_to(el[0, block, rows], (AGG, CZ))
            value = jnp.broadcast_to(ew[0, block, rows], (AGG, CZ))
            sums = sums + jnp.where(label == wanted, value, 0.0)
        return sums

    sums = lax.fori_loop(0, BX, restrict_step, jnp.zeros((AGG, CZ), F32))
    coarse_rhs = lax.dot_general(
        jnp.ones((8, CZ), F32), sums, NT, preferred_element_type=F32, precision=lax.Precision.HIGHEST)

    small_row = rows_of((8, CZ))

    def coarse_step(turn, correction):
        slot = lax.rem(turn, 2)
        high, low = split(correction)
        tile = jnp.where(small_row == 0, high, jnp.where(small_row == 1, low, 0.0))
        cs[slot] = tile
        start("c", slot)
        image = jnp.dot(tile.astype(BF16), mm[0:AGG], preferred_element_type=F32)
        finish("c", slot)
        beside = jnp.concatenate([ch[slot, d] for d in range(6)], axis=1).astype(BF16)
        image = image + jnp.dot(beside, mm[AGG:], preferred_element_type=F32)
        image = jnp.sum(image[:, :AGG] + image[:, AGG:], axis=0, keepdims=True)
        return (1.0 - OMEGA_COARSE) * correction + coarse_scale * (coarse_rhs + image)

    correction = lax.fori_loop(0, KC - 1, coarse_step, coarse_scale * coarse_rhs)

    def lift_step(block, carry):
        index = lc[block, TOP:END].astype(jnp.int32)
        lifted = jnp.concatenate(
            [jnp.take_along_axis(correction, index[8 * g : 8 * g + 8], axis=1, mode="promise_in_bounds")
             for g in range(4)], axis=0)
        for x in (2 * block, 2 * block + 1):
            new = v[1, x + 1, TOP:END] + lifted
            v[1, x + 1, TOP:END] = new
            carry = pack(*carry, new, x)
        return carry

    low, high = lax.fori_loop(0, BX, lift_step, (zero_tile, zero_tile))
    zs[1, 0] = low
    zs[1, 1] = high

    def post_step(turn, carry):
        slot = 1 - lax.rem(turn, 2)
        start("v", slot)
        finish("v", slot)
        sweep(slot, 1 - slot)
        return carry

    lax.fori_loop(0, POST, post_step, 0)
    store = pltpu.make_async_copy(v.at[1, 1 : CX + 1, TOP:END], out_hbm, local_sem.at[0])
    store.start()
    store.wait()


def body(right_side, conductance, absorption, block_agg):
    field = (CX, CY, CZ)
    padded = (CX + 2, CY + 16, CZ)
    any_spec = pl.BlockSpec(memory_space=pl.ANY)

    def f32(*shape):
        return pltpu.VMEM(shape, F32)

    return pl.pallas_call(
        kernel,
        out_shape=jax.ShapeDtypeStruct(field, F32),
        in_specs=[any_spec] * 4,
        out_specs=any_spec,
        scratch_shapes=[
            f32(*field), f32(*field), f32(*padded), pltpu.VMEM((BX, CY // 2, CZ // 2), jnp.int32),
            f32(2, *padded), f32(6, *field), f32(*field), f32(*field), f32(BX, CY + 16, CZ),
            f32(4, BX, CY, CZ), f32(4, BX, CY, CZ),
            f32(2, 8, CZ), f32(2, 8, CZ), f32(2, CY, CZ), f32(2, 16, CZ), f32(2, 16, CZ),
            f32(2, 8, CZ), f32(2, 8, CZ), f32(2, 2, 8, CZ), f32(2, 2, 8, CZ),
            f32(2, CY, CZ), f32(2, 16, CZ), f32(2, 8, CZ),
            pltpu.VMEM((AGG, 8 * CZ), BF16), pltpu.VMEM((2 * AGG, 8 * CZ), BF16),
            f32(AGG, 2 * AGG), f32(7 * AGG, AGG), pltpu.VMEM((7 * AGG, 2 * AGG), BF16),
            f32(2, 8, CZ), f32(2, 6, 8, CZ),
            pltpu.SemaphoreType.DMA((4,)), pltpu.SemaphoreType.DMA((6, 6)), pltpu.SemaphoreType.DMA((6, 6)),
        ],
        compiler_params=pltpu.CompilerParams(collective_id=0, has_side_effects=True),
    )(right_side, conductance, absorption, block_agg)


def solution(mesh):
    spec = P("gx", "gy", "gz")
    return jax.shard_map(body, mesh=mesh, in_specs=(spec,) * 4, out_specs=spec, check_vma=False)
```

```python
import jax
import jax.numpy as jnp
from jax import lax
from jax.experimental import pallas as pl
from jax.experimental.pallas import tpu as pltpu
from jax.sharding import PartitionSpec as P

AGG = 128
POST = 4
KC = 8
OMEGA_FINE = 0.8
OMEGA_COARSE = 0.7
CX, CY, CZ = 24, 32, 128
BX = CX // 2
OWN_1, OWN_2 = 4, 8
TOP = 8
END = TOP + CY
AXES = ("gx", "gy", "gz")
F32 = jnp.float32
BF16 = jnp.bfloat16
NT = (((1,), (1,)), ((), ()))


def harmonic(one_side, other_side):
    summed = one_side + other_side
    return 2.0 * (one_side * other_side) / summed


def safe_harmonic(one_side, other_side):
    summed = one_side + other_side
    return 2.0 * (one_side * other_side) / jnp.where(summed > 0.0, summed, 1.0)


def lanes_of(shape):
    return lax.broadcasted_iota(jnp.int32, shape, 1)


def rows_of(shape):
    return lax.broadcasted_iota(jnp.int32, shape, 0)


def lane_roll(values, shift):
    return pltpu.roll(values, shift % CZ if isinstance(shift, int) else shift, 1)


def row_roll(values, shift):
    return pltpu.roll(values, shift % values.shape[0], 0)


def quad_sum(values):
    pair = values + row_roll(values, -1)
    return pair + lane_roll(pair, -1)


def squeeze_cells(values):
    even = (lanes_of(values.shape) & 1) == 0
    return jnp.where(even, values, lane_roll(row_roll(values, -2), 1))


def split(values):
    high = values.astype(BF16).astype(F32)
    return high, values - high


def spread_row(row):
    return jnp.broadcast_to(row, (16, CZ)).astype(BF16)


def kernel(
    b_hbm, k_hbm, a_hbm, l_hbm, out_hbm,
    bv, av, kp, lv, v, gw, c0, dg, sc, fx, fy, fz, gz, gy, gx, lc, el, ew,
    kxh, kyh, kzs, kzh, lxh, lys, lyh, lzs, lzh, xh, yh, zs, zh,
    fze, wyf, rows_y, xs, ys, acc, mf, mm, cs, ch,
    local_sem, send_sem, recv_sem,
):
    pos = [lax.axis_index(a) for a in AXES]
    size = [lax.axis_size(a) for a in AXES]
    has = []
    dev = []
    for axis in range(3):
        has.append(pos[axis] > 0)
        dev.append({AXES[axis]: pos[axis] - 1})
        has.append(pos[axis] < size[axis] - 1)
        dev.append({AXES[axis]: pos[axis] + 1})
    cells = slice(TOP, END)

    def exchange_of(kind, slot):
        if kind == "k":
            src = [kp.at[1, cells], kp.at[CX, cells], kp.at[1 : CX + 1, TOP : TOP + 1],
                   kp.at[1 : CX + 1, END - 1 : END], kzs.at[0], kzs.at[1]]
            dst = [kxh.at[0], kxh.at[1], kyh.at[0, :, 0:1], kyh.at[1, :, 7:8], kzh.at[0], kzh.at[1]]
            sem = 0
        elif kind == "l":
            src = [lc.at[0, cells], lc.at[BX - 1, cells], lys.at[0], lys.at[1], lzs.at[0], lzs.at[1]]
            dst = [lxh.at[0], lxh.at[1], lyh.at[0], lyh.at[1], lzh.at[0], lzh.at[1]]
            sem = 1
        elif kind == "v":
            src = [v.at[slot, 1, cells], v.at[slot, CX, cells], v.at[slot, 1 : CX + 1, TOP : TOP + 1],
                   v.at[slot, 1 : CX + 1, END - 1 : END], zs.at[slot, 0], zs.at[slot, 1]]
            dst = [xh.at[slot, 0], xh.at[slot, 1], yh.at[slot, 0, :, 0:1], yh.at[slot, 1, :, 7:8],
                   zh.at[slot, 0], zh.at[slot, 1]]
            sem = 2 + slot
        else:
            src = [cs.at[slot]] * 6
            dst = [ch.at[slot, d] for d in range(6)]
            sem = 4 + slot
        return src, dst, sem

    def copy_to(kind, slot, d):
        src, dst, sem = exchange_of(kind, slot)
        return pltpu.make_async_remote_copy(
            src[d], dst[d ^ 1], send_sem.at[sem, d], recv_sem.at[sem, d ^ 1],
            device_id=dev[d], device_id_type=pl.DeviceIdType.MESH)

    def copy_from(kind, slot, d):
        src, dst, sem = exchange_of(kind, slot)
        return pltpu.make_async_remote_copy(
            src[d], dst[d], send_sem.at[sem, d], recv_sem.at[sem, d],
            device_id=dev[d], device_id_type=pl.DeviceIdType.MESH)

    def start(kind, slot=0, sides=(4, 5, 2, 3, 0, 1)):
        for d in sides:
            @pl.when(has[d])
            def _():
                copy_to(kind, slot, d).start()

    def finish(kind, slot=0):
        for d in range(6):
            @pl.when(has[d])
            def _():
                copy_from(kind, slot, d).wait_recv()
        for d in range(6):
            @pl.when(has[d])
            def _():
                copy_to(kind, slot, d).wait_send()

    load_k = pltpu.make_async_copy(k_hbm, kp.at[1 : CX + 1, cells], local_sem.at[0])
    load_l = pltpu.make_async_copy(l_hbm, lv, local_sem.at[1])
    load_a = pltpu.make_async_copy(a_hbm, av, local_sem.at[2])
    load_b = pltpu.make_async_copy(b_hbm, bv, local_sem.at[3])
    load_k.start()
    load_l.start()
    load_a.start()
    load_b.start()

    zero_plane = jnp.zeros((CY, CZ), F32)
    zero_tile = jnp.zeros((8, CZ), F32)
    for side in range(2):
        kxh[side] = zero_plane
        lxh[side] = zero_plane
        lyh[side] = jnp.zeros((16, CZ), F32)
        for half in range(2):
            kzh[side, half] = zero_tile
            lzh[side, half] = zero_tile
        for x in range(CX):
            kyh[side, x] = zero_tile

    barrier = pltpu.get_barrier_semaphore()
    count = jnp.int32(0)
    for d in range(6):
        @pl.when(has[d])
        def _():
            pl.semaphore_signal(barrier, inc=1, device_id=dev[d], device_id_type=pl.DeviceIdType.MESH)
        count = count + has[d].astype(jnp.int32)

    for slot in range(2):
        for d in range(6):
            ch[slot, d] = zero_tile
        for side in range(2):
            xh[slot, side] = zero_plane
            for half in range(2):
                zh[slot, side, half] = zero_tile
            for x in range(CX):
                yh[slot, side, x] = zero_tile
        for edge in (0, CX + 1):
            v[slot, edge, cells] = zero_plane
        for x in range(CX):
            v[slot, x + 1, TOP - 8 : TOP] = zero_tile
            v[slot, x + 1, END : END + 8] = zero_tile
    for edge in (0, CX + 1):
        kp[edge, cells] = zero_plane
    for x in range(CX):
        kp[x + 1, TOP - 8 : TOP] = zero_tile
        kp[x + 1, END : END + 8] = zero_tile
        fy[x, CY : CY + 8] = zero_tile
    fx[0] = zero_plane
    for side in range(2):
        lys[side] = jnp.zeros((16, CZ), F32)
        wyf[side] = jnp.zeros((16, CZ), F32)
        rows_y[side] = jnp.zeros((16, CZ), F32)
    pl.semaphore_wait(barrier, count)

    lane_8 = lanes_of((8, CZ))
    rim = (lane_8 == 0) | (lane_8 == CZ - 1)
    odd = (lane_8 & 1) == 1

    def pack_plane(packed, plane, x):
        for g in range(4):
            piece = jnp.where(rim, plane[8 * g : 8 * g + 8], 0.0)
            packed = packed + lane_roll(piece, 2 * (4 * x + g))
        return packed

    def store_packed(ref, half, packed):
        ref[0, half] = lane_roll(packed, -1)
        ref[1, half] = lane_roll(packed, 1)

    def joined(ref, half):
        return jnp.where(odd, ref[1, half], ref[0, half])

    def unpack_plane(packed, x):
        return [lane_roll(packed, -2 * (4 * x + g)) for g in range(4)]

    load_k.wait()
    start("k", 0, range(4))
    own_k = []
    for half in range(2):
        packed = zero_tile
        for x in range(12):
            packed = pack_plane(packed, kp[12 * half + x + 1, cells], x)
        store_packed(kzs, half, packed)
        own_k.append(packed)
    start("k", 0, (4, 5))

    load_l.wait()
    labels = lv[...].reshape(BX * 16, 64).astype(F32).astype(BF16)
    widen = jnp.where(lanes_of((64, CZ)) // 2 == rows_of((64, CZ)), 1.0, 0.0).astype(BF16)
    wide = jnp.dot(labels, widen, preferred_element_type=F32).astype(BF16)
    tall_shape = (BX * CY, BX * 16)
    heighten = jnp.where(rows_of(tall_shape) // 2 == lanes_of(tall_shape), 1.0, 0.0).astype(BF16)
    tall = jnp.dot(heighten, wide, preferred_element_type=F32)
    for x in range(BX):
        lc[x, cells] = tall[x * CY : (x + 1) * CY]
        lc[x, END : END + 8] = zero_tile
        lys[0, x : x + 1] = tall[x * CY : x * CY + 1]
        lys[1, x : x + 1] = tall[x * CY + CY - 1 : x * CY + CY]
    own_l = []
    for half in range(2):
        packed = zero_tile
        for x in range(6):
            plane = lc[6 * half + x, cells]
            packed = pack_plane(packed, plane, 2 * x)
            packed = pack_plane(packed, plane, 2 * x + 1)
        store_packed(lzs, half, packed)
        own_l.append(packed)
    start("l")

    lane = lanes_of((CY, CZ))
    row = rows_of((CY, CZ))
    load_a.wait()

    def faces(x, fx_low):
        centre = kp[x + 1, cells]
        fx_high = harmonic(centre, kp[x + 2, cells])
        fy_low = harmonic(kp[x + 1, TOP - 1 : END - 1], centre)
        fy[x, 0:CY] = fy_low
        fz_low = jnp.where(lane == 0, 0.0, harmonic(lane_roll(centre, 1), centre))
        fz_high = lane_roll(fz_low, -1)
        fy_high = fy[x, 1 : CY + 1]
        fx[x + 1] = fx_high
        fz[0, x] = fz_low
        fz[1, x] = fz_high
        dg[x] = av[x] + fx_low + fx_high + fy_low + fy_high + fz_low + fz_high
        return fx_high, fy_high, fz_high

    def block_step(block, fx_low):
        x = 2 * block
        fx_mid, fy_high_0, fz_high_0 = faces(x, fx_low)
        fx_high, fy_high_1, fz_high_1 = faces(x + 1, fx_mid)
        wx = quad_sum(fx_high)
        wy = fy_high_0 + fy_high_1
        wy = row_roll(wy + lane_roll(wy, -1), -1)
        wz = fz_high_0 + fz_high_1
        wz = lane_roll(wz + row_roll(wz, -1), -1)
        wa = 0.5 * quad_sum(av[x] + av[x + 1])
        own = lc[block, cells]
        lx = lc[jnp.minimum(block + 1, BX - 1), cells]
        ly = lc[block, TOP + 2 : END + 2]
        lz = lane_roll(own, -2)
        lx = jnp.where(lx == own, -1.0, lx)
        ly = jnp.where((ly == own) | (row >= CY - 2), -1.0, ly)
        lz = jnp.where((lz == own) | (lane >= CZ - 2), -1.0, lz)
        same = ly == lx
        wx = wx + jnp.where(same, wy, 0.0)
        ly = jnp.where(same, -1.0, ly)
        same = lz == lx
        wx = wx + jnp.where(same, wz, 0.0)
        lz = jnp.where(same, -1.0, lz)
        same = lz == ly
        wy = wy + jnp.where(same, wz, 0.0)
        lz = jnp.where(same, -1.0, lz)
        for n, field in enumerate((own, lx, ly, lz)):
            el[n, block] = squeeze_cells(field)
        for n, field in enumerate((wa, wx, wy, wz)):
            ew[n, block] = squeeze_cells(field)
        return fx_high

    def block_pair(turn, fx_low):
        return block_step(2 * turn + 1, block_step(2 * turn, fx_low))

    lax.fori_loop(0, BX // 2, block_pair, zero_plane)

    number = rows_of((16, CZ)).astype(F32)
    numbers = [(number + 16.0 * q).astype(BF16) for q in range(8)]
    one = jnp.ones((16, CZ), BF16)
    zero = jnp.zeros((16, CZ), BF16)

    def place(at, lhs_label, pairs):
        lhs_label = spread_row(lhs_label)
        spread = []
        for label, weight in pairs:
            high, low = split(weight)
            spread.append((spread_row(label), spread_row(high), spread_row(low)))
        for q in range(8):
            xs[16 * q : 16 * q + 16, at : at + CZ] = jnp.where(lhs_label == numbers[q], one, zero)
            y_high = zero
            y_low = zero
            for label, high, low in spread:
                hit = label == numbers[q]
                y_high = jnp.where(hit, high, y_high)
                y_low = jnp.where(hit, low, y_low)
            ys[16 * q : 16 * q + 16, at : at + CZ] = y_high
            ys[AGG + 16 * q : AGG + 16 * q + 16, at : at + CZ] = y_low

    acc[...] = jnp.zeros((AGG, 2 * AGG), F32)

    def own_step(block, carry):
        for m in range(8):
            at = slice(4 * m, 4 * m + 1)
            pairs = [(el[n, block, at], ew[n, block, at]) for n in range(4)]
            place(m * CZ, pairs[0][0], pairs)
        acc[...] += lax.dot_general(xs[...], ys[...], NT, preferred_element_type=F32)
        return carry

    lax.fori_loop(0, OWN_1, own_step, 0)
    load_b.wait()
    finish("k")

    gx[0] = harmonic(kp[1, cells], kxh[0])
    gx[1] = harmonic(kp[CX, cells], kxh[1])
    for half in range(2):
        fze[half] = safe_harmonic(own_k[half], joined(kzh, half))

    def first_step(half, carry):
        packed = zero_tile
        face_z = fze[half]
        for local in range(12):
            x = 12 * half + local
            wall = unpack_plane(face_z, local)
            wall = jnp.concatenate([jnp.where(rim, w, 0.0) for w in wall], axis=0)
            gz[x] = wall
            low = harmonic(kp[x + 1, TOP : TOP + 8], kyh[0, x])
            high = harmonic(kp[x + 1, END - 8 : END], kyh[1, x])
            gy[0, x] = low
            gy[1, x] = high
            diag = dg[x] + wall + jnp.concatenate([low, jnp.zeros((16, CZ), F32), high], axis=0)
            if local == 0:
                diag = diag + jnp.where(half == 0, gx[0], 0.0)
            if local == 11:
                diag = diag + jnp.where(half == 1, gx[1], 0.0)
            scale = OMEGA_FINE / diag
            first = scale * bv[x]
            dg[x] = diag
            sc[x] = scale
            c0[x] = first
            v[0, x + 1, cells] = first
            packed = pack_plane(packed, first, local)
        store_packed(zs.at[0], half, packed)
        return carry

    lax.fori_loop(0, 2, first_step, 0)
    start("v", 0)

    def face_rows(block, carry):
        x = 2 * block
        low = (gy[0, x] + gy[0, x + 1])[0:1]
        high = (gy[1, x] + gy[1, x + 1])[7:8]
        wyf[0, pl.ds(block, 1)] = low + lane_roll(low, -1)
        wyf[1, pl.ds(block, 1)] = high + lane_roll(high, -1)
        return carry

    lax.fori_loop(0, BX, face_rows, 0, unroll=True)
    wxf = [quad_sum(gx[side]) for side in range(2)]

    def scale_step(turn, carry):
        for local in range(4):
            x = 4 * turn + local
            scale = sc[x]
            gw[0, x] = scale * fx[x]
            gw[1, x] = scale * fx[x + 1]
            gw[2, x] = scale * fy[x, 0:CY]
            gw[3, x] = scale * fy[x, 1 : CY + 1]
            gw[4, x] = scale * fz[0, x]
            gw[5, x] = scale * fz[1, x]
            gz[x] = scale * gz[x]
            gy[0, x] = scale[0:8] * gy[0, x]
            gy[1, x] = scale[CY - 8 :] * gy[1, x]
        return carry

    lax.fori_loop(0, CX // 4, scale_step, 0)
    gx[0] = sc[0] * gx[0]
    gx[1] = sc[CX - 1] * gx[1]

    def inner(slot, other):
        def step(turn, carry):
            for local in range(4):
                x = 4 * turn + local
                centre = v[slot, x + 1, cells]
                total = c0[x] + (1.0 - OMEGA_FINE) * centre
                total = total + gw[0, x] * v[slot, x, cells] + gw[1, x] * v[slot, x + 2, cells]
                total = total + gw[2, x] * v[slot, x + 1, TOP - 1 : END - 1]
                total = total + gw[3, x] * v[slot, x + 1, TOP + 1 : END + 1]
                total = total + gw[4, x] * lane_roll(centre, 1) + gw[5, x] * lane_roll(centre, -1)
                v[other, x + 1, cells] = total
            return carry

        lax.fori_loop(0, CX // 4, step, 0)

    def outer(slot, other):
        v[other, 1, cells] += gx[0] * xh[slot, 0]
        v[other, CX, cells] += gx[1] * xh[slot, 1]

        def step(half, carry):
            packed = zero_tile
            halo_z = joined(zh.at[slot], half)
            for local in range(12):
                x = 12 * half + local
                wall = jnp.concatenate(unpack_plane(halo_z, local), axis=0)
                low = gy[0, x] * yh[slot, 0, x]
                high = gy[1, x] * yh[slot, 1, x]
                new = v[other, x + 1, cells] + gz[x] * wall
                new = new + jnp.concatenate([low, jnp.zeros((16, CZ), F32), high], axis=0)
                v[other, x + 1, cells] = new
                packed = pack_plane(packed, new, local)
            store_packed(zs.at[other], half, packed)
            return carry

        lax.fori_loop(0, 2, step, 0)

    inner(0, 1)
    lax.fori_loop(OWN_1, OWN_2, own_step, 0)

    finish("v", 0)
    outer(0, 1)
    start("v", 1)

    lax.fori_loop(OWN_2, BX, own_step, 0)
    sum_own = acc[:, :AGG] + acc[:, AGG:]
    mf[0:AGG] = sum_own + sum_own.T
    finish("l")

    def pair_rows(values):
        return jnp.where((lanes_of(values.shape) & 1) == 0, values, lane_roll(row_roll(values, -1), 1))

    def face_blocks(halves, side, summed):
        out = []
        for values in halves:
            if side:
                values = lane_roll(values, 1)
            if summed:
                values = values + lane_roll(values, -8)
                values = values + row_roll(values, -1)
            out.append(jnp.where((lane_8 & 8) == 0, values, lane_roll(row_roll(values, -2), 8)))
        out = jnp.where(odd, lane_roll(out[1], 1), out[0])
        return jnp.where(lane_8 < 96, out, 0.0) if summed else out

    faces_of = []
    for side in range(2):
        faces_of.append((side, squeeze_cells(lxh[side]), squeeze_cells(lc[side * (BX - 1), cells]),
                         squeeze_cells(wxf[side]), range(0, CY, 4)))
        faces_of.append((2 + side, pair_rows(lyh[side]), pair_rows(lys[side]), pair_rows(wyf[side]), range(0, BX, 2)))
        peers = [joined(lzh, half) for half in range(2)]
        faces_of.append((4 + side, face_blocks(peers, side, False), face_blocks(own_l, side, False),
                         face_blocks([fze[0], fze[1]], side, True), (0, 4)))

    for d, peer, own, weight, at_rows in faces_of:
        for n, r in enumerate(at_rows):
            at = slice(r, r + 1)
            place(n * CZ, peer[at], [(own[at], weight[at])])
        depth = len(at_rows) * CZ
        tile = lax.dot_general(xs[:, :depth], ys[:, :depth], NT, preferred_element_type=F32)
        mf[AGG * (d + 1) : AGG * (d + 2)] = tile[:, :AGG] + tile[:, AGG:]

    column = zero_tile
    for r in range(0, 7 * AGG, 8):
        column = column + mf[r : r + 8]
    coarse_diag = jnp.sum(column, axis=0, keepdims=True)
    coarse_scale = OMEGA_COARSE / coarse_diag
    square = (AGG, AGG)
    mf[0:AGG] = jnp.where(rows_of(square) == lanes_of(square), 0.0, mf[0:AGG])
    for t in range(7):
        high, low = split(mf[AGG * t : AGG * (t + 1)])
        mm[AGG * t : AGG * (t + 1), :AGG] = high.astype(BF16)
        mm[AGG * t : AGG * (t + 1), AGG:] = low.astype(BF16)

    inner(1, 0)

    def residual_step(turn, carry):
        for local in range(4):
            block = 4 * turn + local
            total = zero_plane
            for x in (2 * block, 2 * block + 1):
                total = total + dg[x] * (v[0, x + 1, cells] - v[1, x + 1, cells])
            ew[0, block] = squeeze_cells(quad_sum(total * (1.0 / OMEGA_FINE)))
        return carry

    lax.fori_loop(0, BX // 4, residual_step, 0)
    wanted = rows_of((AGG, CZ)).astype(F32)

    def gather_row(sums, label, value):
        label = jnp.broadcast_to(label, (AGG, CZ))
        return sums + jnp.where(label == wanted, jnp.broadcast_to(value, (AGG, CZ)), 0.0)

    def restrict_step(block, sums):
        for m in range(8):
            at = slice(4 * m, 4 * m + 1)
            sums = gather_row(sums, el[0, block, at], ew[0, block, at])
        return sums

    sums = lax.fori_loop(0, BX, restrict_step, jnp.zeros((AGG, CZ), F32))

    finish("v", 1)
    halo_z = [fze[half] * joined(zh.at[1], half) for half in range(2)]
    inverse = 1.0 / OMEGA_FINE
    for block in range(BX):
        x = 2 * block
        low = sum(gy[0, n] * yh[1, 0, n] * dg[n, 0:8] for n in (x, x + 1))[0:1]
        high = sum(gy[1, n] * yh[1, 1, n] * dg[n, CY - 8 : CY] for n in (x, x + 1))[7:8]
        rows_y[0, block : block + 1] = inverse * (low + lane_roll(low, -1))
        rows_y[1, block : block + 1] = inverse * (high + lane_roll(high, -1))
    for side in range(2):
        plane = gx[side] * xh[1, side] * dg[side * (CX - 1)] * inverse
        values = (squeeze_cells(quad_sum(plane)), pair_rows(rows_y[side]), face_blocks(halo_z, side, True))
        for (d, peer, own, weight, at_rows), value in zip(faces_of[3 * side : 3 * side + 3], values):
            for r in at_rows:
                sums = gather_row(sums, own[r : r + 1], value[r : r + 1])
    coarse_rhs = lax.dot_general(
        jnp.ones((8, CZ), F32), sums, NT, preferred_element_type=F32, precision=lax.Precision.HIGHEST)

    small_row = rows_of((8, CZ))

    def coarse_step(turn, correction):
        slot = lax.rem(turn, 2)
        high, low = split(correction)
        tile = jnp.where(small_row == 0, high, jnp.where(small_row == 1, low, 0.0))
        cs[slot] = tile
        start("c", slot)
        image = jnp.dot(tile.astype(BF16), mm[0:AGG], preferred_element_type=F32)
        base = (1.0 - OMEGA_COARSE) * correction + coarse_scale * coarse_rhs
        finish("c", slot)
        beside = jnp.concatenate([ch[slot, d] for d in range(6)], axis=1).astype(BF16)
        image = image + jnp.dot(beside, mm[AGG:], preferred_element_type=F32)
        image = jnp.sum(image[:, :AGG] + image[:, AGG:], axis=0, keepdims=True)
        return base + coarse_scale * image

    correction = lax.fori_loop(0, KC - 1, coarse_step, coarse_scale * coarse_rhs)

    def lift_step(half, carry):
        packed = zero_tile
        for local in range(6):
            block = 6 * half + local
            index = lc[block, cells].astype(jnp.int32)
            lifted = jnp.concatenate(
                [jnp.take_along_axis(correction, index[8 * g : 8 * g + 8], axis=1, mode="promise_in_bounds")
                 for g in range(4)], axis=0)
            for n in range(2):
                x = 2 * block + n
                new = v[1, x + 1, cells] + lifted
                v[1, x + 1, cells] = new
                packed = pack_plane(packed, new, 2 * local + n)
        store_packed(zs.at[1], half, packed)
        return carry

    lax.fori_loop(0, 2, lift_step, 0)

    def post_step(turn, carry):
        slot = 1 - lax.rem(turn, 2)
        start("v", slot)
        inner(slot, 1 - slot)
        finish("v", slot)
        outer(slot, 1 - slot)
        return carry

    lax.fori_loop(0, POST, post_step, 0)
    store = pltpu.make_async_copy(v.at[1, 1 : CX + 1, cells], out_hbm, local_sem.at[0])
    store.start()
    store.wait()


def body(right_side, conductance, absorption, block_agg):
    field = (CX, CY, CZ)
    padded = (CX + 2, CY + 16, CZ)
    any_spec = pl.BlockSpec(memory_space=pl.ANY)

    def f32(*shape):
        return pltpu.VMEM(shape, F32)

    scratch = dict(
        bv=f32(*field), av=f32(*field), kp=f32(*padded), lv=pltpu.VMEM((BX, CY // 2, CZ // 2), jnp.int32),
        v=f32(2, *padded), gw=f32(6, *field), c0=f32(*field), dg=f32(*field), sc=f32(*field),
        fx=f32(CX + 1, CY, CZ), fy=f32(CX, CY + 8, CZ), fz=f32(2, *field),
        gz=f32(*field), gy=f32(2, CX, 8, CZ), gx=f32(2, CY, CZ),
        lc=f32(BX, CY + 16, CZ), el=f32(4, BX, CY, CZ), ew=f32(4, BX, CY, CZ),
        kxh=f32(2, CY, CZ), kyh=f32(2, CX, 8, CZ), kzs=f32(2, 2, 8, CZ), kzh=f32(2, 2, 8, CZ),
        lxh=f32(2, CY, CZ), lys=f32(2, 16, CZ), lyh=f32(2, 16, CZ), lzs=f32(2, 2, 8, CZ), lzh=f32(2, 2, 8, CZ),
        xh=f32(2, 2, CY, CZ), yh=f32(2, 2, CX, 8, CZ), zs=f32(2, 2, 2, 8, CZ), zh=f32(2, 2, 2, 8, CZ),
        fze=f32(2, 8, CZ), wyf=f32(2, 16, CZ), rows_y=f32(2, 16, CZ),
        xs=pltpu.VMEM((AGG, 8 * CZ), BF16), ys=pltpu.VMEM((2 * AGG, 8 * CZ), BF16),
        acc=f32(AGG, 2 * AGG), mf=f32(7 * AGG, AGG), mm=pltpu.VMEM((7 * AGG, 2 * AGG), BF16),
        cs=f32(2, 8, CZ), ch=f32(2, 6, 8, CZ),
    )
    return pl.pallas_call(
        kernel,
        out_shape=jax.ShapeDtypeStruct(field, F32),
        in_specs=[any_spec] * 4,
        out_specs=any_spec,
        scratch_shapes=list(scratch.values()) + [
            pltpu.SemaphoreType.DMA((4,)), pltpu.SemaphoreType.DMA((6, 6)), pltpu.SemaphoreType.DMA((6, 6)),
        ],
        compiler_params=pltpu.CompilerParams(collective_id=0, has_side_effects=True),
    )(right_side, conductance, absorption, block_agg)


def solution(mesh):
    spec = P("gx", "gy", "gz")
    return jax.shard_map(body, mesh=mesh, in_specs=(spec,) * 4, out_specs=spec, check_vma=False)
```

```python
import jax
import jax.numpy as jnp
from jax import lax
from jax.experimental import pallas as pl
from jax.experimental.pallas import tpu as pltpu
from jax.sharding import PartitionSpec as P

AGG = 128
POST = 4
KC = 8
OMEGA_FINE = 0.8
OMEGA_COARSE = 0.7
CX, CY, CZ = 24, 32, 128
BX = CX // 2
OWN_1, OWN_2 = 4, 8
TOP = 8
END = TOP + CY
AXES = ("gx", "gy", "gz")
F32 = jnp.float32
BF16 = jnp.bfloat16
NT = (((1,), (1,)), ((), ()))


def harmonic(one_side, other_side):
    summed = one_side + other_side
    return 2.0 * (one_side * other_side) / summed


def safe_harmonic(one_side, other_side):
    summed = one_side + other_side
    return 2.0 * (one_side * other_side) / jnp.where(summed > 0.0, summed, 1.0)


def lanes_of(shape):
    return lax.broadcasted_iota(jnp.int32, shape, 1)


def rows_of(shape):
    return lax.broadcasted_iota(jnp.int32, shape, 0)


def lane_roll(values, shift):
    return pltpu.roll(values, shift % CZ if isinstance(shift, int) else shift, 1)


def row_roll(values, shift):
    return pltpu.roll(values, shift % values.shape[0], 0)


def quad_sum(values):
    pair = values + row_roll(values, -1)
    return pair + lane_roll(pair, -1)


def squeeze_cells(values):
    even = (lanes_of(values.shape) & 1) == 0
    return jnp.where(even, values, lane_roll(row_roll(values, -2), 1))


def split(values):
    high = values.astype(BF16).astype(F32)
    return high, values - high


def spread_row(row):
    return jnp.broadcast_to(row, (16, CZ)).astype(BF16)


def kernel(
    b_hbm, k_hbm, a_hbm, l_hbm, out_hbm,
    bv, av, kp, lv, v, gw, c0, dg, sc, fx, fy, fz, gz, gy, gx, lc, el, ew,
    kxh, kyh, kzs, kzh, lxh, lys, lyh, lzs, lzh, xh, yh, zs, zh,
    fze, wyf, rows_y, zp, gzp, hz, xs, ys, acc, mf, mm, cs, ch,
    local_sem, send_sem, recv_sem,
):
    pos = [lax.axis_index(a) for a in AXES]
    size = [lax.axis_size(a) for a in AXES]
    has = []
    dev = []
    for axis in range(3):
        has.append(pos[axis] > 0)
        dev.append({AXES[axis]: pos[axis] - 1})
        has.append(pos[axis] < size[axis] - 1)
        dev.append({AXES[axis]: pos[axis] + 1})
    cells = slice(TOP, END)

    def exchange_of(kind, slot):
        if kind == "k":
            src = [kp.at[1, cells], kp.at[CX, cells], kp.at[1 : CX + 1, TOP : TOP + 1],
                   kp.at[1 : CX + 1, END - 1 : END], kzs.at[0], kzs.at[1]]
            dst = [kxh.at[0], kxh.at[1], kyh.at[0, :, 0:1], kyh.at[1, :, 7:8], kzh.at[0], kzh.at[1]]
            sem = 0
        elif kind == "l":
            src = [lc.at[0, cells], lc.at[BX - 1, cells], lys.at[0], lys.at[1], lzs.at[0], lzs.at[1]]
            dst = [lxh.at[0], lxh.at[1], lyh.at[0], lyh.at[1], lzh.at[0], lzh.at[1]]
            sem = 1
        elif kind == "v":
            src = [v.at[slot, 1, cells], v.at[slot, CX, cells], v.at[slot, 1 : CX + 1, TOP : TOP + 1],
                   v.at[slot, 1 : CX + 1, END - 1 : END], zs.at[slot, 0], zs.at[slot, 1]]
            dst = [xh.at[slot, 0], xh.at[slot, 1], yh.at[slot, 0, :, 0:1], yh.at[slot, 1, :, 7:8],
                   zh.at[slot, 0], zh.at[slot, 1]]
            sem = 2 + slot
        else:
            src = [cs.at[slot]] * 6
            dst = [ch.at[slot, d] for d in range(6)]
            sem = 4 + slot
        return src, dst, sem

    def copy_to(kind, slot, d):
        src, dst, sem = exchange_of(kind, slot)
        return pltpu.make_async_remote_copy(
            src[d], dst[d ^ 1], send_sem.at[sem, d], recv_sem.at[sem, d ^ 1],
            device_id=dev[d], device_id_type=pl.DeviceIdType.MESH)

    def copy_from(kind, slot, d):
        src, dst, sem = exchange_of(kind, slot)
        return pltpu.make_async_remote_copy(
            src[d], dst[d], send_sem.at[sem, d], recv_sem.at[sem, d],
            device_id=dev[d], device_id_type=pl.DeviceIdType.MESH)

    def start(kind, slot=0, sides=(4, 5, 2, 3, 0, 1)):
        for d in sides:
            @pl.when(has[d])
            def _():
                copy_to(kind, slot, d).start()

    def finish_send(kind, slot=0):
        for d in range(6):
            @pl.when(has[d])
            def _():
                copy_to(kind, slot, d).wait_send()

    def finish_recv(kind, slot=0):
        for d in range(6):
            @pl.when(has[d])
            def _():
                copy_from(kind, slot, d).wait_recv()

    def finish(kind, slot=0):
        finish_send(kind, slot)
        finish_recv(kind, slot)

    load_k = pltpu.make_async_copy(k_hbm, kp.at[1 : CX + 1, cells], local_sem.at[0])
    load_l = pltpu.make_async_copy(l_hbm, lv, local_sem.at[1])
    load_a = pltpu.make_async_copy(a_hbm, av, local_sem.at[2])
    load_b = pltpu.make_async_copy(b_hbm, bv, local_sem.at[3])
    load_k.start()
    load_l.start()
    load_a.start()
    load_b.start()

    zero_plane = jnp.zeros((CY, CZ), F32)
    zero_tile = jnp.zeros((8, CZ), F32)
    for side in range(2):
        kxh[side] = zero_plane
        lxh[side] = zero_plane
        lyh[side] = jnp.zeros((16, CZ), F32)
        for half in range(2):
            kzh[side, half] = zero_tile
            lzh[side, half] = zero_tile
        for x in range(CX):
            kyh[side, x] = zero_tile

    barrier = pltpu.get_barrier_semaphore()
    count = jnp.int32(0)
    for d in range(6):
        @pl.when(has[d])
        def _():
            pl.semaphore_signal(barrier, inc=1, device_id=dev[d], device_id_type=pl.DeviceIdType.MESH)
        count = count + has[d].astype(jnp.int32)

    for slot in range(2):
        for d in range(6):
            ch[slot, d] = zero_tile
        for side in range(2):
            xh[slot, side] = zero_plane
            for half in range(2):
                zh[slot, side, half] = zero_tile
            for x in range(CX):
                yh[slot, side, x] = zero_tile
        for edge in (0, CX + 1):
            v[slot, edge, cells] = zero_plane
        for x in range(CX):
            v[slot, x + 1, TOP - 8 : TOP] = zero_tile
            v[slot, x + 1, END : END + 8] = zero_tile
    for edge in (0, CX + 1):
        kp[edge, cells] = zero_plane
    for x in range(CX):
        kp[x + 1, TOP - 8 : TOP] = zero_tile
        kp[x + 1, END : END + 8] = zero_tile
        fy[x, CY : CY + 8] = zero_tile
    fx[0] = zero_plane
    for side in range(2):
        lys[side] = jnp.zeros((16, CZ), F32)
        wyf[side] = jnp.zeros((16, CZ), F32)
        rows_y[side] = jnp.zeros((16, CZ), F32)

    lane_8 = lanes_of((8, CZ))
    rim = (lane_8 == 0) | (lane_8 == CZ - 1)
    odd = (lane_8 & 1) == 1

    def pack_plane(packed, plane, x):
        for g in range(4):
            piece = jnp.where(rim, plane[8 * g : 8 * g + 8], 0.0)
            packed = packed + lane_roll(piece, 2 * (4 * x + g))
        return packed

    def store_packed(ref, half, packed):
        ref[0, half] = lane_roll(packed, -1)
        ref[1, half] = lane_roll(packed, 1)

    def joined(ref, half):
        return jnp.where(odd, ref[1, half], ref[0, half])

    def unpack_plane(packed, x):
        return [lane_roll(packed, -2 * (4 * x + g)) for g in range(4)]

    load_k.wait()
    own_k = []
    for half in range(2):
        packed = zero_tile
        for x in range(12):
            packed = pack_plane(packed, kp[12 * half + x + 1, cells], x)
        store_packed(kzs, half, packed)
        own_k.append(packed)
    pl.semaphore_wait(barrier, count)
    start("k")

    load_l.wait()
    labels = lv[...].reshape(BX * 16, 64).astype(F32).astype(BF16)
    widen = jnp.where(lanes_of((64, CZ)) // 2 == rows_of((64, CZ)), 1.0, 0.0).astype(BF16)
    wide = jnp.dot(labels, widen, preferred_element_type=F32).astype(BF16)
    tall_shape = (BX * CY, BX * 16)
    heighten = jnp.where(rows_of(tall_shape) // 2 == lanes_of(tall_shape), 1.0, 0.0).astype(BF16)
    tall = jnp.dot(heighten, wide, preferred_element_type=F32)
    for x in range(BX):
        lc[x, cells] = tall[x * CY : (x + 1) * CY]
        lc[x, END : END + 8] = zero_tile
        lys[0, x : x + 1] = tall[x * CY : x * CY + 1]
        lys[1, x : x + 1] = tall[x * CY + CY - 1 : x * CY + CY]
    own_l = []
    for half in range(2):
        packed = zero_tile
        for x in range(6):
            plane = lc[6 * half + x, cells]
            packed = pack_plane(packed, plane, 2 * x)
            packed = pack_plane(packed, plane, 2 * x + 1)
        store_packed(lzs, half, packed)
        own_l.append(packed)
    start("l")

    lane = lanes_of((CY, CZ))
    row = rows_of((CY, CZ))
    load_a.wait()

    def faces(x, fx_low):
        centre = kp[x + 1, cells]
        fx_high = harmonic(centre, kp[x + 2, cells])
        fy_low = harmonic(kp[x + 1, TOP - 1 : END - 1], centre)
        fy[x, 0:CY] = fy_low
        fz_low = jnp.where(lane == 0, 0.0, harmonic(lane_roll(centre, 1), centre))
        fz_high = lane_roll(fz_low, -1)
        fy_high = fy[x, 1 : CY + 1]
        fx[x + 1] = fx_high
        fz[0, x] = fz_low
        fz[1, x] = fz_high
        dg[x] = av[x] + fx_low + fx_high + fy_low + fy_high + fz_low + fz_high
        return fx_high, fy_high, fz_high

    def block_step(block, fx_low):
        x = 2 * block
        fx_mid, fy_high_0, fz_high_0 = faces(x, fx_low)
        fx_high, fy_high_1, fz_high_1 = faces(x + 1, fx_mid)
        wx = quad_sum(fx_high)
        wy = fy_high_0 + fy_high_1
        wy = row_roll(wy + lane_roll(wy, -1), -1)
        wz = fz_high_0 + fz_high_1
        wz = lane_roll(wz + row_roll(wz, -1), -1)
        wa = 0.5 * quad_sum(av[x] + av[x + 1])
        own = lc[block, cells]
        lx = lc[jnp.minimum(block + 1, BX - 1), cells]
        ly = lc[block, TOP + 2 : END + 2]
        lz = lane_roll(own, -2)
        lx = jnp.where(lx == own, -1.0, lx)
        ly = jnp.where((ly == own) | (row >= CY - 2), -1.0, ly)
        lz = jnp.where((lz == own) | (lane >= CZ - 2), -1.0, lz)
        same = ly == lx
        wx = wx + jnp.where(same, wy, 0.0)
        ly = jnp.where(same, -1.0, ly)
        same = lz == lx
        wx = wx + jnp.where(same, wz, 0.0)
        lz = jnp.where(same, -1.0, lz)
        same = lz == ly
        wy = wy + jnp.where(same, wz, 0.0)
        lz = jnp.where(same, -1.0, lz)
        for n, field in enumerate((own, lx, ly, lz)):
            el[n, block] = squeeze_cells(field)
        for n, field in enumerate((wa, wx, wy, wz)):
            ew[n, block] = squeeze_cells(field)
        return fx_high

    def block_pair(turn, fx_low):
        return block_step(2 * turn + 1, block_step(2 * turn, fx_low))

    lax.fori_loop(0, BX // 2, block_pair, zero_plane)

    number = rows_of((16, CZ)).astype(F32)
    numbers = [(number + 16.0 * q).astype(BF16) for q in range(8)]
    one = jnp.ones((16, CZ), BF16)
    zero = jnp.zeros((16, CZ), BF16)

    def place(at, lhs_label, pairs):
        lhs_label = spread_row(lhs_label)
        spread = []
        for label, weight in pairs:
            high, low = split(weight)
            spread.append((spread_row(label), spread_row(high), spread_row(low)))
        for q in range(8):
            xs[16 * q : 16 * q + 16, at : at + CZ] = jnp.where(lhs_label == numbers[q], one, zero)
            y_high = zero
            y_low = zero
            for label, high, low in spread:
                hit = label == numbers[q]
                y_high = jnp.where(hit, high, y_high)
                y_low = jnp.where(hit, low, y_low)
            ys[16 * q : 16 * q + 16, at : at + CZ] = y_high
            ys[AGG + 16 * q : AGG + 16 * q + 16, at : at + CZ] = y_low

    acc[...] = jnp.zeros((AGG, 2 * AGG), F32)

    def own_step(block, carry):
        for m in range(8):
            at = slice(4 * m, 4 * m + 1)
            pairs = [(el[n, block, at], ew[n, block, at]) for n in range(4)]
            place(m * CZ, pairs[0][0], pairs)
        acc[...] += lax.dot_general(xs[...], ys[...], NT, preferred_element_type=F32)
        return carry

    lax.fori_loop(0, OWN_1, own_step, 0)
    load_b.wait()
    finish("k")

    gx[0] = harmonic(kp[1, cells], kxh[0])
    gx[1] = harmonic(kp[CX, cells], kxh[1])
    for half in range(2):
        fze[half] = safe_harmonic(own_k[half], joined(kzh, half))

    def first_step(half, carry):
        packed = zero_tile
        face_z = fze[half]
        for local in range(12):
            x = 12 * half + local
            wall = unpack_plane(face_z, local)
            wall = jnp.concatenate([jnp.where(rim, w, 0.0) for w in wall], axis=0)
            gz[x] = wall
            low = harmonic(kp[x + 1, TOP : TOP + 8], kyh[0, x])
            high = harmonic(kp[x + 1, END - 8 : END], kyh[1, x])
            gy[0, x] = low
            gy[1, x] = high
            diag = dg[x] + wall + jnp.concatenate([low, jnp.zeros((16, CZ), F32), high], axis=0)
            if local == 0:
                diag = diag + jnp.where(half == 0, gx[0], 0.0)
            if local == 11:
                diag = diag + jnp.where(half == 1, gx[1], 0.0)
            scale = OMEGA_FINE / diag
            first = scale * bv[x]
            dg[x] = diag
            sc[x] = scale
            c0[x] = first
            v[0, x + 1, cells] = first
            packed = pack_plane(packed, first, local)
        store_packed(zs.at[0], half, packed)
        return carry

    lax.fori_loop(0, 2, first_step, 0)
    start("v", 0)

    def face_rows(block, carry):
        x = 2 * block
        low = (gy[0, x] + gy[0, x + 1])[0:1]
        high = (gy[1, x] + gy[1, x + 1])[7:8]
        wyf[0, pl.ds(block, 1)] = low + lane_roll(low, -1)
        wyf[1, pl.ds(block, 1)] = high + lane_roll(high, -1)
        return carry

    lax.fori_loop(0, BX, face_rows, 0, unroll=True)
    wxf = [quad_sum(gx[side]) for side in range(2)]

    def scale_step(turn, carry):
        for local in range(4):
            x = 4 * turn + local
            scale = sc[x]
            gw[0, x] = scale * fx[x]
            gw[1, x] = scale * fx[x + 1]
            gw[2, x] = scale * fy[x, 0:CY]
            gw[3, x] = scale * fy[x, 1 : CY + 1]
            gw[4, x] = scale * fz[0, x]
            gw[5, x] = scale * fz[1, x]
            gz[x] = scale * gz[x]
            gy[0, x] = scale[0:8] * gy[0, x]
            gy[1, x] = scale[CY - 8 :] * gy[1, x]
        return carry

    lax.fori_loop(0, CX // 4, scale_step, 0)
    gx[0] = sc[0] * gx[0]
    gx[1] = sc[CX - 1] * gx[1]

    def pack_scale(half, carry):
        packed = zero_tile
        for local in range(12):
            packed = pack_plane(packed, gz[12 * half + local], local)
        gzp[half] = packed
        return carry

    lax.fori_loop(0, 2, pack_scale, 0)

    def inner(slot, other):
        def step(half, carry):
            packed = zero_tile
            for local in range(12):
                x = 12 * half + local
                centre = v[slot, x + 1, cells]
                total = c0[x] + (1.0 - OMEGA_FINE) * centre
                total = total + gw[0, x] * v[slot, x, cells] + gw[1, x] * v[slot, x + 2, cells]
                total = total + gw[2, x] * v[slot, x + 1, TOP - 1 : END - 1]
                total = total + gw[3, x] * v[slot, x + 1, TOP + 1 : END + 1]
                total = total + gw[4, x] * lane_roll(centre, 1) + gw[5, x] * lane_roll(centre, -1)
                v[other, x + 1, cells] = total
                packed = pack_plane(packed, total, local)
            zp[half] = packed
            return carry

        lax.fori_loop(0, 2, step, 0)

    def outer_faces(slot, other):
        for half in range(2):
            halo_z = joined(zh.at[slot], half)
            hz[half] = halo_z
            packed = zp[half] + gzp[half] * halo_z
            for local in range(12):
                x = 12 * half + local
                low = jnp.where(rim, gy[0, x] * yh[slot, 0, x], 0.0)
                high = jnp.where(rim, gy[1, x] * yh[slot, 1, x], 0.0)
                packed = packed + lane_roll(low, 8 * local) + lane_roll(high, 8 * local + 6)
            if half == 0:
                packed = pack_plane(packed, gx[0] * xh[slot, 0], 0)
            else:
                packed = pack_plane(packed, gx[1] * xh[slot, 1], 11)
            store_packed(zs.at[other], half, packed)

    def outer_rest(slot, other):
        v[other, 1, cells] += gx[0] * xh[slot, 0]
        v[other, CX, cells] += gx[1] * xh[slot, 1]

        def step(half, carry):
            halo_z = hz[half]
            for local in range(12):
                x = 12 * half + local
                wall = jnp.concatenate(unpack_plane(halo_z, local), axis=0)
                low = gy[0, x] * yh[slot, 0, x]
                high = gy[1, x] * yh[slot, 1, x]
                new = v[other, x + 1, cells] + gz[x] * wall
                new = new + jnp.concatenate([low, jnp.zeros((16, CZ), F32), high], axis=0)
                v[other, x + 1, cells] = new
            return carry

        lax.fori_loop(0, 2, step, 0)

    inner(0, 1)
    lax.fori_loop(OWN_1, OWN_2, own_step, 0)

    finish("v", 0)
    outer_faces(0, 1)
    start("v", 1, (4, 5))
    outer_rest(0, 1)
    start("v", 1, (2, 3, 0, 1))

    lax.fori_loop(OWN_2, BX, own_step, 0)
    sum_own = acc[:, :AGG] + acc[:, AGG:]
    mf[0:AGG] = sum_own + sum_own.T
    finish("l")

    def pair_rows(values):
        return jnp.where((lanes_of(values.shape) & 1) == 0, values, lane_roll(row_roll(values, -1), 1))

    def face_blocks(halves, side, summed):
        out = []
        for values in halves:
            if side:
                values = lane_roll(values, 1)
            if summed:
                values = values + lane_roll(values, -8)
                values = values + row_roll(values, -1)
            out.append(jnp.where((lane_8 & 8) == 0, values, lane_roll(row_roll(values, -2), 8)))
        out = jnp.where(odd, lane_roll(out[1], 1), out[0])
        return jnp.where(lane_8 < 96, out, 0.0) if summed else out

    faces_of = []
    for side in range(2):
        faces_of.append((side, squeeze_cells(lxh[side]), squeeze_cells(lc[side * (BX - 1), cells]),
                         squeeze_cells(wxf[side]), range(0, CY, 4)))
        faces_of.append((2 + side, pair_rows(lyh[side]), pair_rows(lys[side]), pair_rows(wyf[side]), range(0, BX, 2)))
        peers = [joined(lzh, half) for half in range(2)]
        faces_of.append((4 + side, face_blocks(peers, side, False), face_blocks(own_l, side, False),
                         face_blocks([fze[0], fze[1]], side, True), (0, 4)))

    for d, peer, own, weight, at_rows in faces_of:
        for n, r in enumerate(at_rows):
            at = slice(r, r + 1)
            place(n * CZ, peer[at], [(own[at], weight[at])])
        depth = len(at_rows) * CZ
        tile = lax.dot_general(xs[:, :depth], ys[:, :depth], NT, preferred_element_type=F32)
        mf[AGG * (d + 1) : AGG * (d + 2)] = tile[:, :AGG] + tile[:, AGG:]

    column = zero_tile
    for r in range(0, 7 * AGG, 8):
        column = column + mf[r : r + 8]
    coarse_diag = jnp.sum(column, axis=0, keepdims=True)
    coarse_scale = OMEGA_COARSE / coarse_diag
    square = (AGG, AGG)
    mf[0:AGG] = jnp.where(rows_of(square) == lanes_of(square), 0.0, mf[0:AGG])
    for t in range(7):
        high, low = split(mf[AGG * t : AGG * (t + 1)] * coarse_scale)
        mm[AGG * t : AGG * (t + 1), :AGG] = high.astype(BF16)
        mm[AGG * t : AGG * (t + 1), AGG:] = low.astype(BF16)

    inner(1, 0)

    def residual_step(turn, carry):
        for local in range(4):
            block = 4 * turn + local
            total = zero_plane
            for x in (2 * block, 2 * block + 1):
                total = total + dg[x] * (v[0, x + 1, cells] - v[1, x + 1, cells])
            ew[0, block] = squeeze_cells(quad_sum(total * (1.0 / OMEGA_FINE)))
        return carry

    lax.fori_loop(0, BX // 4, residual_step, 0)
    wanted = rows_of((AGG, CZ)).astype(F32)

    def gather_row(sums, label, value):
        label = jnp.broadcast_to(label, (AGG, CZ))
        return sums + jnp.where(label == wanted, jnp.broadcast_to(value, (AGG, CZ)), 0.0)

    def restrict_step(block, sums):
        for m in range(8):
            at = slice(4 * m, 4 * m + 1)
            sums = gather_row(sums, el[0, block, at], ew[0, block, at])
        return sums

    sums = lax.fori_loop(0, BX, restrict_step, jnp.zeros((AGG, CZ), F32))

    finish("v", 1)
    halo_z = [fze[half] * joined(zh.at[1], half) for half in range(2)]
    inverse = 1.0 / OMEGA_FINE
    for block in range(BX):
        x = 2 * block
        low = sum(gy[0, n] * yh[1, 0, n] * dg[n, 0:8] for n in (x, x + 1))[0:1]
        high = sum(gy[1, n] * yh[1, 1, n] * dg[n, CY - 8 : CY] for n in (x, x + 1))[7:8]
        rows_y[0, block : block + 1] = inverse * (low + lane_roll(low, -1))
        rows_y[1, block : block + 1] = inverse * (high + lane_roll(high, -1))
    for side in range(2):
        plane = gx[side] * xh[1, side] * dg[side * (CX - 1)] * inverse
        values = (squeeze_cells(quad_sum(plane)), pair_rows(rows_y[side]), face_blocks(halo_z, side, True))
        for (d, peer, own, weight, at_rows), value in zip(faces_of[3 * side : 3 * side + 3], values):
            for r in at_rows:
                sums = gather_row(sums, own[r : r + 1], value[r : r + 1])
    high, low = split(sums)
    ones = jnp.ones((16, CZ), BF16)
    coarse_rhs = lax.dot_general(ones, high.astype(BF16), NT, preferred_element_type=F32)
    coarse_rhs = coarse_rhs + lax.dot_general(ones, low.astype(BF16), NT, preferred_element_type=F32)
    first_correction = coarse_scale * coarse_rhs[0:8]

    def halves(values):
        high, low = split(values)
        return jnp.concatenate([high, low], axis=0).astype(BF16)

    def both(values):
        values = values[:, :AGG] + values[:, AGG:]
        return values[0:8] + values[8:16]

    def coarse_step(turn, correction):
        slot = lax.rem(turn, 2)
        cs[slot] = correction
        start("c", slot)
        image = jnp.dot(halves(correction), mm[0:AGG], preferred_element_type=F32)
        base = (1.0 - OMEGA_COARSE) * correction + first_correction
        base = base + both(image)
        finish("c", slot)
        beside = jnp.concatenate([ch[slot, d] for d in range(6)], axis=1)
        return base + both(jnp.dot(halves(beside), mm[AGG:], preferred_element_type=F32))

    correction = lax.fori_loop(0, KC - 1, coarse_step, first_correction)

    def lift_step(half, carry):
        packed = zero_tile
        for local in range(6):
            block = 6 * half + local
            index = lc[block, cells].astype(jnp.int32)
            lifted = jnp.concatenate(
                [jnp.take_along_axis(correction, index[8 * g : 8 * g + 8], axis=1, mode="promise_in_bounds")
                 for g in range(4)], axis=0)
            for n in range(2):
                x = 2 * block + n
                new = v[1, x + 1, cells] + lifted
                v[1, x + 1, cells] = new
                packed = pack_plane(packed, new, 2 * local + n)
        store_packed(zs.at[1], half, packed)
        return carry

    lax.fori_loop(0, 2, lift_step, 0)

    def post_step(turn, carry):
        slot = 1 - lax.rem(turn, 2)

        @pl.when(turn > 0)
        def _():
            finish_send("v", 1 - slot)

        inner(slot, 1 - slot)
        finish_recv("v", slot)
        outer_faces(slot, 1 - slot)

        @pl.when(turn < POST - 1)
        def _():
            start("v", 1 - slot, (4, 5))

        outer_rest(slot, 1 - slot)

        @pl.when(turn < POST - 1)
        def _():
            start("v", 1 - slot, (2, 3, 0, 1))

        return carry

    start("v", 1)
    lax.fori_loop(0, POST, post_step, 0)
    finish_send("v", 0)
    store = pltpu.make_async_copy(v.at[1, 1 : CX + 1, cells], out_hbm, local_sem.at[0])
    store.start()
    store.wait()


def body(right_side, conductance, absorption, block_agg):
    field = (CX, CY, CZ)
    padded = (CX + 2, CY + 16, CZ)
    any_spec = pl.BlockSpec(memory_space=pl.ANY)

    def f32(*shape):
        return pltpu.VMEM(shape, F32)

    scratch = dict(
        bv=f32(*field), av=f32(*field), kp=f32(*padded), lv=pltpu.VMEM((BX, CY // 2, CZ // 2), jnp.int32),
        v=f32(2, *padded), gw=f32(6, *field), c0=f32(*field), dg=f32(*field), sc=f32(*field),
        fx=f32(CX + 1, CY, CZ), fy=f32(CX, CY + 8, CZ), fz=f32(2, *field),
        gz=f32(*field), gy=f32(2, CX, 8, CZ), gx=f32(2, CY, CZ),
        lc=f32(BX, CY + 16, CZ), el=f32(4, BX, CY, CZ), ew=f32(4, BX, CY, CZ),
        kxh=f32(2, CY, CZ), kyh=f32(2, CX, 8, CZ), kzs=f32(2, 2, 8, CZ), kzh=f32(2, 2, 8, CZ),
        lxh=f32(2, CY, CZ), lys=f32(2, 16, CZ), lyh=f32(2, 16, CZ), lzs=f32(2, 2, 8, CZ), lzh=f32(2, 2, 8, CZ),
        xh=f32(2, 2, CY, CZ), yh=f32(2, 2, CX, 8, CZ), zs=f32(2, 2, 2, 8, CZ), zh=f32(2, 2, 2, 8, CZ),
        fze=f32(2, 8, CZ), wyf=f32(2, 16, CZ), rows_y=f32(2, 16, CZ), zp=f32(2, 8, CZ), gzp=f32(2, 8, CZ), hz=f32(2, 8, CZ),
        xs=pltpu.VMEM((AGG, 8 * CZ), BF16), ys=pltpu.VMEM((2 * AGG, 8 * CZ), BF16),
        acc=f32(AGG, 2 * AGG), mf=f32(7 * AGG, AGG), mm=pltpu.VMEM((7 * AGG, 2 * AGG), BF16),
        cs=f32(2, 8, CZ), ch=f32(2, 6, 8, CZ),
    )
    return pl.pallas_call(
        kernel,
        out_shape=jax.ShapeDtypeStruct(field, F32),
        in_specs=[any_spec] * 4,
        out_specs=any_spec,
        scratch_shapes=list(scratch.values()) + [
            pltpu.SemaphoreType.DMA((4,)), pltpu.SemaphoreType.DMA((6, 6)), pltpu.SemaphoreType.DMA((6, 6)),
        ],
        compiler_params=pltpu.CompilerParams(collective_id=0, has_side_effects=True),
    )(right_side, conductance, absorption, block_agg)


def solution(mesh):
    spec = P("gx", "gy", "gz")
    return jax.shard_map(body, mesh=mesh, in_specs=(spec,) * 4, out_specs=spec, check_vma=False)
```

```python
import jax
import jax.numpy as jnp
from jax import lax
from jax.experimental import pallas as pl
from jax.experimental.pallas import tpu as pltpu
from jax.sharding import PartitionSpec as P

AGG = 128
POST = 4
KC = 8
OMEGA_FINE = 0.8
OMEGA_COARSE = 0.7
CX, CY, CZ = 24, 32, 128
BX = CX // 2
OWN_1, OWN_2 = 4, 8
TOP = 8
END = TOP + CY
AXES = ("gx", "gy", "gz")
F32 = jnp.float32
BF16 = jnp.bfloat16
NT = (((1,), (1,)), ((), ()))


def harmonic(one_side, other_side):
    summed = one_side + other_side
    return 2.0 * (one_side * other_side) / summed


def safe_harmonic(one_side, other_side):
    summed = one_side + other_side
    return 2.0 * (one_side * other_side) / jnp.where(summed > 0.0, summed, 1.0)


def lanes_of(shape):
    return lax.broadcasted_iota(jnp.int32, shape, 1)


def rows_of(shape):
    return lax.broadcasted_iota(jnp.int32, shape, 0)


def lane_roll(values, shift):
    return pltpu.roll(values, shift % CZ if isinstance(shift, int) else shift, 1)


def row_roll(values, shift):
    return pltpu.roll(values, shift % values.shape[0], 0)


def quad_sum(values):
    pair = values + row_roll(values, -1)
    return pair + lane_roll(pair, -1)


def squeeze_cells(values):
    even = (lanes_of(values.shape) & 1) == 0
    return jnp.where(even, values, lane_roll(row_roll(values, -2), 1))


def split(values):
    high = values.astype(BF16).astype(F32)
    return high, values - high


def spread_row(row):
    return jnp.broadcast_to(row, (16, CZ)).astype(BF16)


def kernel(
    b_hbm, k_hbm, a_hbm, l_hbm, out_hbm,
    bv, av, kp, lv, v, gw, c0, dg, sc, fx, fy, fz, gz, gy, gx, lc, el, ew,
    kxh, kyh, kzs, kzh, lxh, lys, lyh, lzs, lzh, xh, yh, zs, zh,
    fze, wyf, rows_y, zp, gzp, hz, tp, xs, ys, acc, mf, mm, cs, ch,
    local_sem, send_sem, recv_sem,
):
    pos = [lax.axis_index(a) for a in AXES]
    size = [lax.axis_size(a) for a in AXES]
    has = []
    dev = []
    for axis in range(3):
        has.append(pos[axis] > 0)
        dev.append({AXES[axis]: pos[axis] - 1})
        has.append(pos[axis] < size[axis] - 1)
        dev.append({AXES[axis]: pos[axis] + 1})
    cells = slice(TOP, END)

    def exchange_of(kind, slot):
        if kind == "k":
            src = [kp.at[1, cells], kp.at[CX, cells], kp.at[1 : CX + 1, TOP : TOP + 1],
                   kp.at[1 : CX + 1, END - 1 : END], kzs.at[0], kzs.at[1]]
            dst = [kxh.at[0], kxh.at[1], kyh.at[0, :, 0:1], kyh.at[1, :, 7:8], kzh.at[0], kzh.at[1]]
            sem = 0
        elif kind == "l":
            src = [lc.at[0, cells], lc.at[BX - 1, cells], lys.at[0], lys.at[1], lzs.at[0], lzs.at[1]]
            dst = [lxh.at[0], lxh.at[1], lyh.at[0], lyh.at[1], lzh.at[0], lzh.at[1]]
            sem = 1
        elif kind == "v":
            src = [v.at[slot, 1, cells], v.at[slot, CX, cells], v.at[slot, 1 : CX + 1, TOP : TOP + 1],
                   v.at[slot, 1 : CX + 1, END - 1 : END], zs.at[slot, 0], zs.at[slot, 1]]
            dst = [xh.at[slot, 0], xh.at[slot, 1], yh.at[slot, 0, :, 0:1], yh.at[slot, 1, :, 7:8],
                   zh.at[slot, 0], zh.at[slot, 1]]
            sem = 2 + slot
        else:
            src = [cs.at[slot]] * 6
            dst = [ch.at[slot, d] for d in range(6)]
            sem = 4 + slot
        return src, dst, sem

    def copy_to(kind, slot, d):
        src, dst, sem = exchange_of(kind, slot)
        return pltpu.make_async_remote_copy(
            src[d], dst[d ^ 1], send_sem.at[sem, d], recv_sem.at[sem, d ^ 1],
            device_id=dev[d], device_id_type=pl.DeviceIdType.MESH)

    def copy_from(kind, slot, d):
        src, dst, sem = exchange_of(kind, slot)
        return pltpu.make_async_remote_copy(
            src[d], dst[d], send_sem.at[sem, d], recv_sem.at[sem, d],
            device_id=dev[d], device_id_type=pl.DeviceIdType.MESH)

    def start(kind, slot=0, sides=(4, 5, 2, 3, 0, 1)):
        for d in sides:
            @pl.when(has[d])
            def _():
                copy_to(kind, slot, d).start()

    def finish_send(kind, slot=0):
        for d in range(6):
            @pl.when(has[d])
            def _():
                copy_to(kind, slot, d).wait_send()

    def finish_recv(kind, slot=0):
        for d in range(6):
            @pl.when(has[d])
            def _():
                copy_from(kind, slot, d).wait_recv()

    def finish(kind, slot=0):
        finish_send(kind, slot)
        finish_recv(kind, slot)

    load_k = pltpu.make_async_copy(k_hbm, kp.at[1 : CX + 1, cells], local_sem.at[0])
    load_l = pltpu.make_async_copy(l_hbm, lv, local_sem.at[1])
    load_a = pltpu.make_async_copy(a_hbm, av, local_sem.at[2])
    load_b = pltpu.make_async_copy(b_hbm, bv, local_sem.at[3])
    load_k.start()
    load_l.start()
    load_a.start()
    load_b.start()

    zero_plane = jnp.zeros((CY, CZ), F32)
    zero_tile = jnp.zeros((8, CZ), F32)
    for side in range(2):
        kxh[side] = zero_plane
        lxh[side] = zero_plane
        lyh[side] = jnp.zeros((16, CZ), F32)
        for half in range(2):
            kzh[side, half] = zero_tile
            lzh[side, half] = zero_tile
        for x in range(CX):
            kyh[side, x] = zero_tile

    barrier = pltpu.get_barrier_semaphore()
    count = jnp.int32(0)
    for d in range(6):
        @pl.when(has[d])
        def _():
            pl.semaphore_signal(barrier, inc=1, device_id=dev[d], device_id_type=pl.DeviceIdType.MESH)
        count = count + has[d].astype(jnp.int32)

    for slot in range(2):
        for d in range(6):
            ch[slot, d] = zero_tile
        for side in range(2):
            xh[slot, side] = zero_plane
            for half in range(2):
                zh[slot, side, half] = zero_tile
            for x in range(CX):
                yh[slot, side, x] = zero_tile
        for edge in (0, CX + 1):
            v[slot, edge, cells] = zero_plane
        for x in range(CX):
            v[slot, x + 1, TOP - 8 : TOP] = zero_tile
            v[slot, x + 1, END : END + 8] = zero_tile
    for edge in (0, CX + 1):
        kp[edge, cells] = zero_plane
    for x in range(CX):
        kp[x + 1, TOP - 8 : TOP] = zero_tile
        kp[x + 1, END : END + 8] = zero_tile
        fy[x, CY : CY + 8] = zero_tile
    fx[0] = zero_plane
    for side in range(2):
        lys[side] = jnp.zeros((16, CZ), F32)
        wyf[side] = jnp.zeros((16, CZ), F32)
        rows_y[side] = jnp.zeros((16, CZ), F32)

    lane_8 = lanes_of((8, CZ))
    rim = (lane_8 == 0) | (lane_8 == CZ - 1)
    odd = (lane_8 & 1) == 1

    def pack_plane(packed, plane, x):
        for g in range(4):
            piece = jnp.where(rim, plane[8 * g : 8 * g + 8], 0.0)
            packed = packed + lane_roll(piece, 2 * (4 * x + g))
        return packed

    def store_packed(ref, half, packed):
        ref[0, half] = lane_roll(packed, -1)
        ref[1, half] = lane_roll(packed, 1)

    def joined(ref, half):
        return jnp.where(odd, ref[1, half], ref[0, half])

    def unpack_plane(packed, x):
        return [lane_roll(packed, -2 * (4 * x + g)) for g in range(4)]

    load_k.wait()
    own_k = []
    for half in range(2):
        packed = zero_tile
        for x in range(12):
            packed = pack_plane(packed, kp[12 * half + x + 1, cells], x)
        store_packed(kzs, half, packed)
        own_k.append(packed)
    pl.semaphore_wait(barrier, count)
    start("k")

    load_l.wait()
    labels = lv[...].reshape(BX * 16, 64).astype(F32).astype(BF16)
    widen = jnp.where(lanes_of((64, CZ)) // 2 == rows_of((64, CZ)), 1.0, 0.0).astype(BF16)
    wide = jnp.dot(labels, widen, preferred_element_type=F32).astype(BF16)
    tall_shape = (BX * CY, BX * 16)
    heighten = jnp.where(rows_of(tall_shape) // 2 == lanes_of(tall_shape), 1.0, 0.0).astype(BF16)
    tall = jnp.dot(heighten, wide, preferred_element_type=F32)
    for x in range(BX):
        lc[x, cells] = tall[x * CY : (x + 1) * CY]
        lc[x, END : END + 8] = zero_tile
        lys[0, x : x + 1] = tall[x * CY : x * CY + 1]
        lys[1, x : x + 1] = tall[x * CY + CY - 1 : x * CY + CY]
    own_l = []
    for half in range(2):
        packed = zero_tile
        for x in range(6):
            plane = lc[6 * half + x, cells]
            packed = pack_plane(packed, plane, 2 * x)
            packed = pack_plane(packed, plane, 2 * x + 1)
        store_packed(lzs, half, packed)
        own_l.append(packed)
    start("l")

    lane = lanes_of((CY, CZ))
    row = rows_of((CY, CZ))
    load_a.wait()

    def faces(x, fx_low):
        centre = kp[x + 1, cells]
        fx_high = harmonic(centre, kp[x + 2, cells])
        fy_low = harmonic(kp[x + 1, TOP - 1 : END - 1], centre)
        fy[x, 0:CY] = fy_low
        fz_low = jnp.where(lane == 0, 0.0, harmonic(lane_roll(centre, 1), centre))
        fz_high = lane_roll(fz_low, -1)
        fy_high = fy[x, 1 : CY + 1]
        fx[x + 1] = fx_high
        fz[0, x] = fz_low
        fz[1, x] = fz_high
        dg[x] = av[x] + fx_low + fx_high + fy_low + fy_high + fz_low + fz_high
        return fx_high, fy_high, fz_high

    def block_step(block, fx_low):
        x = 2 * block
        fx_mid, fy_high_0, fz_high_0 = faces(x, fx_low)
        fx_high, fy_high_1, fz_high_1 = faces(x + 1, fx_mid)
        wx = quad_sum(fx_high)
        wy = fy_high_0 + fy_high_1
        wy = row_roll(wy + lane_roll(wy, -1), -1)
        wz = fz_high_0 + fz_high_1
        wz = lane_roll(wz + row_roll(wz, -1), -1)
        wa = 0.5 * quad_sum(av[x] + av[x + 1])
        own = lc[block, cells]
        lx = lc[jnp.minimum(block + 1, BX - 1), cells]
        ly = lc[block, TOP + 2 : END + 2]
        lz = lane_roll(own, -2)
        lx = jnp.where(lx == own, -1.0, lx)
        ly = jnp.where((ly == own) | (row >= CY - 2), -1.0, ly)
        lz = jnp.where((lz == own) | (lane >= CZ - 2), -1.0, lz)
        same = ly == lx
        wx = wx + jnp.where(same, wy, 0.0)
        ly = jnp.where(same, -1.0, ly)
        same = lz == lx
        wx = wx + jnp.where(same, wz, 0.0)
        lz = jnp.where(same, -1.0, lz)
        same = lz == ly
        wy = wy + jnp.where(same, wz, 0.0)
        lz = jnp.where(same, -1.0, lz)
        for n, field in enumerate((own, lx, ly, lz)):
            el[n, block] = squeeze_cells(field)
        for n, field in enumerate((wa, wx, wy, wz)):
            ew[n, block] = squeeze_cells(field)
        return fx_high

    def block_pair(turn, fx_low):
        return block_step(2 * turn + 1, block_step(2 * turn, fx_low))

    lax.fori_loop(0, BX // 2, block_pair, zero_plane)

    number = rows_of((16, CZ)).astype(F32)
    numbers = [(number + 16.0 * q).astype(BF16) for q in range(8)]
    one = jnp.ones((16, CZ), BF16)
    zero = jnp.zeros((16, CZ), BF16)

    def place(at, lhs_label, pairs):
        lhs_label = spread_row(lhs_label)
        spread = []
        for label, weight in pairs:
            high, low = split(weight)
            spread.append((spread_row(label), spread_row(high), spread_row(low)))
        for q in range(8):
            xs[16 * q : 16 * q + 16, at : at + CZ] = jnp.where(lhs_label == numbers[q], one, zero)
            y_high = zero
            y_low = zero
            for label, high, low in spread:
                hit = label == numbers[q]
                y_high = jnp.where(hit, high, y_high)
                y_low = jnp.where(hit, low, y_low)
            ys[16 * q : 16 * q + 16, at : at + CZ] = y_high
            ys[AGG + 16 * q : AGG + 16 * q + 16, at : at + CZ] = y_low

    acc[...] = jnp.zeros((AGG, 2 * AGG), F32)

    def own_step(block, carry):
        for m in range(8):
            at = slice(4 * m, 4 * m + 1)
            pairs = [(el[n, block, at], ew[n, block, at]) for n in range(4)]
            place(m * CZ, pairs[0][0], pairs)
        acc[...] += lax.dot_general(xs[...], ys[...], NT, preferred_element_type=F32)
        return carry

    lax.fori_loop(0, OWN_1, own_step, 0)
    load_b.wait()
    own_d = []
    own_b = []
    for half in range(2):
        packed_d = zero_tile
        packed_b = zero_tile
        for local in range(12):
            packed_d = pack_plane(packed_d, dg[12 * half + local], local)
            packed_b = pack_plane(packed_b, bv[12 * half + local], local)
        own_d.append(packed_d)
        own_b.append(packed_b)
    finish("k")

    gx[0] = harmonic(kp[1, cells], kxh[0])
    gx[1] = harmonic(kp[CX, cells], kxh[1])
    for half in range(2):
        face_z = safe_harmonic(own_k[half], joined(kzh, half))
        fze[half] = face_z
        diag = own_d[half] + face_z
        for local in range(12):
            x = 12 * half + local
            low = harmonic(kp[x + 1, TOP : TOP + 8], kyh[0, x])
            high = harmonic(kp[x + 1, END - 8 : END], kyh[1, x])
            gy[0, x] = low
            gy[1, x] = high
            diag = diag + lane_roll(jnp.where(rim, low, 0.0), 8 * local)
            diag = diag + lane_roll(jnp.where(rim, high, 0.0), 8 * local + 6)
        diag = pack_plane(diag, gx[half], 11 * half)
        first = OMEGA_FINE * own_b[half] / jnp.where(diag > 0.0, diag, 1.0)
        store_packed(zs.at[0], half, first)
    start("v", 0, (4, 5))

    def first_part(x, g):
        at = slice(8 * g, 8 * g + 8)
        wall = jnp.where(rim, lane_roll(fze[x // 12], -2 * (4 * (x % 12) + g)), 0.0)
        gz[x, at] = wall
        diag = dg[x, at] + wall
        if g == 0:
            diag = diag + gy[0, x]
        if g == 3:
            diag = diag + gy[1, x]
        if x == 0:
            diag = diag + gx[0, at]
        if x == CX - 1:
            diag = diag + gx[1, at]
        scale = OMEGA_FINE / diag
        first = scale * bv[x, at]
        dg[x, at] = diag
        sc[x, at] = scale
        c0[x, at] = first
        v[0, x + 1, TOP + 8 * g : TOP + 8 * g + 8] = first

    for x in range(CX):
        for g in (range(4) if x in (0, CX - 1) else (0, 3)):
            first_part(x, g)
    start("v", 0, (2, 3, 0, 1))
    for x in range(1, CX - 1):
        for g in (1, 2):
            first_part(x, g)

    def face_rows(block, carry):
        x = 2 * block
        low = (gy[0, x] + gy[0, x + 1])[0:1]
        high = (gy[1, x] + gy[1, x + 1])[7:8]
        wyf[0, pl.ds(block, 1)] = low + lane_roll(low, -1)
        wyf[1, pl.ds(block, 1)] = high + lane_roll(high, -1)
        return carry

    lax.fori_loop(0, BX, face_rows, 0, unroll=True)
    wxf = [quad_sum(gx[side]) for side in range(2)]

    def scale_step(turn, carry):
        for local in range(4):
            x = 4 * turn + local
            scale = sc[x]
            gw[0, x] = scale * fx[x]
            gw[1, x] = scale * fx[x + 1]
            gw[2, x] = scale * fy[x, 0:CY]
            gw[3, x] = scale * fy[x, 1 : CY + 1]
            gw[4, x] = scale * fz[0, x]
            gw[5, x] = scale * fz[1, x]
            gz[x] = scale * gz[x]
            gy[0, x] = scale[0:8] * gy[0, x]
            gy[1, x] = scale[CY - 8 :] * gy[1, x]
        return carry

    lax.fori_loop(0, CX // 4, scale_step, 0)
    gx[0] = sc[0] * gx[0]
    gx[1] = sc[CX - 1] * gx[1]

    def pack_scale(half, carry):
        packed = zero_tile
        for local in range(12):
            packed = pack_plane(packed, gz[12 * half + local], local)
        gzp[half] = packed
        return carry

    lax.fori_loop(0, 2, pack_scale, 0)

    def inner(slot):
        def step(half, carry):
            packed = zero_tile
            for local in range(12):
                x = 12 * half + local
                centre = v[slot, x + 1, cells]
                total = c0[x] + (1.0 - OMEGA_FINE) * centre
                total = total + gw[0, x] * v[slot, x, cells] + gw[1, x] * v[slot, x + 2, cells]
                total = total + gw[2, x] * v[slot, x + 1, TOP - 1 : END - 1]
                total = total + gw[3, x] * v[slot, x + 1, TOP + 1 : END + 1]
                total = total + gw[4, x] * lane_roll(centre, 1) + gw[5, x] * lane_roll(centre, -1)
                tp[x] = total
                packed = pack_plane(packed, total, local)
            zp[half] = packed
            return carry

        lax.fori_loop(0, 2, step, 0)

    def outer_faces(slot, other):
        for half in range(2):
            halo_z = joined(zh.at[slot], half)
            hz[half] = halo_z
            packed = zp[half] + gzp[half] * halo_z
            for local in range(12):
                x = 12 * half + local
                low = jnp.where(rim, gy[0, x] * yh[slot, 0, x], 0.0)
                high = jnp.where(rim, gy[1, x] * yh[slot, 1, x], 0.0)
                packed = packed + lane_roll(low, 8 * local) + lane_roll(high, 8 * local + 6)
            if half == 0:
                packed = pack_plane(packed, gx[0] * xh[slot, 0], 0)
            else:
                packed = pack_plane(packed, gx[1] * xh[slot, 1], 11)
            store_packed(zs.at[other], half, packed)

    def finished(slot, x, g):
        at = slice(8 * g, 8 * g + 8)
        wall = lane_roll(hz[x // 12], -2 * (4 * (x % 12) + g))
        new = tp[x, at] + gz[x, at] * wall
        if g == 0:
            new = new + gy[0, x] * yh[slot, 0, x]
        if g == 3:
            new = new + gy[1, x] * yh[slot, 1, x]
        if x == 0:
            new = new + gx[0, at] * xh[slot, 0, at]
        if x == CX - 1:
            new = new + gx[1, at] * xh[slot, 1, at]
        return new

    def outer_edges(slot, other):
        for x in range(CX):
            for g in (range(4) if x in (0, CX - 1) else (0, 3)):
                v[other, x + 1, TOP + 8 * g : TOP + 8 * g + 8] = finished(slot, x, g)

    def outer_middle(other):
        for x in range(1, CX - 1):
            for g in (1, 2):
                v[other, x + 1, TOP + 8 * g : TOP + 8 * g + 8] = finished(None, x, g)

    inner(0)
    lax.fori_loop(OWN_1, OWN_2, own_step, 0)

    finish("v", 0)
    outer_faces(0, 1)
    start("v", 1, (4, 5))
    outer_edges(0, 1)
    start("v", 1, (2, 3, 0, 1))
    outer_middle(1)

    lax.fori_loop(OWN_2, BX, own_step, 0)
    sum_own = acc[:, :AGG] + acc[:, AGG:]
    mf[0:AGG] = sum_own + sum_own.T
    finish("l")

    def pair_rows(values):
        return jnp.where((lanes_of(values.shape) & 1) == 0, values, lane_roll(row_roll(values, -1), 1))

    def face_blocks(halves, side, summed):
        out = []
        for values in halves:
            if side:
                values = lane_roll(values, 1)
            if summed:
                values = values + lane_roll(values, -8)
                values = values + row_roll(values, -1)
            out.append(jnp.where((lane_8 & 8) == 0, values, lane_roll(row_roll(values, -2), 8)))
        out = jnp.where(odd, lane_roll(out[1], 1), out[0])
        return jnp.where(lane_8 < 96, out, 0.0) if summed else out

    faces_of = []
    for side in range(2):
        faces_of.append((side, squeeze_cells(lxh[side]), squeeze_cells(lc[side * (BX - 1), cells]),
                         squeeze_cells(wxf[side]), range(0, CY, 4)))
        faces_of.append((2 + side, pair_rows(lyh[side]), pair_rows(lys[side]), pair_rows(wyf[side]), range(0, BX, 2)))
        peers = [joined(lzh, half) for half in range(2)]
        faces_of.append((4 + side, face_blocks(peers, side, False), face_blocks(own_l, side, False),
                         face_blocks([fze[0], fze[1]], side, True), (0, 4)))

    for d, peer, own, weight, at_rows in faces_of:
        for n, r in enumerate(at_rows):
            at = slice(r, r + 1)
            place(n * CZ, peer[at], [(own[at], weight[at])])
        depth = len(at_rows) * CZ
        tile = lax.dot_general(xs[:, :depth], ys[:, :depth], NT, preferred_element_type=F32)
        mf[AGG * (d + 1) : AGG * (d + 2)] = tile[:, :AGG] + tile[:, AGG:]

    column = zero_tile
    for r in range(0, 7 * AGG, 8):
        column = column + mf[r : r + 8]
    coarse_diag = jnp.sum(column, axis=0, keepdims=True)
    coarse_scale = OMEGA_COARSE / coarse_diag
    square = (AGG, AGG)
    mf[0:AGG] = jnp.where(rows_of(square) == lanes_of(square), 0.0, mf[0:AGG])
    for t in range(7):
        high, low = split(mf[AGG * t : AGG * (t + 1)] * coarse_scale)
        mm[AGG * t : AGG * (t + 1), :AGG] = high.astype(BF16)
        mm[AGG * t : AGG * (t + 1), AGG:] = low.astype(BF16)

    inner(1)

    def residual_step(turn, carry):
        for local in range(4):
            block = 4 * turn + local
            total = zero_plane
            for x in (2 * block, 2 * block + 1):
                total = total + dg[x] * (tp[x] - v[1, x + 1, cells])
            ew[0, block] = squeeze_cells(quad_sum(total * (1.0 / OMEGA_FINE)))
        return carry

    lax.fori_loop(0, BX // 4, residual_step, 0)
    wanted = rows_of((AGG, CZ)).astype(F32)

    def gather_row(sums, label, value):
        label = jnp.broadcast_to(label, (AGG, CZ))
        return sums + jnp.where(label == wanted, jnp.broadcast_to(value, (AGG, CZ)), 0.0)

    def restrict_step(block, sums):
        for m in range(8):
            at = slice(4 * m, 4 * m + 1)
            sums = gather_row(sums, el[0, block, at], ew[0, block, at])
        return sums

    sums = lax.fori_loop(0, BX, restrict_step, jnp.zeros((AGG, CZ), F32))

    finish("v", 1)
    halo_z = [fze[half] * joined(zh.at[1], half) for half in range(2)]
    inverse = 1.0 / OMEGA_FINE
    for block in range(BX):
        x = 2 * block
        low = sum(gy[0, n] * yh[1, 0, n] * dg[n, 0:8] for n in (x, x + 1))[0:1]
        high = sum(gy[1, n] * yh[1, 1, n] * dg[n, CY - 8 : CY] for n in (x, x + 1))[7:8]
        rows_y[0, block : block + 1] = inverse * (low + lane_roll(low, -1))
        rows_y[1, block : block + 1] = inverse * (high + lane_roll(high, -1))
    for side in range(2):
        plane = gx[side] * xh[1, side] * dg[side * (CX - 1)] * inverse
        values = (squeeze_cells(quad_sum(plane)), pair_rows(rows_y[side]), face_blocks(halo_z, side, True))
        for (d, peer, own, weight, at_rows), value in zip(faces_of[3 * side : 3 * side + 3], values):
            for r in at_rows:
                sums = gather_row(sums, own[r : r + 1], value[r : r + 1])
    high, low = split(sums)
    ones = jnp.ones((16, CZ), BF16)
    coarse_rhs = lax.dot_general(ones, high.astype(BF16), NT, preferred_element_type=F32)
    coarse_rhs = coarse_rhs + lax.dot_general(ones, low.astype(BF16), NT, preferred_element_type=F32)
    first_correction = coarse_scale * coarse_rhs[0:8]

    def halves(values):
        high, low = split(values)
        return jnp.concatenate([high, low], axis=0).astype(BF16)

    def both(values):
        values = values[:, :AGG] + values[:, AGG:]
        return values[0:8] + values[8:16]

    def coarse_step(turn, correction):
        slot = lax.rem(turn, 2)
        cs[slot] = correction
        start("c", slot)
        image = jnp.dot(halves(correction), mm[0:AGG], preferred_element_type=F32)
        base = (1.0 - OMEGA_COARSE) * correction + first_correction
        base = base + both(image)
        finish("c", slot)
        beside = jnp.concatenate([ch[slot, d] for d in range(6)], axis=1)
        return base + both(jnp.dot(halves(beside), mm[AGG:], preferred_element_type=F32))

    correction = lax.fori_loop(0, KC - 1, coarse_step, first_correction)

    def lift_step(half, carry):
        packed = zero_tile
        for local in range(6):
            block = 6 * half + local
            index = lc[block, cells].astype(jnp.int32)
            lifted = jnp.concatenate(
                [jnp.take_along_axis(correction, index[8 * g : 8 * g + 8], axis=1, mode="promise_in_bounds")
                 for g in range(4)], axis=0)
            for n in range(2):
                x = 2 * block + n
                new = v[1, x + 1, cells] + lifted
                v[1, x + 1, cells] = new
                packed = pack_plane(packed, new, 2 * local + n)
        store_packed(zs.at[1], half, packed)
        return carry

    lax.fori_loop(0, 2, lift_step, 0)

    def post_step(turn, carry):
        slot = 1 - lax.rem(turn, 2)

        @pl.when(turn > 0)
        def _():
            finish_send("v", 1 - slot)

        inner(slot)
        finish_recv("v", slot)
        outer_faces(slot, 1 - slot)

        @pl.when(turn < POST - 1)
        def _():
            start("v", 1 - slot, (4, 5))

        outer_edges(slot, 1 - slot)

        @pl.when(turn < POST - 1)
        def _():
            start("v", 1 - slot, (2, 3, 0, 1))

        outer_middle(1 - slot)

        return carry

    start("v", 1)
    lax.fori_loop(0, POST, post_step, 0)
    finish_send("v", 0)
    store = pltpu.make_async_copy(v.at[1, 1 : CX + 1, cells], out_hbm, local_sem.at[0])
    store.start()
    store.wait()


def body(right_side, conductance, absorption, block_agg):
    field = (CX, CY, CZ)
    padded = (CX + 2, CY + 16, CZ)
    any_spec = pl.BlockSpec(memory_space=pl.ANY)

    def f32(*shape):
        return pltpu.VMEM(shape, F32)

    scratch = dict(
        bv=f32(*field), av=f32(*field), kp=f32(*padded), lv=pltpu.VMEM((BX, CY // 2, CZ // 2), jnp.int32),
        v=f32(2, *padded), gw=f32(6, *field), c0=f32(*field), dg=f32(*field), sc=f32(*field),
        fx=f32(CX + 1, CY, CZ), fy=f32(CX, CY + 8, CZ), fz=f32(2, *field),
        gz=f32(*field), gy=f32(2, CX, 8, CZ), gx=f32(2, CY, CZ),
        lc=f32(BX, CY + 16, CZ), el=f32(4, BX, CY, CZ), ew=f32(4, BX, CY, CZ),
        kxh=f32(2, CY, CZ), kyh=f32(2, CX, 8, CZ), kzs=f32(2, 2, 8, CZ), kzh=f32(2, 2, 8, CZ),
        lxh=f32(2, CY, CZ), lys=f32(2, 16, CZ), lyh=f32(2, 16, CZ), lzs=f32(2, 2, 8, CZ), lzh=f32(2, 2, 8, CZ),
        xh=f32(2, 2, CY, CZ), yh=f32(2, 2, CX, 8, CZ), zs=f32(2, 2, 2, 8, CZ), zh=f32(2, 2, 2, 8, CZ),
        fze=f32(2, 8, CZ), wyf=f32(2, 16, CZ), rows_y=f32(2, 16, CZ), zp=f32(2, 8, CZ), gzp=f32(2, 8, CZ), hz=f32(2, 8, CZ), tp=f32(*field),
        xs=pltpu.VMEM((AGG, 8 * CZ), BF16), ys=pltpu.VMEM((2 * AGG, 8 * CZ), BF16),
        acc=f32(AGG, 2 * AGG), mf=f32(7 * AGG, AGG), mm=pltpu.VMEM((7 * AGG, 2 * AGG), BF16),
        cs=f32(2, 8, CZ), ch=f32(2, 6, 8, CZ),
    )
    return pl.pallas_call(
        kernel,
        out_shape=jax.ShapeDtypeStruct(field, F32),
        in_specs=[any_spec] * 4,
        out_specs=any_spec,
        scratch_shapes=list(scratch.values()) + [
            pltpu.SemaphoreType.DMA((4,)), pltpu.SemaphoreType.DMA((6, 6)), pltpu.SemaphoreType.DMA((6, 6)),
        ],
        compiler_params=pltpu.CompilerParams(collective_id=0, has_side_effects=True),
    )(right_side, conductance, absorption, block_agg)


def solution(mesh):
    spec = P("gx", "gy", "gz")
    return jax.shard_map(body, mesh=mesh, in_specs=(spec,) * 4, out_specs=spec, check_vma=False)
```

```python
import jax
import jax.numpy as jnp
from jax import lax
from jax.experimental import pallas as pl
from jax.experimental.pallas import tpu as pltpu
from jax.sharding import PartitionSpec as P

AGG = 128
POST = 4
KC = 8
OMEGA_FINE = 0.8
OMEGA_COARSE = 0.7
CX, CY, CZ = 24, 32, 128
BX = CX // 2
OWN_1, OWN_2 = 2, 6
TOP = 8
END = TOP + CY
AXES = ("gx", "gy", "gz")
F32 = jnp.float32
BF16 = jnp.bfloat16
NT = (((1,), (1,)), ((), ()))


def harmonic(one_side, other_side):
    summed = one_side + other_side
    return 2.0 * (one_side * other_side) / summed


def safe_harmonic(one_side, other_side):
    summed = one_side + other_side
    return 2.0 * (one_side * other_side) / jnp.where(summed > 0.0, summed, 1.0)


def lanes_of(shape):
    return lax.broadcasted_iota(jnp.int32, shape, 1)


def rows_of(shape):
    return lax.broadcasted_iota(jnp.int32, shape, 0)


def lane_roll(values, shift):
    return pltpu.roll(values, shift % CZ if isinstance(shift, int) else shift, 1)


def row_roll(values, shift):
    return pltpu.roll(values, shift % values.shape[0], 0)


def quad_sum(values):
    pair = values + row_roll(values, -1)
    return pair + lane_roll(pair, -1)


def squeeze_cells(values):
    even = (lanes_of(values.shape) & 1) == 0
    return jnp.where(even, values, lane_roll(row_roll(values, -2), 1))


def split(values):
    high = values.astype(BF16).astype(F32)
    return high, values - high


def spread_row(row):
    return jnp.broadcast_to(row, (16, CZ)).astype(BF16)


def kernel(
    b_hbm, k_hbm, a_hbm, l_hbm, out_hbm,
    bv, av, kp, lv, v, gw, c0, dg, sc, fx, fy, fz, gz, gy, gx, lc, el, ew,
    kxh, kyh, kzs, kzh, lxh, lys, lyh, lzs, lzh, xh, yh, zs, zh,
    fze, wyf, rows_y, zp, gzp, hz, tp, xs, ys, acc, mf, mm, cs, ch,
    local_sem, send_sem, recv_sem,
):
    pos = [lax.axis_index(a) for a in AXES]
    size = [lax.axis_size(a) for a in AXES]
    has = []
    dev = []
    for axis in range(3):
        has.append(pos[axis] > 0)
        dev.append({AXES[axis]: pos[axis] - 1})
        has.append(pos[axis] < size[axis] - 1)
        dev.append({AXES[axis]: pos[axis] + 1})
    cells = slice(TOP, END)

    def exchange_of(kind, slot):
        if kind == "k":
            src = [kp.at[1, cells], kp.at[CX, cells], kp.at[1 : CX + 1, TOP : TOP + 1],
                   kp.at[1 : CX + 1, END - 1 : END], kzs.at[0], kzs.at[1]]
            dst = [kxh.at[0], kxh.at[1], kyh.at[0, :, 0:1], kyh.at[1, :, 7:8], kzh.at[0], kzh.at[1]]
            sem = 0
        elif kind == "l":
            src = [lc.at[0, cells], lc.at[BX - 1, cells], lys.at[0], lys.at[1], lzs.at[0], lzs.at[1]]
            dst = [lxh.at[0], lxh.at[1], lyh.at[0], lyh.at[1], lzh.at[0], lzh.at[1]]
            sem = 1
        elif kind == "v":
            src = [v.at[slot, 1, cells], v.at[slot, CX, cells], v.at[slot, 1 : CX + 1, TOP : TOP + 1],
                   v.at[slot, 1 : CX + 1, END - 1 : END], zs.at[slot, 0], zs.at[slot, 1]]
            dst = [xh.at[slot, 0], xh.at[slot, 1], yh.at[slot, 0, :, 0:1], yh.at[slot, 1, :, 7:8],
                   zh.at[slot, 0], zh.at[slot, 1]]
            sem = 2 + slot
        else:
            src = [cs.at[slot]] * 6
            dst = [ch.at[slot, d] for d in range(6)]
            sem = 4 + slot
        return src, dst, sem

    def copy_to(kind, slot, d):
        src, dst, sem = exchange_of(kind, slot)
        return pltpu.make_async_remote_copy(
            src[d], dst[d ^ 1], send_sem.at[sem, d], recv_sem.at[sem, d ^ 1],
            device_id=dev[d], device_id_type=pl.DeviceIdType.MESH)

    def copy_from(kind, slot, d):
        src, dst, sem = exchange_of(kind, slot)
        return pltpu.make_async_remote_copy(
            src[d], dst[d], send_sem.at[sem, d], recv_sem.at[sem, d],
            device_id=dev[d], device_id_type=pl.DeviceIdType.MESH)

    def start(kind, slot=0, sides=(4, 5, 2, 3, 0, 1)):
        for d in sides:
            @pl.when(has[d])
            def _():
                copy_to(kind, slot, d).start()

    def finish_send(kind, slot=0):
        for d in range(6):
            @pl.when(has[d])
            def _():
                copy_to(kind, slot, d).wait_send()

    def finish_recv(kind, slot=0):
        for d in range(6):
            @pl.when(has[d])
            def _():
                copy_from(kind, slot, d).wait_recv()

    def finish(kind, slot=0):
        finish_send(kind, slot)
        finish_recv(kind, slot)

    load_k = pltpu.make_async_copy(k_hbm, kp.at[1 : CX + 1, cells], local_sem.at[0])
    load_l = pltpu.make_async_copy(l_hbm, lv, local_sem.at[1])
    load_a = pltpu.make_async_copy(a_hbm, av, local_sem.at[2])
    load_b = pltpu.make_async_copy(b_hbm, bv, local_sem.at[3])
    load_k.start()
    load_l.start()
    load_a.start()
    load_b.start()

    zero_plane = jnp.zeros((CY, CZ), F32)
    zero_tile = jnp.zeros((8, CZ), F32)
    for side in range(2):
        kxh[side] = zero_plane
        lxh[side] = zero_plane
        lyh[side] = jnp.zeros((16, CZ), F32)
        for half in range(2):
            kzh[side, half] = zero_tile
            lzh[side, half] = zero_tile
        for x in range(CX):
            kyh[side, x] = zero_tile

    barrier = pltpu.get_barrier_semaphore()
    count = jnp.int32(0)
    for d in range(6):
        @pl.when(has[d])
        def _():
            pl.semaphore_signal(barrier, inc=1, device_id=dev[d], device_id_type=pl.DeviceIdType.MESH)
        count = count + has[d].astype(jnp.int32)

    for slot in range(2):
        for d in range(6):
            ch[slot, d] = zero_tile
        for side in range(2):
            xh[slot, side] = zero_plane
            for half in range(2):
                zh[slot, side, half] = zero_tile
            for x in range(CX):
                yh[slot, side, x] = zero_tile
        for edge in (0, CX + 1):
            v[slot, edge, cells] = zero_plane
        for x in range(CX):
            v[slot, x + 1, TOP - 8 : TOP] = zero_tile
            v[slot, x + 1, END : END + 8] = zero_tile
    for edge in (0, CX + 1):
        kp[edge, cells] = zero_plane
    for x in range(CX):
        kp[x + 1, TOP - 8 : TOP] = zero_tile
        kp[x + 1, END : END + 8] = zero_tile
        fy[x, CY : CY + 8] = zero_tile
    fx[0] = zero_plane
    for side in range(2):
        lys[side] = jnp.zeros((16, CZ), F32)
        wyf[side] = jnp.zeros((16, CZ), F32)
        rows_y[side] = jnp.zeros((16, CZ), F32)

    lane_8 = lanes_of((8, CZ))
    rim = (lane_8 == 0) | (lane_8 == CZ - 1)
    odd = (lane_8 & 1) == 1

    def pack_plane(packed, plane, x):
        for g in range(4):
            piece = jnp.where(rim, plane[8 * g : 8 * g + 8], 0.0)
            packed = packed + lane_roll(piece, 2 * (4 * x + g))
        return packed

    def store_packed(ref, half, packed):
        ref[0, half] = lane_roll(packed, -1)
        ref[1, half] = lane_roll(packed, 1)

    def joined(ref, half):
        return jnp.where(odd, ref[1, half], ref[0, half])

    def unpack_plane(packed, x):
        return [lane_roll(packed, -2 * (4 * x + g)) for g in range(4)]

    load_k.wait()
    own_k = []
    for half in range(2):
        packed = zero_tile
        for x in range(12):
            packed = pack_plane(packed, kp[12 * half + x + 1, cells], x)
        store_packed(kzs, half, packed)
        own_k.append(packed)
    pl.semaphore_wait(barrier, count)
    start("k")

    load_l.wait()
    labels = lv[...].reshape(BX * 16, 64).astype(F32).astype(BF16)
    widen = jnp.where(lanes_of((64, CZ)) // 2 == rows_of((64, CZ)), 1.0, 0.0).astype(BF16)
    wide = jnp.dot(labels, widen, preferred_element_type=F32).astype(BF16)
    tall_shape = (BX * CY, BX * 16)
    heighten = jnp.where(rows_of(tall_shape) // 2 == lanes_of(tall_shape), 1.0, 0.0).astype(BF16)
    tall = jnp.dot(heighten, wide, preferred_element_type=F32)
    for x in range(BX):
        lc[x, cells] = tall[x * CY : (x + 1) * CY]
        lc[x, END : END + 8] = zero_tile
        lys[0, x : x + 1] = tall[x * CY : x * CY + 1]
        lys[1, x : x + 1] = tall[x * CY + CY - 1 : x * CY + CY]
    own_l = []
    for half in range(2):
        packed = zero_tile
        for x in range(6):
            plane = lc[6 * half + x, cells]
            packed = pack_plane(packed, plane, 2 * x)
            packed = pack_plane(packed, plane, 2 * x + 1)
        store_packed(lzs, half, packed)
        own_l.append(packed)
    start("l")

    lane = lanes_of((CY, CZ))
    row = rows_of((CY, CZ))
    load_a.wait()

    def faces(x, fx_low):
        centre = kp[x + 1, cells]
        fx_high = harmonic(centre, kp[x + 2, cells])
        fy_low = harmonic(kp[x + 1, TOP - 1 : END - 1], centre)
        fy[x, 0:CY] = fy_low
        fz_low = jnp.where(lane == 0, 0.0, harmonic(lane_roll(centre, 1), centre))
        fz_high = lane_roll(fz_low, -1)
        fy_high = fy[x, 1 : CY + 1]
        fx[x + 1] = fx_high
        fz[0, x] = fz_low
        fz[1, x] = fz_high
        dg[x] = av[x] + fx_low + fx_high + fy_low + fy_high + fz_low + fz_high
        return fx_high, fy_high, fz_high

    def block_step(block, carry):
        fx_low, cut_below = carry
        x = 2 * block
        fx_mid, fy_high_0, fz_high_0 = faces(x, fx_low)
        fx_high, fy_high_1, fz_high_1 = faces(x + 1, fx_mid)
        wx = quad_sum(fx_high)
        wy = fy_high_0 + fy_high_1
        wy = row_roll(wy + lane_roll(wy, -1), -1)
        wz = fz_high_0 + fz_high_1
        wz = lane_roll(wz + row_roll(wz, -1), -1)
        wa = quad_sum(av[x] + av[x + 1])
        own = lc[block, cells]
        lx = lc[jnp.minimum(block + 1, BX - 1), cells]
        ly = lc[block, TOP + 2 : END + 2]
        lz = lane_roll(own, -2)
        lx = jnp.where(lx == own, -1.0, lx)
        ly = jnp.where((ly == own) | (row >= CY - 2), -1.0, ly)
        lz = jnp.where((lz == own) | (lane >= CZ - 2), -1.0, lz)
        cut_x = jnp.where(lx < 0.0, 0.0, wx)
        cut_y = jnp.where(ly < 0.0, 0.0, wy)
        cut_z = jnp.where(lz < 0.0, 0.0, wz)
        leaving = wa + cut_below + cut_x + cut_y + row_roll(cut_y, 2) + cut_z + lane_roll(cut_z, 2)
        ew[0, block] = squeeze_cells(leaving)
        same = ly == lx
        wx = wx + jnp.where(same, wy, 0.0)
        ly = jnp.where(same, -1.0, ly)
        same = lz == lx
        wx = wx + jnp.where(same, wz, 0.0)
        lz = jnp.where(same, -1.0, lz)
        same = lz == ly
        wy = wy + jnp.where(same, wz, 0.0)
        lz = jnp.where(same, -1.0, lz)
        for n, field in enumerate((own, lx, ly, lz)):
            el[n, block] = squeeze_cells(field)
        for n, field in enumerate((wx, wy, wz)):
            ew[n + 1, block] = squeeze_cells(field)
        return fx_high, cut_x

    def block_pair(turn, carry):
        return block_step(2 * turn + 1, block_step(2 * turn, carry))

    lax.fori_loop(0, BX // 2, block_pair, (zero_plane, zero_plane))

    number = rows_of((16, CZ)).astype(F32)
    numbers = [(number + 16.0 * q).astype(BF16) for q in range(8)]
    one = jnp.ones((16, CZ), BF16)
    zero = jnp.zeros((16, CZ), BF16)

    def place(at, lhs_label, pairs):
        lhs_label = spread_row(lhs_label)
        spread = []
        for label, weight in pairs:
            high, low = split(weight)
            spread.append((spread_row(label), spread_row(high), spread_row(low)))
        for q in range(8):
            xs[16 * q : 16 * q + 16, at : at + CZ] = jnp.where(lhs_label == numbers[q], one, zero)
            y_high = zero
            y_low = zero
            for label, high, low in spread:
                hit = label == numbers[q]
                y_high = jnp.where(hit, high, y_high)
                y_low = jnp.where(hit, low, y_low)
            ys[16 * q : 16 * q + 16, at : at + CZ] = y_high
            ys[AGG + 16 * q : AGG + 16 * q + 16, at : at + CZ] = y_low

    acc[...] = jnp.zeros((AGG, 2 * AGG), F32)

    def own_step(block, carry):
        for m in range(8):
            at = slice(4 * m, 4 * m + 1)
            pairs = [(el[n, block, at], ew[n, block, at]) for n in range(1, 4)]
            place(m * CZ, el[0, block, at], pairs)
        acc[...] += lax.dot_general(xs[...], ys[...], NT, preferred_element_type=F32)
        return carry

    lax.fori_loop(0, OWN_1, own_step, 0)
    load_b.wait()
    own_d = []
    own_b = []
    for half in range(2):
        packed_d = zero_tile
        packed_b = zero_tile
        for local in range(12):
            packed_d = pack_plane(packed_d, dg[12 * half + local], local)
            packed_b = pack_plane(packed_b, bv[12 * half + local], local)
        own_d.append(packed_d)
        own_b.append(packed_b)
    finish("k")

    gx[0] = harmonic(kp[1, cells], kxh[0])
    gx[1] = harmonic(kp[CX, cells], kxh[1])
    for half in range(2):
        face_z = safe_harmonic(own_k[half], joined(kzh, half))
        fze[half] = face_z
        diag = own_d[half] + face_z
        for local in range(12):
            x = 12 * half + local
            low = harmonic(kp[x + 1, TOP : TOP + 8], kyh[0, x])
            high = harmonic(kp[x + 1, END - 8 : END], kyh[1, x])
            gy[0, x] = low
            gy[1, x] = high
            diag = diag + lane_roll(jnp.where(rim, low, 0.0), 8 * local)
            diag = diag + lane_roll(jnp.where(rim, high, 0.0), 8 * local + 6)
        diag = pack_plane(diag, gx[half], 11 * half)
        first = OMEGA_FINE * own_b[half] / jnp.where(diag > 0.0, diag, 1.0)
        store_packed(zs.at[0], half, first)
    start("v", 0, (4, 5))

    def first_part(x, g):
        at = slice(8 * g, 8 * g + 8)
        wall = jnp.where(rim, lane_roll(fze[x // 12], -2 * (4 * (x % 12) + g)), 0.0)
        gz[x, at] = wall
        diag = dg[x, at] + wall
        if g == 0:
            diag = diag + gy[0, x]
        if g == 3:
            diag = diag + gy[1, x]
        if x == 0:
            diag = diag + gx[0, at]
        if x == CX - 1:
            diag = diag + gx[1, at]
        scale = OMEGA_FINE / diag
        first = scale * bv[x, at]
        dg[x, at] = diag
        sc[x, at] = scale
        c0[x, at] = first
        v[0, x + 1, TOP + 8 * g : TOP + 8 * g + 8] = first

    for x in range(CX):
        for g in (range(4) if x in (0, CX - 1) else (0, 3)):
            first_part(x, g)
    start("v", 0, (2, 3, 0, 1))
    for x in range(1, CX - 1):
        for g in (1, 2):
            first_part(x, g)

    def face_rows(block, carry):
        x = 2 * block
        low = (gy[0, x] + gy[0, x + 1])[0:1]
        high = (gy[1, x] + gy[1, x + 1])[7:8]
        wyf[0, pl.ds(block, 1)] = low + lane_roll(low, -1)
        wyf[1, pl.ds(block, 1)] = high + lane_roll(high, -1)
        return carry

    lax.fori_loop(0, BX, face_rows, 0, unroll=True)
    wxf = [quad_sum(gx[side]) for side in range(2)]

    def scale_step(turn, carry):
        for local in range(4):
            x = 4 * turn + local
            scale = sc[x]
            gw[0, x] = scale * fx[x]
            gw[1, x] = scale * fx[x + 1]
            gw[2, x] = scale * fy[x, 0:CY]
            gw[3, x] = scale * fy[x, 1 : CY + 1]
            gw[4, x] = scale * fz[0, x]
            gw[5, x] = scale * fz[1, x]
            gz[x] = scale * gz[x]
            gy[0, x] = scale[0:8] * gy[0, x]
            gy[1, x] = scale[CY - 8 :] * gy[1, x]
        return carry

    lax.fori_loop(0, CX // 4, scale_step, 0)
    gx[0] = sc[0] * gx[0]
    gx[1] = sc[CX - 1] * gx[1]

    def pack_scale(half, carry):
        packed = zero_tile
        for local in range(12):
            packed = pack_plane(packed, gz[12 * half + local], local)
        gzp[half] = packed
        return carry

    lax.fori_loop(0, 2, pack_scale, 0)

    def inner(slot):
        def step(half, carry):
            packed = zero_tile
            for local in range(12):
                x = 12 * half + local
                centre = v[slot, x + 1, cells]
                total = c0[x] + (1.0 - OMEGA_FINE) * centre
                total = total + gw[0, x] * v[slot, x, cells] + gw[1, x] * v[slot, x + 2, cells]
                total = total + gw[2, x] * v[slot, x + 1, TOP - 1 : END - 1]
                total = total + gw[3, x] * v[slot, x + 1, TOP + 1 : END + 1]
                total = total + gw[4, x] * lane_roll(centre, 1) + gw[5, x] * lane_roll(centre, -1)
                tp[x] = total
                packed = pack_plane(packed, total, local)
            zp[half] = packed
            return carry

        lax.fori_loop(0, 2, step, 0)

    def outer_faces(slot, other):
        for half in range(2):
            halo_z = joined(zh.at[slot], half)
            hz[half] = halo_z
            packed = zp[half] + gzp[half] * halo_z
            for local in range(12):
                x = 12 * half + local
                low = jnp.where(rim, gy[0, x] * yh[slot, 0, x], 0.0)
                high = jnp.where(rim, gy[1, x] * yh[slot, 1, x], 0.0)
                packed = packed + lane_roll(low, 8 * local) + lane_roll(high, 8 * local + 6)
            if half == 0:
                packed = pack_plane(packed, gx[0] * xh[slot, 0], 0)
            else:
                packed = pack_plane(packed, gx[1] * xh[slot, 1], 11)
            store_packed(zs.at[other], half, packed)

    def finished(slot, x, g):
        at = slice(8 * g, 8 * g + 8)
        wall = lane_roll(hz[x // 12], -2 * (4 * (x % 12) + g))
        new = tp[x, at] + gz[x, at] * wall
        if g == 0:
            new = new + gy[0, x] * yh[slot, 0, x]
        if g == 3:
            new = new + gy[1, x] * yh[slot, 1, x]
        if x == 0:
            new = new + gx[0, at] * xh[slot, 0, at]
        if x == CX - 1:
            new = new + gx[1, at] * xh[slot, 1, at]
        return new

    def outer_edges(slot, other):
        for x in range(CX):
            for g in (range(4) if x in (0, CX - 1) else (0, 3)):
                v[other, x + 1, TOP + 8 * g : TOP + 8 * g + 8] = finished(slot, x, g)

    def outer_middle(other):
        for x in range(1, CX - 1):
            for g in (1, 2):
                v[other, x + 1, TOP + 8 * g : TOP + 8 * g + 8] = finished(None, x, g)

    wanted = rows_of((AGG, CZ)).astype(F32)

    def gather_row(sums, label, value):
        label = jnp.broadcast_to(label, (AGG, CZ))
        return sums + jnp.where(label == wanted, jnp.broadcast_to(value, (AGG, CZ)), 0.0)

    def restrict_step(block, sums):
        for m in range(8):
            at = slice(4 * m, 4 * m + 1)
            sums = gather_row(sums, el[0, block, at], ew[0, block, at])
        return sums

    def aggregate_row(sums):
        high, low = split(sums)
        ones = jnp.ones((16, CZ), BF16)
        out = lax.dot_general(ones, high.astype(BF16), NT, preferred_element_type=F32)
        return (out + lax.dot_general(ones, low.astype(BF16), NT, preferred_element_type=F32))[0:8]

    inner(0)
    diag_sums = lax.fori_loop(0, BX, restrict_step, jnp.zeros((AGG, CZ), F32))
    lax.fori_loop(OWN_1, OWN_2, own_step, 0)

    finish("v", 0)
    outer_faces(0, 1)
    start("v", 1, (4, 5))
    outer_edges(0, 1)
    start("v", 1, (2, 3, 0, 1))
    outer_middle(1)

    finish("l")

    def pair_rows(values):
        return jnp.where((lanes_of(values.shape) & 1) == 0, values, lane_roll(row_roll(values, -1), 1))

    def face_blocks(halves, side, summed):
        out = []
        for values in halves:
            if side:
                values = lane_roll(values, 1)
            if summed:
                values = values + lane_roll(values, -8)
                values = values + row_roll(values, -1)
            out.append(jnp.where((lane_8 & 8) == 0, values, lane_roll(row_roll(values, -2), 8)))
        out = jnp.where(odd, lane_roll(out[1], 1), out[0])
        return jnp.where(lane_8 < 96, out, 0.0) if summed else out

    faces_of = []
    for side in range(2):
        faces_of.append((side, squeeze_cells(lxh[side]), squeeze_cells(lc[side * (BX - 1), cells]),
                         squeeze_cells(wxf[side]), range(0, CY, 4)))
        faces_of.append((2 + side, pair_rows(lyh[side]), pair_rows(lys[side]), pair_rows(wyf[side]), range(0, BX, 2)))
        peers = [joined(lzh, half) for half in range(2)]
        faces_of.append((4 + side, face_blocks(peers, side, False), face_blocks(own_l, side, False),
                         face_blocks([fze[0], fze[1]], side, True), (0, 4)))

    for d, peer, own, weight, at_rows in faces_of:
        for n, r in enumerate(at_rows):
            at = slice(r, r + 1)
            place(n * CZ, peer[at], [(own[at], weight[at])])
        depth = len(at_rows) * CZ
        tile = lax.dot_general(xs[:, :depth], ys[:, :depth], NT, preferred_element_type=F32)
        mf[AGG * d : AGG * (d + 1)] = tile[:, :AGG] + tile[:, AGG:]
        for r in at_rows:
            diag_sums = gather_row(diag_sums, own[r : r + 1], weight[r : r + 1])

    coarse_scale = OMEGA_COARSE / aggregate_row(diag_sums)

    def store_tile(t, tile):
        high, low = split(tile * coarse_scale[0:1])
        mm[AGG * t : AGG * (t + 1), :AGG] = high.astype(BF16)
        mm[AGG * t : AGG * (t + 1), AGG:] = low.astype(BF16)

    for d in range(6):
        store_tile(d + 1, mf[AGG * d : AGG * (d + 1)])

    inner(1)

    def residual_step(turn, carry):
        for local in range(4):
            block = 4 * turn + local
            total = zero_plane
            for x in (2 * block, 2 * block + 1):
                total = total + dg[x] * (tp[x] - v[1, x + 1, cells])
            ew[0, block] = squeeze_cells(quad_sum(total * (1.0 / OMEGA_FINE)))
        return carry

    lax.fori_loop(0, BX // 4, residual_step, 0)
    sums = lax.fori_loop(0, BX, restrict_step, jnp.zeros((AGG, CZ), F32))

    finish("v", 1)
    halo_z = [fze[half] * joined(zh.at[1], half) for half in range(2)]
    inverse = 1.0 / OMEGA_FINE
    for block in range(BX):
        x = 2 * block
        low = sum(gy[0, n] * yh[1, 0, n] * dg[n, 0:8] for n in (x, x + 1))[0:1]
        high = sum(gy[1, n] * yh[1, 1, n] * dg[n, CY - 8 : CY] for n in (x, x + 1))[7:8]
        rows_y[0, block : block + 1] = inverse * (low + lane_roll(low, -1))
        rows_y[1, block : block + 1] = inverse * (high + lane_roll(high, -1))
    for side in range(2):
        plane = gx[side] * xh[1, side] * dg[side * (CX - 1)] * inverse
        values = (squeeze_cells(quad_sum(plane)), pair_rows(rows_y[side]), face_blocks(halo_z, side, True))
        for (d, peer, own, weight, at_rows), value in zip(faces_of[3 * side : 3 * side + 3], values):
            for r in at_rows:
                sums = gather_row(sums, own[r : r + 1], value[r : r + 1])
    first_correction = coarse_scale * aggregate_row(sums)

    def halves(values):
        high, low = split(values)
        return jnp.concatenate([high, low], axis=0).astype(BF16)

    def both(values):
        values = values[:, :AGG] + values[:, AGG:]
        return values[0:8] + values[8:16]

    def coarse_step(turn, correction, first=False):
        slot = 0 if first else lax.rem(turn, 2)
        cs[slot] = correction
        start("c", slot)
        if first:
            lax.fori_loop(OWN_2, BX, own_step, 0)
            sum_own = acc[:, :AGG] + acc[:, AGG:]
            store_tile(0, sum_own + sum_own.T)
        image = jnp.dot(halves(correction), mm[0:AGG], preferred_element_type=F32)
        base = (1.0 - OMEGA_COARSE) * correction + first_correction
        base = base + both(image)
        finish("c", slot)
        beside = jnp.concatenate([ch[slot, d] for d in range(6)], axis=1)
        return base + both(jnp.dot(halves(beside), mm[AGG:], preferred_element_type=F32))

    correction = lax.fori_loop(1, KC - 1, coarse_step, coarse_step(0, first_correction, True))

    def lift_step(half, carry):
        packed = zero_tile
        for local in range(6):
            block = 6 * half + local
            index = lc[block, cells].astype(jnp.int32)
            lifted = jnp.concatenate(
                [jnp.take_along_axis(correction, index[8 * g : 8 * g + 8], axis=1, mode="promise_in_bounds")
                 for g in range(4)], axis=0)
            for n in range(2):
                x = 2 * block + n
                new = v[1, x + 1, cells] + lifted
                v[1, x + 1, cells] = new
                packed = pack_plane(packed, new, 2 * local + n)
        store_packed(zs.at[1], half, packed)
        return carry

    lax.fori_loop(0, 2, lift_step, 0)

    def post_step(turn, carry):
        slot = 1 - lax.rem(turn, 2)

        @pl.when(turn > 0)
        def _():
            finish_send("v", 1 - slot)

        inner(slot)
        finish_recv("v", slot)
        outer_faces(slot, 1 - slot)

        @pl.when(turn < POST - 1)
        def _():
            start("v", 1 - slot, (4, 5))

        outer_edges(slot, 1 - slot)

        @pl.when(turn < POST - 1)
        def _():
            start("v", 1 - slot, (2, 3, 0, 1))

        outer_middle(1 - slot)

        return carry

    start("v", 1)
    lax.fori_loop(0, POST, post_step, 0)
    finish_send("v", 0)
    store = pltpu.make_async_copy(v.at[1, 1 : CX + 1, cells], out_hbm, local_sem.at[0])
    store.start()
    store.wait()


def body(right_side, conductance, absorption, block_agg):
    field = (CX, CY, CZ)
    padded = (CX + 2, CY + 16, CZ)
    any_spec = pl.BlockSpec(memory_space=pl.ANY)

    def f32(*shape):
        return pltpu.VMEM(shape, F32)

    scratch = dict(
        bv=f32(*field), av=f32(*field), kp=f32(*padded), lv=pltpu.VMEM((BX, CY // 2, CZ // 2), jnp.int32),
        v=f32(2, *padded), gw=f32(6, *field), c0=f32(*field), dg=f32(*field), sc=f32(*field),
        fx=f32(CX + 1, CY, CZ), fy=f32(CX, CY + 8, CZ), fz=f32(2, *field),
        gz=f32(*field), gy=f32(2, CX, 8, CZ), gx=f32(2, CY, CZ),
        lc=f32(BX, CY + 16, CZ), el=f32(4, BX, CY, CZ), ew=f32(4, BX, CY, CZ),
        kxh=f32(2, CY, CZ), kyh=f32(2, CX, 8, CZ), kzs=f32(2, 2, 8, CZ), kzh=f32(2, 2, 8, CZ),
        lxh=f32(2, CY, CZ), lys=f32(2, 16, CZ), lyh=f32(2, 16, CZ), lzs=f32(2, 2, 8, CZ), lzh=f32(2, 2, 8, CZ),
        xh=f32(2, 2, CY, CZ), yh=f32(2, 2, CX, 8, CZ), zs=f32(2, 2, 2, 8, CZ), zh=f32(2, 2, 2, 8, CZ),
        fze=f32(2, 8, CZ), wyf=f32(2, 16, CZ), rows_y=f32(2, 16, CZ), zp=f32(2, 8, CZ), gzp=f32(2, 8, CZ), hz=f32(2, 8, CZ), tp=f32(*field),
        xs=pltpu.VMEM((AGG, 8 * CZ), BF16), ys=pltpu.VMEM((2 * AGG, 8 * CZ), BF16),
        acc=f32(AGG, 2 * AGG), mf=f32(6 * AGG, AGG), mm=pltpu.VMEM((7 * AGG, 2 * AGG), BF16),
        cs=f32(2, 8, CZ), ch=f32(2, 6, 8, CZ),
    )
    return pl.pallas_call(
        kernel,
        out_shape=jax.ShapeDtypeStruct(field, F32),
        in_specs=[any_spec] * 4,
        out_specs=any_spec,
        scratch_shapes=list(scratch.values()) + [
            pltpu.SemaphoreType.DMA((4,)), pltpu.SemaphoreType.DMA((6, 6)), pltpu.SemaphoreType.DMA((6, 6)),
        ],
        compiler_params=pltpu.CompilerParams(collective_id=0, has_side_effects=True),
    )(right_side, conductance, absorption, block_agg)


def solution(mesh):
    spec = P("gx", "gy", "gz")
    return jax.shard_map(body, mesh=mesh, in_specs=(spec,) * 4, out_specs=spec, check_vma=False)
```

```python
import jax
import jax.numpy as jnp
from jax import lax
from jax.experimental import pallas as pl
from jax.experimental.pallas import tpu as pltpu
from jax.sharding import PartitionSpec as P

AGG = 128
POST = 4
KC = 8
OMEGA_FINE = 0.8
OMEGA_COARSE = 0.7
CX, CY, CZ = 24, 32, 128
BX = CX // 2
OWN_1, OWN_2 = 1, 5
TOP = 8
END = TOP + CY
AXES = ("gx", "gy", "gz")
F32 = jnp.float32
BF16 = jnp.bfloat16
NT = (((1,), (1,)), ((), ()))


def harmonic(one_side, other_side):
    summed = one_side + other_side
    return 2.0 * (one_side * other_side) / summed


def safe_harmonic(one_side, other_side):
    summed = one_side + other_side
    return 2.0 * (one_side * other_side) / jnp.where(summed > 0.0, summed, 1.0)


def lanes_of(shape):
    return lax.broadcasted_iota(jnp.int32, shape, 1)


def rows_of(shape):
    return lax.broadcasted_iota(jnp.int32, shape, 0)


def lane_roll(values, shift):
    return pltpu.roll(values, shift % CZ if isinstance(shift, int) else shift, 1)


def row_roll(values, shift):
    return pltpu.roll(values, shift % values.shape[0], 0)


def quad_sum(values):
    pair = values + row_roll(values, -1)
    return pair + lane_roll(pair, -1)


def squeeze_cells(values):
    even = (lanes_of(values.shape) & 1) == 0
    return jnp.where(even, values, lane_roll(row_roll(values, -2), 1))


def split(values):
    high = values.astype(BF16).astype(F32)
    return high, values - high


def spread_row(row):
    return jnp.broadcast_to(row, (16, CZ)).astype(BF16)


def kernel(
    b_hbm, k_hbm, a_hbm, l_hbm, out,
    bv, av, kp, lv, v, gw, c0, dg, sc, fx, fy, fz, gz, gy, gx, lc, el, ew,
    kxh, kyh, kzs, kzh, lxh, lys, lyh, lzs, lzh, xh, yh, zs, zh,
    fze, wyf, rows_y, zp, gzp, hz, tp, xs, ys, acc, mf, mm, cs, ch,
    local_sem, send_sem, recv_sem,
):
    pos = [lax.axis_index(a) for a in AXES]
    size = [lax.axis_size(a) for a in AXES]
    has = []
    dev = []
    for axis in range(3):
        has.append(pos[axis] > 0)
        dev.append({AXES[axis]: pos[axis] - 1})
        has.append(pos[axis] < size[axis] - 1)
        dev.append({AXES[axis]: pos[axis] + 1})
    cells = slice(TOP, END)

    def exchange_of(kind, slot):
        if kind == "k":
            src = [kp.at[1, cells], kp.at[CX, cells], kp.at[1 : CX + 1, TOP : TOP + 1],
                   kp.at[1 : CX + 1, END - 1 : END], kzs.at[0], kzs.at[1]]
            dst = [kxh.at[0], kxh.at[1], kyh.at[0, :, 0:1], kyh.at[1, :, 7:8], kzh.at[0], kzh.at[1]]
            sem = 0
        elif kind == "l":
            src = [lc.at[0, cells], lc.at[BX - 1, cells], lys.at[0], lys.at[1], lzs.at[0], lzs.at[1]]
            dst = [lxh.at[0], lxh.at[1], lyh.at[0], lyh.at[1], lzh.at[0], lzh.at[1]]
            sem = 1
        elif kind == "v":
            src = [v.at[slot, 1, cells], v.at[slot, CX, cells], v.at[slot, 1 : CX + 1, TOP : TOP + 1],
                   v.at[slot, 1 : CX + 1, END - 1 : END], zs.at[slot, 0], zs.at[slot, 1]]
            dst = [xh.at[slot, 0], xh.at[slot, 1], yh.at[slot, 0, :, 0:1], yh.at[slot, 1, :, 7:8],
                   zh.at[slot, 0], zh.at[slot, 1]]
            sem = 2 + slot
        else:
            src = [cs.at[slot]] * 6
            dst = [ch.at[slot, d] for d in range(6)]
            sem = 4 + slot
        return src, dst, sem

    def copy_to(kind, slot, d):
        src, dst, sem = exchange_of(kind, slot)
        return pltpu.make_async_remote_copy(
            src[d], dst[d ^ 1], send_sem.at[sem, d], recv_sem.at[sem, d ^ 1],
            device_id=dev[d], device_id_type=pl.DeviceIdType.MESH)

    def copy_from(kind, slot, d):
        src, dst, sem = exchange_of(kind, slot)
        return pltpu.make_async_remote_copy(
            src[d], dst[d], send_sem.at[sem, d], recv_sem.at[sem, d],
            device_id=dev[d], device_id_type=pl.DeviceIdType.MESH)

    def start(kind, slot=0, sides=(4, 5, 2, 3, 0, 1)):
        for d in sides:
            @pl.when(has[d])
            def _():
                copy_to(kind, slot, d).start()

    def finish_send(kind, slot=0):
        for d in range(6):
            @pl.when(has[d])
            def _():
                copy_to(kind, slot, d).wait_send()

    def finish_recv(kind, slot=0):
        for d in range(6):
            @pl.when(has[d])
            def _():
                copy_from(kind, slot, d).wait_recv()

    def finish(kind, slot=0):
        finish_send(kind, slot)
        finish_recv(kind, slot)

    load_k = pltpu.make_async_copy(k_hbm, kp.at[1 : CX + 1, cells], local_sem.at[0])
    load_l = pltpu.make_async_copy(l_hbm, lv, local_sem.at[1])
    load_a = pltpu.make_async_copy(a_hbm, av, local_sem.at[2])
    load_b = pltpu.make_async_copy(b_hbm, bv, local_sem.at[3])
    load_k.start()
    load_l.start()
    load_a.start()
    load_b.start()

    zero_plane = jnp.zeros((CY, CZ), F32)
    zero_tile = jnp.zeros((8, CZ), F32)
    for side in range(2):
        kxh[side] = zero_plane
        lxh[side] = zero_plane
        lyh[side] = jnp.zeros((16, CZ), F32)
        for half in range(2):
            kzh[side, half] = zero_tile
            lzh[side, half] = zero_tile
        for x in range(CX):
            kyh[side, x] = zero_tile

    barrier = pltpu.get_barrier_semaphore()
    count = jnp.int32(0)
    for d in range(6):
        @pl.when(has[d])
        def _():
            pl.semaphore_signal(barrier, inc=1, device_id=dev[d], device_id_type=pl.DeviceIdType.MESH)
        count = count + has[d].astype(jnp.int32)

    for slot in range(2):
        for d in range(6):
            ch[slot, d] = zero_tile
        for side in range(2):
            xh[slot, side] = zero_plane
            for half in range(2):
                zh[slot, side, half] = zero_tile
            for x in range(CX):
                yh[slot, side, x] = zero_tile
        for edge in (0, CX + 1):
            v[slot, edge, cells] = zero_plane
        for x in range(CX):
            v[slot, x + 1, TOP - 8 : TOP] = zero_tile
            v[slot, x + 1, END : END + 8] = zero_tile
    for edge in (0, CX + 1):
        kp[edge, cells] = zero_plane
    for x in range(CX):
        kp[x + 1, TOP - 8 : TOP] = zero_tile
        kp[x + 1, END : END + 8] = zero_tile
        fy[x, CY : CY + 8] = zero_tile
    fx[0] = zero_plane
    for side in range(2):
        lys[side] = jnp.zeros((16, CZ), F32)
        wyf[side] = jnp.zeros((16, CZ), F32)
        rows_y[side] = jnp.zeros((16, CZ), F32)

    lane_8 = lanes_of((8, CZ))
    rim = (lane_8 == 0) | (lane_8 == CZ - 1)
    odd = (lane_8 & 1) == 1

    def pack_plane(packed, plane, x):
        for g in range(4):
            piece = jnp.where(rim, plane[8 * g : 8 * g + 8], 0.0)
            packed = packed + lane_roll(piece, 2 * (4 * x + g))
        return packed

    def store_packed(ref, half, packed):
        ref[0, half] = lane_roll(packed, -1)
        ref[1, half] = lane_roll(packed, 1)

    def joined(ref, half):
        return jnp.where(odd, ref[1, half], ref[0, half])

    def unpack_plane(packed, x):
        return [lane_roll(packed, -2 * (4 * x + g)) for g in range(4)]

    load_k.wait()
    own_k = []
    for half in range(2):
        packed = zero_tile
        for x in range(12):
            packed = pack_plane(packed, kp[12 * half + x + 1, cells], x)
        store_packed(kzs, half, packed)
        own_k.append(packed)
    pl.semaphore_wait(barrier, count)
    start("k")

    load_l.wait()
    labels = lv[...].reshape(BX * 16, 64).astype(F32).astype(BF16)
    widen = jnp.where(lanes_of((64, CZ)) // 2 == rows_of((64, CZ)), 1.0, 0.0).astype(BF16)
    wide = jnp.dot(labels, widen, preferred_element_type=F32).astype(BF16)
    tall_shape = (BX * CY, BX * 16)
    heighten = jnp.where(rows_of(tall_shape) // 2 == lanes_of(tall_shape), 1.0, 0.0).astype(BF16)
    tall = jnp.dot(heighten, wide, preferred_element_type=F32)
    for x in range(BX):
        lc[x, cells] = tall[x * CY : (x + 1) * CY]
        lc[x, END : END + 8] = zero_tile
        lys[0, x : x + 1] = tall[x * CY : x * CY + 1]
        lys[1, x : x + 1] = tall[x * CY + CY - 1 : x * CY + CY]
    own_l = []
    for half in range(2):
        packed = zero_tile
        for x in range(6):
            plane = lc[6 * half + x, cells]
            packed = pack_plane(packed, plane, 2 * x)
            packed = pack_plane(packed, plane, 2 * x + 1)
        store_packed(lzs, half, packed)
        own_l.append(packed)
    start("l")

    lane = lanes_of((CY, CZ))
    row = rows_of((CY, CZ))
    load_a.wait()

    def faces(x, fx_low):
        centre = kp[x + 1, cells]
        fx_high = harmonic(centre, kp[x + 2, cells])
        fy_low = harmonic(kp[x + 1, TOP - 1 : END - 1], centre)
        fy[x, 0:CY] = fy_low
        fz_low = jnp.where(lane == 0, 0.0, harmonic(lane_roll(centre, 1), centre))
        fz_high = lane_roll(fz_low, -1)
        fy_high = fy[x, 1 : CY + 1]
        fx[x + 1] = fx_high
        fz[0, x] = fz_low
        fz[1, x] = fz_high
        dg[x] = av[x] + fx_low + fx_high + fy_low + fy_high + fz_low + fz_high
        return fx_high, fy_high, fz_high

    def block_step(block, carry):
        fx_low, cut_below = carry
        x = 2 * block
        fx_mid, fy_high_0, fz_high_0 = faces(x, fx_low)
        fx_high, fy_high_1, fz_high_1 = faces(x + 1, fx_mid)
        wx = quad_sum(fx_high)
        wy = fy_high_0 + fy_high_1
        wy = row_roll(wy + lane_roll(wy, -1), -1)
        wz = fz_high_0 + fz_high_1
        wz = lane_roll(wz + row_roll(wz, -1), -1)
        wa = quad_sum(av[x] + av[x + 1])
        own = lc[block, cells]
        lx = lc[min(block + 1, BX - 1), cells]
        ly = lc[block, TOP + 2 : END + 2]
        lz = lane_roll(own, -2)
        lx = jnp.where(lx == own, -1.0, lx)
        ly = jnp.where((ly == own) | (row >= CY - 2), -1.0, ly)
        lz = jnp.where((lz == own) | (lane >= CZ - 2), -1.0, lz)
        cut_x = jnp.where(lx < 0.0, 0.0, wx)
        cut_y = jnp.where(ly < 0.0, 0.0, wy)
        cut_z = jnp.where(lz < 0.0, 0.0, wz)
        leaving = wa + cut_below + cut_x + cut_y + row_roll(cut_y, 2) + cut_z + lane_roll(cut_z, 2)
        ew[0, block] = squeeze_cells(leaving)
        same = ly == lx
        wx = wx + jnp.where(same, wy, 0.0)
        ly = jnp.where(same, -1.0, ly)
        same = lz == lx
        wx = wx + jnp.where(same, wz, 0.0)
        lz = jnp.where(same, -1.0, lz)
        same = lz == ly
        wy = wy + jnp.where(same, wz, 0.0)
        lz = jnp.where(same, -1.0, lz)
        for n, field in enumerate((own, lx, ly, lz)):
            el[n, block] = squeeze_cells(field)
        for n, field in enumerate((wx, wy, wz)):
            ew[n + 1, block] = squeeze_cells(field)
        return fx_high, cut_x

    below = (zero_plane, zero_plane)
    for block in range(BX):
        below = block_step(block, below)

    number = rows_of((16, CZ)).astype(F32)
    numbers = [(number + 16.0 * q).astype(BF16) for q in range(8)]
    one = jnp.ones((16, CZ), BF16)
    zero = jnp.zeros((16, CZ), BF16)

    def place(at, lhs_label, pairs):
        lhs_label = spread_row(lhs_label)
        spread = []
        for label, weight in pairs:
            high, low = split(weight)
            spread.append((spread_row(label), spread_row(high), spread_row(low)))
        for q in range(8):
            xs[16 * q : 16 * q + 16, at : at + CZ] = jnp.where(lhs_label == numbers[q], one, zero)
            y_high = zero
            y_low = zero
            for label, high, low in spread:
                hit = label == numbers[q]
                y_high = jnp.where(hit, high, y_high)
                y_low = jnp.where(hit, low, y_low)
            ys[16 * q : 16 * q + 16, at : at + CZ] = y_high
            ys[AGG + 16 * q : AGG + 16 * q + 16, at : at + CZ] = y_low

    acc[...] = jnp.zeros((AGG, 2 * AGG), F32)

    def own_step(block, carry):
        for m in range(8):
            at = slice(4 * m, 4 * m + 1)
            pairs = [(el[n, block, at], ew[n, block, at]) for n in range(1, 4)]
            place(m * CZ, el[0, block, at], pairs)
        acc[...] += lax.dot_general(xs[...], ys[...], NT, preferred_element_type=F32)
        return carry

    lax.fori_loop(0, OWN_1, own_step, 0)
    load_b.wait()
    own_d = []
    own_b = []
    for half in range(2):
        packed_d = zero_tile
        packed_b = zero_tile
        for local in range(12):
            packed_d = pack_plane(packed_d, dg[12 * half + local], local)
            packed_b = pack_plane(packed_b, bv[12 * half + local], local)
        own_d.append(packed_d)
        own_b.append(packed_b)
    finish("k")

    gx[0] = harmonic(kp[1, cells], kxh[0])
    gx[1] = harmonic(kp[CX, cells], kxh[1])
    for half in range(2):
        face_z = safe_harmonic(own_k[half], joined(kzh, half))
        fze[half] = face_z
        diag = own_d[half] + face_z
        for local in range(12):
            x = 12 * half + local
            low = harmonic(kp[x + 1, TOP : TOP + 8], kyh[0, x])
            high = harmonic(kp[x + 1, END - 8 : END], kyh[1, x])
            gy[0, x] = low
            gy[1, x] = high
            diag = diag + lane_roll(jnp.where(rim, low, 0.0), 8 * local)
            diag = diag + lane_roll(jnp.where(rim, high, 0.0), 8 * local + 6)
        diag = pack_plane(diag, gx[half], 11 * half)
        first = OMEGA_FINE * own_b[half] / jnp.where(diag > 0.0, diag, 1.0)
        store_packed(zs.at[0], half, first)
    start("v", 0, (4, 5))

    def first_part(x, g):
        at = slice(8 * g, 8 * g + 8)
        wall = jnp.where(rim, lane_roll(fze[x // 12], -2 * (4 * (x % 12) + g)), 0.0)
        gz[x, at] = wall
        diag = dg[x, at] + wall
        if g == 0:
            diag = diag + gy[0, x]
        if g == 3:
            diag = diag + gy[1, x]
        if x == 0:
            diag = diag + gx[0, at]
        if x == CX - 1:
            diag = diag + gx[1, at]
        scale = OMEGA_FINE / diag
        first = scale * bv[x, at]
        dg[x, at] = diag
        sc[x, at] = scale
        c0[x, at] = first
        v[0, x + 1, TOP + 8 * g : TOP + 8 * g + 8] = first

    for x in range(CX):
        for g in (range(4) if x in (0, CX - 1) else (0, 3)):
            first_part(x, g)
    start("v", 0, (2, 3, 0, 1))
    for x in range(1, CX - 1):
        for g in (1, 2):
            first_part(x, g)

    def face_rows(block, carry):
        x = 2 * block
        low = (gy[0, x] + gy[0, x + 1])[0:1]
        high = (gy[1, x] + gy[1, x + 1])[7:8]
        wyf[0, pl.ds(block, 1)] = low + lane_roll(low, -1)
        wyf[1, pl.ds(block, 1)] = high + lane_roll(high, -1)
        return carry

    lax.fori_loop(0, BX, face_rows, 0, unroll=True)
    wxf = [quad_sum(gx[side]) for side in range(2)]

    def scale_step(turn, carry):
        for local in range(4):
            x = 4 * turn + local
            scale = sc[x]
            gw[0, x] = scale * fx[x]
            gw[1, x] = scale * fx[x + 1]
            gw[2, x] = scale * fy[x, 0:CY]
            gw[3, x] = scale * fy[x, 1 : CY + 1]
            gw[4, x] = scale * fz[0, x]
            gw[5, x] = scale * fz[1, x]
            gz[x] = scale * gz[x]
            gy[0, x] = scale[0:8] * gy[0, x]
            gy[1, x] = scale[CY - 8 :] * gy[1, x]
        return carry

    lax.fori_loop(0, CX // 4, scale_step, 0)
    gx[0] = sc[0] * gx[0]
    gx[1] = sc[CX - 1] * gx[1]

    def pack_scale(half, carry):
        packed = zero_tile
        for local in range(12):
            packed = pack_plane(packed, gz[12 * half + local], local)
        gzp[half] = packed
        return carry

    lax.fori_loop(0, 2, pack_scale, 0)

    def inner(slot):
        def step(half, carry):
            packed = zero_tile
            for local in range(12):
                x = 12 * half + local
                centre = v[slot, x + 1, cells]
                total = c0[x] + (1.0 - OMEGA_FINE) * centre
                total = total + gw[0, x] * v[slot, x, cells] + gw[1, x] * v[slot, x + 2, cells]
                total = total + gw[2, x] * v[slot, x + 1, TOP - 1 : END - 1]
                total = total + gw[3, x] * v[slot, x + 1, TOP + 1 : END + 1]
                total = total + gw[4, x] * lane_roll(centre, 1) + gw[5, x] * lane_roll(centre, -1)
                tp[x] = total
                packed = pack_plane(packed, total, local)
            zp[half] = packed
            return carry

        lax.fori_loop(0, 2, step, 0)

    def outer_faces(slot, other):
        for half in range(2):
            halo_z = joined(zh.at[slot], half)
            hz[half] = halo_z
            packed = zp[half] + gzp[half] * halo_z
            for local in range(12):
                x = 12 * half + local
                low = jnp.where(rim, gy[0, x] * yh[slot, 0, x], 0.0)
                high = jnp.where(rim, gy[1, x] * yh[slot, 1, x], 0.0)
                packed = packed + lane_roll(low, 8 * local) + lane_roll(high, 8 * local + 6)
            if half == 0:
                packed = pack_plane(packed, gx[0] * xh[slot, 0], 0)
            else:
                packed = pack_plane(packed, gx[1] * xh[slot, 1], 11)
            store_packed(zs.at[other], half, packed)

    def finished(slot, x, g):
        at = slice(8 * g, 8 * g + 8)
        wall = lane_roll(hz[x // 12], -2 * (4 * (x % 12) + g))
        new = tp[x, at] + gz[x, at] * wall
        if g == 0:
            new = new + gy[0, x] * yh[slot, 0, x]
        if g == 3:
            new = new + gy[1, x] * yh[slot, 1, x]
        if x == 0:
            new = new + gx[0, at] * xh[slot, 0, at]
        if x == CX - 1:
            new = new + gx[1, at] * xh[slot, 1, at]
        return new

    def outer_edges(slot, other):
        for x in range(CX):
            for g in (range(4) if x in (0, CX - 1) else (0, 3)):
                v[other, x + 1, TOP + 8 * g : TOP + 8 * g + 8] = finished(slot, x, g)

    def outer_middle(other):
        for x in range(1, CX - 1):
            for g in (1, 2):
                v[other, x + 1, TOP + 8 * g : TOP + 8 * g + 8] = finished(None, x, g)

    wanted = rows_of((AGG, CZ)).astype(F32)

    def gather_row(sums, label, value):
        label = jnp.broadcast_to(label, (AGG, CZ))
        return sums + jnp.where(label == wanted, jnp.broadcast_to(value, (AGG, CZ)), 0.0)

    def restrict_step(block, sums):
        for m in range(8):
            at = slice(4 * m, 4 * m + 1)
            sums = gather_row(sums, el[0, block, at], ew[0, block, at])
        return sums

    def aggregate_row(sums):
        high, low = split(sums)
        ones = jnp.ones((16, CZ), BF16)
        out = lax.dot_general(ones, high.astype(BF16), NT, preferred_element_type=F32)
        return (out + lax.dot_general(ones, low.astype(BF16), NT, preferred_element_type=F32))[0:8]

    inner(0)
    diag_sums = lax.fori_loop(0, BX, restrict_step, jnp.zeros((AGG, CZ), F32))
    lax.fori_loop(OWN_1, OWN_2, own_step, 0)

    finish("v", 0)
    outer_faces(0, 1)
    start("v", 1, (4, 5))
    outer_edges(0, 1)
    start("v", 1, (2, 3, 0, 1))
    outer_middle(1)

    finish("l")

    def pair_rows(values):
        return jnp.where((lanes_of(values.shape) & 1) == 0, values, lane_roll(row_roll(values, -1), 1))

    def face_blocks(halves, side, summed):
        out = []
        for values in halves:
            if side:
                values = lane_roll(values, 1)
            if summed:
                values = values + lane_roll(values, -8)
                values = values + row_roll(values, -1)
            out.append(jnp.where((lane_8 & 8) == 0, values, lane_roll(row_roll(values, -2), 8)))
        out = jnp.where(odd, lane_roll(out[1], 1), out[0])
        return jnp.where(lane_8 < 96, out, 0.0) if summed else out

    faces_of = []
    for side in range(2):
        faces_of.append((side, squeeze_cells(lxh[side]), squeeze_cells(lc[side * (BX - 1), cells]),
                         squeeze_cells(wxf[side]), range(0, CY, 4)))
        faces_of.append((2 + side, pair_rows(lyh[side]), pair_rows(lys[side]), pair_rows(wyf[side]), range(0, BX, 2)))
        peers = [joined(lzh, half) for half in range(2)]
        faces_of.append((4 + side, face_blocks(peers, side, False), face_blocks(own_l, side, False),
                         face_blocks([fze[0], fze[1]], side, True), (0, 4)))

    for d, peer, own, weight, at_rows in faces_of:
        for n, r in enumerate(at_rows):
            at = slice(r, r + 1)
            place(n * CZ, peer[at], [(own[at], weight[at])])
        depth = len(at_rows) * CZ
        tile = lax.dot_general(xs[:, :depth], ys[:, :depth], NT, preferred_element_type=F32)
        mf[AGG * d : AGG * (d + 1)] = tile[:, :AGG] + tile[:, AGG:]
        for r in at_rows:
            diag_sums = gather_row(diag_sums, own[r : r + 1], weight[r : r + 1])

    coarse_scale = OMEGA_COARSE / aggregate_row(diag_sums)

    def store_tile(t, tile):
        high, low = split(tile * coarse_scale[0:1])
        mm[AGG * t : AGG * (t + 1), :AGG] = high.astype(BF16)
        mm[AGG * t : AGG * (t + 1), AGG:] = low.astype(BF16)

    for d in range(6):
        store_tile(d + 1, mf[AGG * d : AGG * (d + 1)])

    inner(1)

    def residual_step(turn, carry):
        for local in range(4):
            block = 4 * turn + local
            total = zero_plane
            for x in (2 * block, 2 * block + 1):
                total = total + dg[x] * (tp[x] - v[1, x + 1, cells])
            ew[0, block] = squeeze_cells(quad_sum(total * (1.0 / OMEGA_FINE)))
        return carry

    lax.fori_loop(0, BX // 4, residual_step, 0)
    sums = lax.fori_loop(0, BX, restrict_step, jnp.zeros((AGG, CZ), F32))

    finish("v", 1)
    halo_z = [fze[half] * joined(zh.at[1], half) for half in range(2)]
    inverse = 1.0 / OMEGA_FINE
    for block in range(BX):
        x = 2 * block
        low = sum(gy[0, n] * yh[1, 0, n] * dg[n, 0:8] for n in (x, x + 1))[0:1]
        high = sum(gy[1, n] * yh[1, 1, n] * dg[n, CY - 8 : CY] for n in (x, x + 1))[7:8]
        rows_y[0, block : block + 1] = inverse * (low + lane_roll(low, -1))
        rows_y[1, block : block + 1] = inverse * (high + lane_roll(high, -1))
    for side in range(2):
        plane = gx[side] * xh[1, side] * dg[side * (CX - 1)] * inverse
        values = (squeeze_cells(quad_sum(plane)), pair_rows(rows_y[side]), face_blocks(halo_z, side, True))
        for (d, peer, own, weight, at_rows), value in zip(faces_of[3 * side : 3 * side + 3], values):
            for r in at_rows:
                sums = gather_row(sums, own[r : r + 1], value[r : r + 1])
    first_correction = coarse_scale * aggregate_row(sums)

    def halves(values):
        high, low = split(values)
        return jnp.concatenate([high, low], axis=0).astype(BF16)

    def both(values):
        values = values[:, :AGG] + values[:, AGG:]
        return values[0:8] + values[8:16]

    def coarse_step(turn, correction, first=False):
        slot = turn % 2
        cs[slot] = correction
        start("c", slot)
        if first:
            lax.fori_loop(OWN_2, BX, own_step, 0)
            sum_own = acc[:, :AGG] + acc[:, AGG:]
            store_tile(0, sum_own + sum_own.T)
        image = jnp.dot(halves(correction), mm[0:AGG], preferred_element_type=F32)
        base = (1.0 - OMEGA_COARSE) * correction + first_correction
        base = base + both(image)
        finish("c", slot)
        beside = jnp.concatenate([ch[slot, d] for d in range(6)], axis=1)
        return base + both(jnp.dot(halves(beside), mm[AGG:], preferred_element_type=F32))

    correction = coarse_step(0, first_correction, True)
    for turn in range(1, KC - 1):
        correction = coarse_step(turn, correction)

    def lift_step(half, carry):
        packed = zero_tile
        for local in range(6):
            block = 6 * half + local
            index = lc[block, cells].astype(jnp.int32)
            lifted = jnp.concatenate(
                [jnp.take_along_axis(correction, index[8 * g : 8 * g + 8], axis=1, mode="promise_in_bounds")
                 for g in range(4)], axis=0)
            for n in range(2):
                x = 2 * block + n
                new = v[1, x + 1, cells] + lifted
                v[1, x + 1, cells] = new
                packed = pack_plane(packed, new, 2 * local + n)
        store_packed(zs.at[1], half, packed)
        return carry

    lax.fori_loop(0, 2, lift_step, 0)

    start("v", 1)
    for turn in range(POST):
        slot = 1 - turn % 2
        if turn:
            finish_send("v", 1 - slot)
        inner(slot)
        finish_recv("v", slot)
        if turn < POST - 1:
            outer_faces(slot, 1 - slot)
            start("v", 1 - slot, (4, 5))
            outer_edges(slot, 1 - slot)
            start("v", 1 - slot, (2, 3, 0, 1))
            outer_middle(1 - slot)
    finish_send("v", 0)
    for half in range(2):
        hz[half] = joined(zh.at[0], half)
    for x in range(CX):
        for g in range(4):
            out[x, 8 * g : 8 * g + 8] = finished(0, x, g)


def body(right_side, conductance, absorption, block_agg):
    field = (CX, CY, CZ)
    padded = (CX + 2, CY + 16, CZ)
    any_spec = pl.BlockSpec(memory_space=pl.ANY)

    def f32(*shape):
        return pltpu.VMEM(shape, F32)

    scratch = dict(
        bv=f32(*field), av=f32(*field), kp=f32(*padded), lv=pltpu.VMEM((BX, CY // 2, CZ // 2), jnp.int32),
        v=f32(2, *padded), gw=f32(6, *field), c0=f32(*field), dg=f32(*field), sc=f32(*field),
        fx=f32(CX + 1, CY, CZ), fy=f32(CX, CY + 8, CZ), fz=f32(2, *field),
        gz=f32(*field), gy=f32(2, CX, 8, CZ), gx=f32(2, CY, CZ),
        lc=f32(BX, CY + 16, CZ), el=f32(4, BX, CY, CZ), ew=f32(4, BX, CY, CZ),
        kxh=f32(2, CY, CZ), kyh=f32(2, CX, 8, CZ), kzs=f32(2, 2, 8, CZ), kzh=f32(2, 2, 8, CZ),
        lxh=f32(2, CY, CZ), lys=f32(2, 16, CZ), lyh=f32(2, 16, CZ), lzs=f32(2, 2, 8, CZ), lzh=f32(2, 2, 8, CZ),
        xh=f32(2, 2, CY, CZ), yh=f32(2, 2, CX, 8, CZ), zs=f32(2, 2, 2, 8, CZ), zh=f32(2, 2, 2, 8, CZ),
        fze=f32(2, 8, CZ), wyf=f32(2, 16, CZ), rows_y=f32(2, 16, CZ), zp=f32(2, 8, CZ), gzp=f32(2, 8, CZ), hz=f32(2, 8, CZ), tp=f32(*field),
        xs=pltpu.VMEM((AGG, 8 * CZ), BF16), ys=pltpu.VMEM((2 * AGG, 8 * CZ), BF16),
        acc=f32(AGG, 2 * AGG), mf=f32(6 * AGG, AGG), mm=pltpu.VMEM((7 * AGG, 2 * AGG), BF16),
        cs=f32(2, 8, CZ), ch=f32(2, 6, 8, CZ),
    )
    return pl.pallas_call(
        kernel,
        out_shape=pltpu.VMEM(field, F32),
        in_specs=[any_spec] * 4,
        out_specs=pl.BlockSpec(memory_space=pltpu.VMEM),
        scratch_shapes=list(scratch.values()) + [
            pltpu.SemaphoreType.DMA((4,)), pltpu.SemaphoreType.DMA((6, 6)), pltpu.SemaphoreType.DMA((6, 6)),
        ],
        compiler_params=pltpu.CompilerParams(collective_id=0, has_side_effects=True),
    )(right_side, conductance, absorption, block_agg)


def solution(mesh):
    spec = P("gx", "gy", "gz")
    return jax.shard_map(body, mesh=mesh, in_specs=(spec,) * 4, out_specs=spec, check_vma=False)
```

```python
import jax
import jax.numpy as jnp
from jax import lax
from jax.experimental import pallas as pl
from jax.experimental.pallas import tpu as pltpu
from jax.sharding import PartitionSpec as P

AGG = 128
POST = 4
KC = 8
OMEGA_FINE = 0.8
OMEGA_COARSE = 0.7
CX, CY, CZ = 24, 32, 128
BX = CX // 2
OWN_1, OWN_2 = 1, 5
TOP = 8
END = TOP + CY
AXES = ("gx", "gy", "gz")
F32 = jnp.float32
BF16 = jnp.bfloat16
NT = (((1,), (1,)), ((), ()))


def harmonic(one_side, other_side):
    summed = one_side + other_side
    return 2.0 * (one_side * other_side) / summed


def safe_harmonic(one_side, other_side):
    summed = one_side + other_side
    return 2.0 * (one_side * other_side) / jnp.where(summed > 0.0, summed, 1.0)


def lanes_of(shape):
    return lax.broadcasted_iota(jnp.int32, shape, 1)


def rows_of(shape):
    return lax.broadcasted_iota(jnp.int32, shape, 0)


def lane_roll(values, shift):
    return pltpu.roll(values, shift % CZ if isinstance(shift, int) else shift, 1)


def row_roll(values, shift):
    return pltpu.roll(values, shift % values.shape[0], 0)


def quad_sum(values):
    pair = values + row_roll(values, -1)
    return pair + lane_roll(pair, -1)


def squeeze_cells(values):
    even = (lanes_of(values.shape) & 1) == 0
    return jnp.where(even, values, lane_roll(row_roll(values, -2), 1))


def split(values):
    high = values.astype(BF16).astype(F32)
    return high, values - high


def spread_row(row):
    return jnp.broadcast_to(row, (16, CZ)).astype(BF16)


def kernel(
    b_hbm, k_hbm, a_hbm, l_hbm, out,
    bv, av, kp, lv, v, gw, c0, dg, sc, fx, fy, fz, gz, gy, gx, lc, el, ew,
    kxh, kyh, kzs, kzh, lxh, lys, lyh, lzs, lzh, xh, yh, zs, zh,
    fze, wyf, rows_y, zp, gzp, hz, tp, xs, ys, acc, mf, mm, cs, ch,
    local_sem, send_sem, recv_sem,
):
    pos = [lax.axis_index(a) for a in AXES]
    size = [lax.axis_size(a) for a in AXES]
    has = []
    dev = []
    for axis in range(3):
        has.append(pos[axis] > 0)
        dev.append({AXES[axis]: pos[axis] - 1})
        has.append(pos[axis] < size[axis] - 1)
        dev.append({AXES[axis]: pos[axis] + 1})
    cells = slice(TOP, END)

    def exchange_of(kind, slot):
        if kind == "k":
            src = [kp.at[1, cells], kp.at[CX, cells], kp.at[1 : CX + 1, TOP : TOP + 1],
                   kp.at[1 : CX + 1, END - 1 : END], kzs.at[0], kzs.at[1]]
            dst = [kxh.at[0], kxh.at[1], kyh.at[0, :, 0:1], kyh.at[1, :, 7:8], kzh.at[0], kzh.at[1]]
            sem = 0
        elif kind == "l":
            src = [lc.at[0, cells], lc.at[BX - 1, cells], lys.at[0], lys.at[1], lzs.at[0], lzs.at[1]]
            dst = [lxh.at[0], lxh.at[1], lyh.at[0], lyh.at[1], lzh.at[0], lzh.at[1]]
            sem = 1
        elif kind == "v":
            src = [v.at[slot, 1, cells], v.at[slot, CX, cells], v.at[slot, 1 : CX + 1, TOP : TOP + 1],
                   v.at[slot, 1 : CX + 1, END - 1 : END], zs.at[slot, 0], zs.at[slot, 1]]
            dst = [xh.at[slot, 0], xh.at[slot, 1], yh.at[slot, 0, :, 0:1], yh.at[slot, 1, :, 7:8],
                   zh.at[slot, 0], zh.at[slot, 1]]
            sem = 2 + slot
        else:
            src = [cs.at[slot, 0:1]] * 6
            dst = [ch.at[slot, d, 0:1] for d in range(6)]
            sem = 4 + slot
        return src, dst, sem

    def copy_to(kind, slot, d):
        src, dst, sem = exchange_of(kind, slot)
        return pltpu.make_async_remote_copy(
            src[d], dst[d ^ 1], send_sem.at[sem, d], recv_sem.at[sem, d ^ 1],
            device_id=dev[d], device_id_type=pl.DeviceIdType.MESH)

    def copy_from(kind, slot, d):
        src, dst, sem = exchange_of(kind, slot)
        return pltpu.make_async_remote_copy(
            src[d], dst[d], send_sem.at[sem, d], recv_sem.at[sem, d],
            device_id=dev[d], device_id_type=pl.DeviceIdType.MESH)

    def start(kind, slot=0, sides=(4, 5, 2, 3, 0, 1)):
        for d in sides:
            @pl.when(has[d])
            def _():
                copy_to(kind, slot, d).start()

    def finish_send(kind, slot=0):
        for d in range(6):
            @pl.when(has[d])
            def _():
                copy_to(kind, slot, d).wait_send()

    def finish_recv(kind, slot=0):
        for d in range(6):
            @pl.when(has[d])
            def _():
                copy_from(kind, slot, d).wait_recv()

    def finish(kind, slot=0):
        finish_send(kind, slot)
        finish_recv(kind, slot)

    load_k = pltpu.make_async_copy(k_hbm, kp.at[1 : CX + 1, cells], local_sem.at[0])
    load_l = pltpu.make_async_copy(l_hbm, lv, local_sem.at[1])
    load_a = pltpu.make_async_copy(a_hbm, av, local_sem.at[2])
    load_b = pltpu.make_async_copy(b_hbm, bv, local_sem.at[3])
    load_k.start()
    load_l.start()
    load_a.start()
    load_b.start()

    zero_plane = jnp.zeros((CY, CZ), F32)
    zero_tile = jnp.zeros((8, CZ), F32)
    for side in range(2):
        kxh[side] = zero_plane
        lxh[side] = zero_plane
        lyh[side] = jnp.zeros((16, CZ), F32)
        for half in range(2):
            kzh[side, half] = zero_tile
            lzh[side, half] = zero_tile
        for x in range(CX):
            kyh[side, x] = zero_tile

    barrier = pltpu.get_barrier_semaphore()
    count = jnp.int32(0)
    for d in range(6):
        @pl.when(has[d])
        def _():
            pl.semaphore_signal(barrier, inc=1, device_id=dev[d], device_id_type=pl.DeviceIdType.MESH)
        count = count + has[d].astype(jnp.int32)

    for slot in range(2):
        for d in range(6):
            ch[slot, d] = zero_tile
        for side in range(2):
            xh[slot, side] = zero_plane
            for half in range(2):
                zh[slot, side, half] = zero_tile
            for x in range(CX):
                yh[slot, side, x] = zero_tile
        for edge in (0, CX + 1):
            v[slot, edge, cells] = zero_plane
        for x in range(CX):
            v[slot, x + 1, TOP - 8 : TOP] = zero_tile
            v[slot, x + 1, END : END + 8] = zero_tile
    for edge in (0, CX + 1):
        kp[edge, cells] = zero_plane
    for x in range(CX):
        kp[x + 1, TOP - 8 : TOP] = zero_tile
        kp[x + 1, END : END + 8] = zero_tile
        fy[x, CY : CY + 8] = zero_tile
    fx[0] = zero_plane
    for side in range(2):
        lys[side] = jnp.zeros((16, CZ), F32)
        wyf[side] = jnp.zeros((16, CZ), F32)
        rows_y[side] = jnp.zeros((16, CZ), F32)

    lane_8 = lanes_of((8, CZ))
    rim = (lane_8 == 0) | (lane_8 == CZ - 1)
    odd = (lane_8 & 1) == 1

    def pack_plane(packed, plane, x):
        for g in range(4):
            piece = jnp.where(rim, plane[8 * g : 8 * g + 8], 0.0)
            packed = packed + lane_roll(piece, 2 * (4 * x + g))
        return packed

    def store_packed(ref, half, packed):
        ref[0, half] = lane_roll(packed, -1)
        ref[1, half] = lane_roll(packed, 1)

    def joined(ref, half):
        return jnp.where(odd, ref[1, half], ref[0, half])

    def unpack_plane(packed, x):
        return [lane_roll(packed, -2 * (4 * x + g)) for g in range(4)]

    load_k.wait()
    own_k = []
    for half in range(2):
        packed = zero_tile
        for x in range(12):
            packed = pack_plane(packed, kp[12 * half + x + 1, cells], x)
        store_packed(kzs, half, packed)
        own_k.append(packed)
    pl.semaphore_wait(barrier, count)
    start("k")

    load_l.wait()
    labels = lv[...].reshape(BX * 16, 64).astype(F32).astype(BF16)
    widen = jnp.where(lanes_of((64, CZ)) // 2 == rows_of((64, CZ)), 1.0, 0.0).astype(BF16)
    wide = jnp.dot(labels, widen, preferred_element_type=F32).astype(BF16)
    tall_shape = (BX * CY, BX * 16)
    heighten = jnp.where(rows_of(tall_shape) // 2 == lanes_of(tall_shape), 1.0, 0.0).astype(BF16)
    tall = jnp.dot(heighten, wide, preferred_element_type=F32)
    for x in range(BX):
        lc[x, cells] = tall[x * CY : (x + 1) * CY]
        lc[x, END : END + 8] = zero_tile
        lys[0, x : x + 1] = tall[x * CY : x * CY + 1]
        lys[1, x : x + 1] = tall[x * CY + CY - 1 : x * CY + CY]
    own_l = []
    for half in range(2):
        packed = zero_tile
        for x in range(6):
            plane = lc[6 * half + x, cells]
            packed = pack_plane(packed, plane, 2 * x)
            packed = pack_plane(packed, plane, 2 * x + 1)
        store_packed(lzs, half, packed)
        own_l.append(packed)
    start("l")

    lane = lanes_of((CY, CZ))
    row = rows_of((CY, CZ))
    load_a.wait()

    def faces(x, fx_low):
        centre = kp[x + 1, cells]
        fx_high = harmonic(centre, kp[x + 2, cells])
        fy_low = harmonic(kp[x + 1, TOP - 1 : END - 1], centre)
        fy[x, 0:CY] = fy_low
        fz_low = jnp.where(lane == 0, 0.0, harmonic(lane_roll(centre, 1), centre))
        fz_high = lane_roll(fz_low, -1)
        fy_high = fy[x, 1 : CY + 1]
        fx[x + 1] = fx_high
        fz[0, x] = fz_low
        fz[1, x] = fz_high
        dg[x] = av[x] + fx_low + fx_high + fy_low + fy_high + fz_low + fz_high
        return fx_high, fy_high, fz_high

    def block_step(block, carry):
        fx_low, cut_below = carry
        x = 2 * block
        fx_mid, fy_high_0, fz_high_0 = faces(x, fx_low)
        fx_high, fy_high_1, fz_high_1 = faces(x + 1, fx_mid)
        wx = quad_sum(fx_high)
        wy = fy_high_0 + fy_high_1
        wy = row_roll(wy + lane_roll(wy, -1), -1)
        wz = fz_high_0 + fz_high_1
        wz = lane_roll(wz + row_roll(wz, -1), -1)
        wa = quad_sum(av[x] + av[x + 1])
        own = lc[block, cells]
        lx = lc[min(block + 1, BX - 1), cells]
        ly = lc[block, TOP + 2 : END + 2]
        lz = lane_roll(own, -2)
        lx = jnp.where(lx == own, -1.0, lx)
        ly = jnp.where((ly == own) | (row >= CY - 2), -1.0, ly)
        lz = jnp.where((lz == own) | (lane >= CZ - 2), -1.0, lz)
        cut_x = jnp.where(lx < 0.0, 0.0, wx)
        cut_y = jnp.where(ly < 0.0, 0.0, wy)
        cut_z = jnp.where(lz < 0.0, 0.0, wz)
        leaving = wa + cut_below + cut_x + cut_y + row_roll(cut_y, 2) + cut_z + lane_roll(cut_z, 2)
        ew[0, block] = squeeze_cells(leaving)
        same = ly == lx
        wx = wx + jnp.where(same, wy, 0.0)
        ly = jnp.where(same, -1.0, ly)
        same = lz == lx
        wx = wx + jnp.where(same, wz, 0.0)
        lz = jnp.where(same, -1.0, lz)
        same = lz == ly
        wy = wy + jnp.where(same, wz, 0.0)
        lz = jnp.where(same, -1.0, lz)
        for n, field in enumerate((own, lx, ly, lz)):
            el[n, block] = squeeze_cells(field)
        for n, field in enumerate((wx, wy, wz)):
            ew[n + 1, block] = squeeze_cells(field)
        return fx_high, cut_x

    below = (zero_plane, zero_plane)
    for block in range(BX):
        below = block_step(block, below)

    number = rows_of((16, CZ)).astype(F32)
    numbers = [(number + 16.0 * q).astype(BF16) for q in range(8)]
    one = jnp.ones((16, CZ), BF16)
    zero = jnp.zeros((16, CZ), BF16)

    def place(at, lhs_label, pairs):
        lhs_label = spread_row(lhs_label)
        spread = []
        for label, weight in pairs:
            high, low = split(weight)
            spread.append((spread_row(label), spread_row(high), spread_row(low)))
        for q in range(8):
            xs[16 * q : 16 * q + 16, at : at + CZ] = jnp.where(lhs_label == numbers[q], one, zero)
            y_high = zero
            y_low = zero
            for label, high, low in spread:
                hit = label == numbers[q]
                y_high = jnp.where(hit, high, y_high)
                y_low = jnp.where(hit, low, y_low)
            ys[16 * q : 16 * q + 16, at : at + CZ] = y_high
            ys[AGG + 16 * q : AGG + 16 * q + 16, at : at + CZ] = y_low

    acc[...] = jnp.zeros((AGG, 2 * AGG), F32)

    def own_step(block, carry):
        for m in range(8):
            at = slice(4 * m, 4 * m + 1)
            pairs = [(el[n, block, at], ew[n, block, at]) for n in range(1, 4)]
            place(m * CZ, el[0, block, at], pairs)
        acc[...] += lax.dot_general(xs[...], ys[...], NT, preferred_element_type=F32)
        return carry

    lax.fori_loop(0, OWN_1, own_step, 0)
    load_b.wait()
    own_d = []
    own_b = []
    for half in range(2):
        packed_d = zero_tile
        packed_b = zero_tile
        for local in range(12):
            packed_d = pack_plane(packed_d, dg[12 * half + local], local)
            packed_b = pack_plane(packed_b, bv[12 * half + local], local)
        own_d.append(packed_d)
        own_b.append(packed_b)
    finish("k")

    gx[0] = harmonic(kp[1, cells], kxh[0])
    gx[1] = harmonic(kp[CX, cells], kxh[1])
    for half in range(2):
        face_z = safe_harmonic(own_k[half], joined(kzh, half))
        fze[half] = face_z
        diag = own_d[half] + face_z
        for local in range(12):
            x = 12 * half + local
            low = harmonic(kp[x + 1, TOP : TOP + 8], kyh[0, x])
            high = harmonic(kp[x + 1, END - 8 : END], kyh[1, x])
            gy[0, x] = low
            gy[1, x] = high
            diag = diag + lane_roll(jnp.where(rim, low, 0.0), 8 * local)
            diag = diag + lane_roll(jnp.where(rim, high, 0.0), 8 * local + 6)
        diag = pack_plane(diag, gx[half], 11 * half)
        first = OMEGA_FINE * own_b[half] / jnp.where(diag > 0.0, diag, 1.0)
        store_packed(zs.at[0], half, first)
    start("v", 0, (4, 5))

    def first_part(x, g):
        at = slice(8 * g, 8 * g + 8)
        wall = jnp.where(rim, lane_roll(fze[x // 12], -2 * (4 * (x % 12) + g)), 0.0)
        gz[x, at] = wall
        diag = dg[x, at] + wall
        if g == 0:
            diag = diag + gy[0, x]
        if g == 3:
            diag = diag + gy[1, x]
        if x == 0:
            diag = diag + gx[0, at]
        if x == CX - 1:
            diag = diag + gx[1, at]
        scale = OMEGA_FINE / diag
        first = scale * bv[x, at]
        dg[x, at] = diag
        sc[x, at] = scale
        c0[x, at] = first
        v[0, x + 1, TOP + 8 * g : TOP + 8 * g + 8] = first

    for x in range(CX):
        for g in (range(4) if x in (0, CX - 1) else (0, 3)):
            first_part(x, g)
    start("v", 0, (2, 3, 0, 1))
    for x in range(1, CX - 1):
        for g in (1, 2):
            first_part(x, g)

    def face_rows(block, carry):
        x = 2 * block
        low = (gy[0, x] + gy[0, x + 1])[0:1]
        high = (gy[1, x] + gy[1, x + 1])[7:8]
        wyf[0, pl.ds(block, 1)] = low + lane_roll(low, -1)
        wyf[1, pl.ds(block, 1)] = high + lane_roll(high, -1)
        return carry

    lax.fori_loop(0, BX, face_rows, 0, unroll=True)
    wxf = [quad_sum(gx[side]) for side in range(2)]

    def scale_step(turn, carry):
        for local in range(4):
            x = 4 * turn + local
            scale = sc[x]
            gw[0, x] = scale * fx[x]
            gw[1, x] = scale * fx[x + 1]
            gw[2, x] = scale * fy[x, 0:CY]
            gw[3, x] = scale * fy[x, 1 : CY + 1]
            gw[4, x] = scale * fz[0, x]
            gw[5, x] = scale * fz[1, x]
            gz[x] = scale * gz[x]
            gy[0, x] = scale[0:8] * gy[0, x]
            gy[1, x] = scale[CY - 8 :] * gy[1, x]
        return carry

    lax.fori_loop(0, CX // 4, scale_step, 0)
    gx[0] = sc[0] * gx[0]
    gx[1] = sc[CX - 1] * gx[1]

    def pack_scale(half, carry):
        packed = zero_tile
        for local in range(12):
            packed = pack_plane(packed, gz[12 * half + local], local)
        gzp[half] = packed
        return carry

    lax.fori_loop(0, 2, pack_scale, 0)

    def inner(slot):
        def step(half, carry):
            packed = zero_tile
            for local in range(12):
                x = 12 * half + local
                centre = v[slot, x + 1, cells]
                total = c0[x] + (1.0 - OMEGA_FINE) * centre
                total = total + gw[0, x] * v[slot, x, cells] + gw[1, x] * v[slot, x + 2, cells]
                total = total + gw[2, x] * v[slot, x + 1, TOP - 1 : END - 1]
                total = total + gw[3, x] * v[slot, x + 1, TOP + 1 : END + 1]
                total = total + gw[4, x] * lane_roll(centre, 1) + gw[5, x] * lane_roll(centre, -1)
                tp[x] = total
                packed = pack_plane(packed, total, local)
            zp[half] = packed
            return carry

        lax.fori_loop(0, 2, step, 0)

    def outer_faces(slot, other):
        for half in range(2):
            halo_z = joined(zh.at[slot], half)
            hz[half] = halo_z
            packed = zp[half] + gzp[half] * halo_z
            for local in range(12):
                x = 12 * half + local
                low = jnp.where(rim, gy[0, x] * yh[slot, 0, x], 0.0)
                high = jnp.where(rim, gy[1, x] * yh[slot, 1, x], 0.0)
                packed = packed + lane_roll(low, 8 * local) + lane_roll(high, 8 * local + 6)
            if half == 0:
                packed = pack_plane(packed, gx[0] * xh[slot, 0], 0)
            else:
                packed = pack_plane(packed, gx[1] * xh[slot, 1], 11)
            store_packed(zs.at[other], half, packed)

    def finished(slot, x, g):
        at = slice(8 * g, 8 * g + 8)
        wall = lane_roll(hz[x // 12], -2 * (4 * (x % 12) + g))
        new = tp[x, at] + gz[x, at] * wall
        if g == 0:
            new = new + gy[0, x] * yh[slot, 0, x]
        if g == 3:
            new = new + gy[1, x] * yh[slot, 1, x]
        if x == 0:
            new = new + gx[0, at] * xh[slot, 0, at]
        if x == CX - 1:
            new = new + gx[1, at] * xh[slot, 1, at]
        return new

    def outer_edges(slot, other):
        for x in range(CX):
            for g in (range(4) if x in (0, CX - 1) else (0, 3)):
                v[other, x + 1, TOP + 8 * g : TOP + 8 * g + 8] = finished(slot, x, g)

    def outer_middle(other):
        for x in range(1, CX - 1):
            for g in (1, 2):
                v[other, x + 1, TOP + 8 * g : TOP + 8 * g + 8] = finished(None, x, g)

    wanted = rows_of((AGG, CZ)).astype(F32)

    def gather_row(sums, label, value):
        label = jnp.broadcast_to(label, (AGG, CZ))
        return sums + jnp.where(label == wanted, jnp.broadcast_to(value, (AGG, CZ)), 0.0)

    def restrict_step(block, sums):
        for m in range(8):
            at = slice(4 * m, 4 * m + 1)
            sums = gather_row(sums, el[0, block, at], ew[0, block, at])
        return sums

    def aggregate_row(sums):
        high, low = split(sums)
        ones = jnp.ones((16, CZ), BF16)
        out = lax.dot_general(ones, high.astype(BF16), NT, preferred_element_type=F32)
        return (out + lax.dot_general(ones, low.astype(BF16), NT, preferred_element_type=F32))[0:8]

    inner(0)
    diag_sums = lax.fori_loop(0, BX, restrict_step, jnp.zeros((AGG, CZ), F32))
    lax.fori_loop(OWN_1, OWN_2, own_step, 0)

    finish("v", 0)
    outer_faces(0, 1)
    start("v", 1, (4, 5))
    outer_edges(0, 1)
    start("v", 1, (2, 3, 0, 1))
    outer_middle(1)

    finish("l")

    def pair_rows(values):
        return jnp.where((lanes_of(values.shape) & 1) == 0, values, lane_roll(row_roll(values, -1), 1))

    def face_blocks(halves, side, summed):
        out = []
        for values in halves:
            if side:
                values = lane_roll(values, 1)
            if summed:
                values = values + lane_roll(values, -8)
                values = values + row_roll(values, -1)
            out.append(jnp.where((lane_8 & 8) == 0, values, lane_roll(row_roll(values, -2), 8)))
        out = jnp.where(odd, lane_roll(out[1], 1), out[0])
        return jnp.where(lane_8 < 96, out, 0.0) if summed else out

    faces_of = []
    for side in range(2):
        faces_of.append((side, squeeze_cells(lxh[side]), squeeze_cells(lc[side * (BX - 1), cells]),
                         squeeze_cells(wxf[side]), range(0, CY, 4)))
        faces_of.append((2 + side, pair_rows(lyh[side]), pair_rows(lys[side]), pair_rows(wyf[side]), range(0, BX, 2)))
        peers = [joined(lzh, half) for half in range(2)]
        faces_of.append((4 + side, face_blocks(peers, side, False), face_blocks(own_l, side, False),
                         face_blocks([fze[0], fze[1]], side, True), (0, 4)))

    for d, peer, own, weight, at_rows in faces_of:
        for n, r in enumerate(at_rows):
            at = slice(r, r + 1)
            place(n * CZ, peer[at], [(own[at], weight[at])])
        depth = len(at_rows) * CZ
        tile = lax.dot_general(xs[:, :depth], ys[:, :depth], NT, preferred_element_type=F32)
        mf[AGG * d : AGG * (d + 1)] = tile[:, :AGG] + tile[:, AGG:]
        for r in at_rows:
            diag_sums = gather_row(diag_sums, own[r : r + 1], weight[r : r + 1])

    coarse_scale = OMEGA_COARSE / aggregate_row(diag_sums)

    def store_tile(t, tile):
        high, low = split(tile * coarse_scale[0:1])
        mm[AGG * t : AGG * (t + 1), :AGG] = high.astype(BF16)
        mm[AGG * t : AGG * (t + 1), AGG:] = low.astype(BF16)

    for d in range(6):
        store_tile(d + 1, mf[AGG * d : AGG * (d + 1)])

    inner(1)

    def residual_step(turn, carry):
        for local in range(4):
            block = 4 * turn + local
            total = zero_plane
            for x in (2 * block, 2 * block + 1):
                total = total + dg[x] * (tp[x] - v[1, x + 1, cells])
            ew[0, block] = squeeze_cells(quad_sum(total * (1.0 / OMEGA_FINE)))
        return carry

    lax.fori_loop(0, BX // 4, residual_step, 0)
    sums = lax.fori_loop(0, BX, restrict_step, jnp.zeros((AGG, CZ), F32))

    finish("v", 1)
    halo_z = [fze[half] * joined(zh.at[1], half) for half in range(2)]
    inverse = 1.0 / OMEGA_FINE
    for block in range(BX):
        x = 2 * block
        low = sum(gy[0, n] * yh[1, 0, n] * dg[n, 0:8] for n in (x, x + 1))[0:1]
        high = sum(gy[1, n] * yh[1, 1, n] * dg[n, CY - 8 : CY] for n in (x, x + 1))[7:8]
        rows_y[0, block : block + 1] = inverse * (low + lane_roll(low, -1))
        rows_y[1, block : block + 1] = inverse * (high + lane_roll(high, -1))
    for side in range(2):
        plane = gx[side] * xh[1, side] * dg[side * (CX - 1)] * inverse
        values = (squeeze_cells(quad_sum(plane)), pair_rows(rows_y[side]), face_blocks(halo_z, side, True))
        for (d, peer, own, weight, at_rows), value in zip(faces_of[3 * side : 3 * side + 3], values):
            for r in at_rows:
                sums = gather_row(sums, own[r : r + 1], value[r : r + 1])
    first_correction = coarse_scale * aggregate_row(sums)

    def halves(values):
        high, low = split(values)
        return jnp.concatenate([high, low], axis=0).astype(BF16)

    def both(values):
        values = values[:, :AGG] + values[:, AGG:]
        return values[0:8] + values[8:16]

    def coarse_step(turn, correction, first=False):
        slot = turn % 2
        cs[slot] = correction
        start("c", slot)
        if first:
            lax.fori_loop(OWN_2, BX, own_step, 0)
            sum_own = acc[:, :AGG] + acc[:, AGG:]
            store_tile(0, sum_own + sum_own.T)
        image = jnp.dot(halves(correction), mm[0:AGG], preferred_element_type=F32)
        base = (1.0 - OMEGA_COARSE) * correction + first_correction
        base = base + both(image)
        finish("c", slot)
        beside = jnp.concatenate([jnp.broadcast_to(ch[slot, d, 0:1], (8, CZ)) for d in range(6)], axis=1)
        return base + both(jnp.dot(halves(beside), mm[AGG:], preferred_element_type=F32))

    correction = coarse_step(0, first_correction, True)
    for turn in range(1, KC - 1):
        correction = coarse_step(turn, correction)

    def lift_step(half, carry):
        packed = zero_tile
        for local in range(6):
            block = 6 * half + local
            index = lc[block, cells].astype(jnp.int32)
            lifted = jnp.concatenate(
                [jnp.take_along_axis(correction, index[8 * g : 8 * g + 8], axis=1, mode="promise_in_bounds")
                 for g in range(4)], axis=0)
            for n in range(2):
                x = 2 * block + n
                new = v[1, x + 1, cells] + lifted
                v[1, x + 1, cells] = new
                packed = pack_plane(packed, new, 2 * local + n)
        store_packed(zs.at[1], half, packed)
        return carry

    lax.fori_loop(0, 2, lift_step, 0)

    start("v", 1)
    for turn in range(POST):
        slot = 1 - turn % 2
        if turn:
            finish_send("v", 1 - slot)
        inner(slot)
        finish_recv("v", slot)
        if turn < POST - 1:
            outer_faces(slot, 1 - slot)
            start("v", 1 - slot, (4, 5))
            outer_edges(slot, 1 - slot)
            start("v", 1 - slot, (2, 3, 0, 1))
            outer_middle(1 - slot)
    finish_send("v", 0)
    for half in range(2):
        hz[half] = joined(zh.at[0], half)
    for x in range(CX):
        for g in range(4):
            out[x, 8 * g : 8 * g + 8] = finished(0, x, g)


def body(right_side, conductance, absorption, block_agg):
    field = (CX, CY, CZ)
    padded = (CX + 2, CY + 16, CZ)
    any_spec = pl.BlockSpec(memory_space=pl.ANY)

    def f32(*shape):
        return pltpu.VMEM(shape, F32)

    scratch = dict(
        bv=f32(*field), av=f32(*field), kp=f32(*padded), lv=pltpu.VMEM((BX, CY // 2, CZ // 2), jnp.int32),
        v=f32(2, *padded), gw=f32(6, *field), c0=f32(*field), dg=f32(*field), sc=f32(*field),
        fx=f32(CX + 1, CY, CZ), fy=f32(CX, CY + 8, CZ), fz=f32(2, *field),
        gz=f32(*field), gy=f32(2, CX, 8, CZ), gx=f32(2, CY, CZ),
        lc=f32(BX, CY + 16, CZ), el=f32(4, BX, CY, CZ), ew=f32(4, BX, CY, CZ),
        kxh=f32(2, CY, CZ), kyh=f32(2, CX, 8, CZ), kzs=f32(2, 2, 8, CZ), kzh=f32(2, 2, 8, CZ),
        lxh=f32(2, CY, CZ), lys=f32(2, 16, CZ), lyh=f32(2, 16, CZ), lzs=f32(2, 2, 8, CZ), lzh=f32(2, 2, 8, CZ),
        xh=f32(2, 2, CY, CZ), yh=f32(2, 2, CX, 8, CZ), zs=f32(2, 2, 2, 8, CZ), zh=f32(2, 2, 2, 8, CZ),
        fze=f32(2, 8, CZ), wyf=f32(2, 16, CZ), rows_y=f32(2, 16, CZ), zp=f32(2, 8, CZ), gzp=f32(2, 8, CZ), hz=f32(2, 8, CZ), tp=f32(*field),
        xs=pltpu.VMEM((AGG, 8 * CZ), BF16), ys=pltpu.VMEM((2 * AGG, 8 * CZ), BF16),
        acc=f32(AGG, 2 * AGG), mf=f32(6 * AGG, AGG), mm=pltpu.VMEM((7 * AGG, 2 * AGG), BF16),
        cs=f32(2, 8, CZ), ch=f32(2, 6, 8, CZ),
    )
    return pl.pallas_call(
        kernel,
        out_shape=pltpu.VMEM(field, F32),
        in_specs=[any_spec] * 4,
        out_specs=pl.BlockSpec(memory_space=pltpu.VMEM),
        scratch_shapes=list(scratch.values()) + [
            pltpu.SemaphoreType.DMA((4,)), pltpu.SemaphoreType.DMA((6, 6)), pltpu.SemaphoreType.DMA((6, 6)),
        ],
        compiler_params=pltpu.CompilerParams(collective_id=0, has_side_effects=True),
    )(right_side, conductance, absorption, block_agg)


def solution(mesh):
    spec = P("gx", "gy", "gz")
    return jax.shard_map(body, mesh=mesh, in_specs=(spec,) * 4, out_specs=spec, check_vma=False)
```

```python
import jax
import jax.numpy as jnp
from jax import lax
from jax.experimental import pallas as pl
from jax.experimental.pallas import tpu as pltpu
from jax.sharding import PartitionSpec as P

AGG = 128
POST = 4
KC = 8
OMEGA_FINE = 0.8
OMEGA_COARSE = 0.7
CX, CY, CZ = 24, 32, 128
BX = CX // 2
OWN_1, OWN_2 = 1, 5
TOP = 8
END = TOP + CY
AXES = ("gx", "gy", "gz")
F32 = jnp.float32
BF16 = jnp.bfloat16
NT = (((1,), (1,)), ((), ()))


def harmonic(one_side, other_side):
    summed = one_side + other_side
    return 2.0 * (one_side * other_side) / summed


def safe_harmonic(one_side, other_side):
    summed = one_side + other_side
    return 2.0 * (one_side * other_side) / jnp.where(summed > 0.0, summed, 1.0)


def lanes_of(shape):
    return lax.broadcasted_iota(jnp.int32, shape, 1)


def rows_of(shape):
    return lax.broadcasted_iota(jnp.int32, shape, 0)


def lane_roll(values, shift):
    return pltpu.roll(values, shift % CZ if isinstance(shift, int) else shift, 1)


def row_roll(values, shift):
    return pltpu.roll(values, shift % values.shape[0], 0)


def quad_sum(values):
    pair = values + row_roll(values, -1)
    return pair + lane_roll(pair, -1)


def squeeze_cells(values):
    even = (lanes_of(values.shape) & 1) == 0
    return jnp.where(even, values, lane_roll(row_roll(values, -2), 1))


def split(values):
    high = values.astype(BF16).astype(F32)
    return high, values - high


def spread_row(row):
    return jnp.broadcast_to(row, (16, CZ)).astype(BF16)


def kernel(
    b_hbm, k_hbm, a_hbm, l_hbm, out,
    bv, av, kp, lv, v, gw, c0, dg, sc, fx, fy, fz, gz, gy, gx, lc, el, ew,
    kxh, kyh, kzs, kzh, lxh, lys, lyh, lzs, lzh, xh, yh, zs, zh,
    fze, wyf, rows_y, zp, gzp, hz, tp, xs, ys, acc, mf, mm, cs, ch,
    local_sem, send_sem, recv_sem,
):
    pos = [lax.axis_index(a) for a in AXES]
    size = [lax.axis_size(a) for a in AXES]
    has = []
    dev = []
    for axis in range(3):
        has.append(pos[axis] > 0)
        dev.append({AXES[axis]: pos[axis] - 1})
        has.append(pos[axis] < size[axis] - 1)
        dev.append({AXES[axis]: pos[axis] + 1})
    cells = slice(TOP, END)

    def exchange_of(kind, slot):
        if kind == "k":
            src = [kp.at[1, cells], kp.at[CX, cells], kp.at[1 : CX + 1, TOP : TOP + 1],
                   kp.at[1 : CX + 1, END - 1 : END], kzs.at[0], kzs.at[1]]
            dst = [kxh.at[0], kxh.at[1], kyh.at[0, :, 0:1], kyh.at[1, :, 7:8], kzh.at[0], kzh.at[1]]
            sem = 0
        elif kind == "l":
            src = [lc.at[0, cells], lc.at[BX - 1, cells], lys.at[0], lys.at[1], lzs.at[0], lzs.at[1]]
            dst = [lxh.at[0], lxh.at[1], lyh.at[0], lyh.at[1], lzh.at[0], lzh.at[1]]
            sem = 1
        elif kind == "v":
            src = [v.at[slot, 1, cells], v.at[slot, CX, cells], v.at[slot, 1 : CX + 1, TOP : TOP + 1],
                   v.at[slot, 1 : CX + 1, END - 1 : END], zs.at[slot, 0], zs.at[slot, 1]]
            dst = [xh.at[slot, 0], xh.at[slot, 1], yh.at[slot, 0, :, 0:1], yh.at[slot, 1, :, 7:8],
                   zh.at[slot, 0], zh.at[slot, 1]]
            sem = 2 + slot
        else:
            src = [cs.at[slot, 0:1]] * 6
            dst = [ch.at[slot, d, 0:1] for d in range(6)]
            sem = 4 + slot
        return src, dst, sem

    def copy_to(kind, slot, d):
        src, dst, sem = exchange_of(kind, slot)
        return pltpu.make_async_remote_copy(
            src[d], dst[d ^ 1], send_sem.at[sem, d], recv_sem.at[sem, d ^ 1],
            device_id=dev[d], device_id_type=pl.DeviceIdType.MESH)

    def copy_from(kind, slot, d):
        src, dst, sem = exchange_of(kind, slot)
        return pltpu.make_async_remote_copy(
            src[d], dst[d], send_sem.at[sem, d], recv_sem.at[sem, d],
            device_id=dev[d], device_id_type=pl.DeviceIdType.MESH)

    def start(kind, slot=0, sides=(4, 5, 2, 3, 0, 1)):
        for d in sides:
            @pl.when(has[d])
            def _():
                copy_to(kind, slot, d).start()

    def finish_send(kind, slot=0):
        for d in range(6):
            @pl.when(has[d])
            def _():
                copy_to(kind, slot, d).wait_send()

    def finish_recv(kind, slot=0):
        for d in range(6):
            @pl.when(has[d])
            def _():
                copy_from(kind, slot, d).wait_recv()

    def finish(kind, slot=0):
        finish_send(kind, slot)
        finish_recv(kind, slot)

    load_k = pltpu.make_async_copy(k_hbm, kp.at[1 : CX + 1, cells], local_sem.at[0])
    load_l = pltpu.make_async_copy(l_hbm, lv, local_sem.at[1])
    load_a = pltpu.make_async_copy(a_hbm, av, local_sem.at[2])
    load_b = pltpu.make_async_copy(b_hbm, bv, local_sem.at[3])
    load_k.start()
    load_l.start()
    load_a.start()
    load_b.start()

    zero_plane = jnp.zeros((CY, CZ), F32)
    zero_tile = jnp.zeros((8, CZ), F32)
    for side in range(2):
        kxh[side] = zero_plane
        lxh[side] = zero_plane
        lyh[side] = jnp.zeros((16, CZ), F32)
        for half in range(2):
            kzh[side, half] = zero_tile
            lzh[side, half] = zero_tile
        for x in range(CX):
            kyh[side, x] = zero_tile

    barrier = pltpu.get_barrier_semaphore()
    count = jnp.int32(0)
    for d in range(6):
        @pl.when(has[d])
        def _():
            pl.semaphore_signal(barrier, inc=1, device_id=dev[d], device_id_type=pl.DeviceIdType.MESH)
        count = count + has[d].astype(jnp.int32)

    for slot in range(2):
        for d in range(6):
            ch[slot, d] = zero_tile
        for side in range(2):
            xh[slot, side] = zero_plane
            for half in range(2):
                zh[slot, side, half] = zero_tile
            for x in range(CX):
                yh[slot, side, x] = zero_tile
        for edge in (0, CX + 1):
            v[slot, edge, cells] = zero_plane
        for x in range(CX):
            v[slot, x + 1, TOP - 8 : TOP] = zero_tile
            v[slot, x + 1, END : END + 8] = zero_tile
    for edge in (0, CX + 1):
        kp[edge, cells] = zero_plane
    for x in range(CX):
        kp[x + 1, TOP - 8 : TOP] = zero_tile
        kp[x + 1, END : END + 8] = zero_tile
        fy[x, CY : CY + 8] = zero_tile
    fx[0] = zero_plane
    for side in range(2):
        lys[side] = jnp.zeros((16, CZ), F32)
        wyf[side] = jnp.zeros((16, CZ), F32)
        rows_y[side] = jnp.zeros((16, CZ), F32)

    lane_8 = lanes_of((8, CZ))
    rim = (lane_8 == 0) | (lane_8 == CZ - 1)
    odd = (lane_8 & 1) == 1

    def pack_plane(packed, plane, x):
        for g in range(4):
            piece = jnp.where(rim, plane[8 * g : 8 * g + 8], 0.0)
            packed = packed + lane_roll(piece, 2 * (4 * x + g))
        return packed

    def store_packed(ref, half, packed):
        ref[0, half] = lane_roll(packed, -1)
        ref[1, half] = lane_roll(packed, 1)

    def joined(ref, half):
        return jnp.where(odd, ref[1, half], ref[0, half])

    def unpack_plane(packed, x):
        return [lane_roll(packed, -2 * (4 * x + g)) for g in range(4)]

    load_k.wait()
    own_k = []
    for half in range(2):
        packed = zero_tile
        for x in range(12):
            packed = pack_plane(packed, kp[12 * half + x + 1, cells], x)
        store_packed(kzs, half, packed)
        own_k.append(packed)
    pl.semaphore_wait(barrier, count)
    start("k")

    load_l.wait()
    labels = lv[...].reshape(BX * 16, 64).astype(F32).astype(BF16)
    widen = jnp.where(lanes_of((64, CZ)) // 2 == rows_of((64, CZ)), 1.0, 0.0).astype(BF16)
    wide = jnp.dot(labels, widen, preferred_element_type=F32).astype(BF16)
    tall_shape = (BX * CY, BX * 16)
    heighten = jnp.where(rows_of(tall_shape) // 2 == lanes_of(tall_shape), 1.0, 0.0).astype(BF16)
    tall = jnp.dot(heighten, wide, preferred_element_type=F32)
    for x in range(BX):
        lc[x, cells] = tall[x * CY : (x + 1) * CY]
        lc[x, END : END + 8] = zero_tile
        lys[0, x : x + 1] = tall[x * CY : x * CY + 1]
        lys[1, x : x + 1] = tall[x * CY + CY - 1 : x * CY + CY]
    own_l = []
    for half in range(2):
        packed = zero_tile
        for x in range(6):
            plane = lc[6 * half + x, cells]
            packed = pack_plane(packed, plane, 2 * x)
            packed = pack_plane(packed, plane, 2 * x + 1)
        store_packed(lzs, half, packed)
        own_l.append(packed)
    start("l")

    lane = lanes_of((CY, CZ))
    row = rows_of((CY, CZ))
    load_a.wait()

    def faces(x, fx_low):
        centre = kp[x + 1, cells]
        fx_high = harmonic(centre, kp[x + 2, cells])
        fy_low = harmonic(kp[x + 1, TOP - 1 : END - 1], centre)
        fy[x, 0:CY] = fy_low
        fz_low = jnp.where(lane == 0, 0.0, harmonic(lane_roll(centre, 1), centre))
        fz_high = lane_roll(fz_low, -1)
        fy_high = fy[x, 1 : CY + 1]
        fx[x + 1] = fx_high
        fz[0, x] = fz_low
        fz[1, x] = fz_high
        dg[x] = av[x] + fx_low + fx_high + fy_low + fy_high + fz_low + fz_high
        return fx_high, fy_high, fz_high

    def block_step(block, carry):
        fx_low, cut_below = carry
        x = 2 * block
        fx_mid, fy_high_0, fz_high_0 = faces(x, fx_low)
        fx_high, fy_high_1, fz_high_1 = faces(x + 1, fx_mid)
        wx = quad_sum(fx_high)
        wy = fy_high_0 + fy_high_1
        wy = row_roll(wy + lane_roll(wy, -1), -1)
        wz = fz_high_0 + fz_high_1
        wz = lane_roll(wz + row_roll(wz, -1), -1)
        wa = quad_sum(av[x] + av[x + 1])
        own = lc[block, cells]
        lx = lc[min(block + 1, BX - 1), cells]
        ly = lc[block, TOP + 2 : END + 2]
        lz = lane_roll(own, -2)
        lx = jnp.where(lx == own, -1.0, lx)
        ly = jnp.where((ly == own) | (row >= CY - 2), -1.0, ly)
        lz = jnp.where((lz == own) | (lane >= CZ - 2), -1.0, lz)
        cut_x = jnp.where(lx < 0.0, 0.0, wx)
        cut_y = jnp.where(ly < 0.0, 0.0, wy)
        cut_z = jnp.where(lz < 0.0, 0.0, wz)
        leaving = wa + cut_below + cut_x + cut_y + row_roll(cut_y, 2) + cut_z + lane_roll(cut_z, 2)
        ew[0, block] = squeeze_cells(leaving)
        same = ly == lx
        wx = wx + jnp.where(same, wy, 0.0)
        ly = jnp.where(same, -1.0, ly)
        same = lz == lx
        wx = wx + jnp.where(same, wz, 0.0)
        lz = jnp.where(same, -1.0, lz)
        same = lz == ly
        wy = wy + jnp.where(same, wz, 0.0)
        lz = jnp.where(same, -1.0, lz)
        for n, field in enumerate((own, lx, ly, lz)):
            el[n, block] = squeeze_cells(field)
        for n, field in enumerate((wx, wy, wz)):
            ew[n + 1, block] = squeeze_cells(field)
        return fx_high, cut_x

    below = (zero_plane, zero_plane)
    for block in range(BX):
        below = block_step(block, below)

    number = rows_of((16, CZ)).astype(F32)
    numbers = [(number + 16.0 * q).astype(BF16) for q in range(8)]
    one = jnp.ones((16, CZ), BF16)
    zero = jnp.zeros((16, CZ), BF16)

    def place(at, lhs_label, pairs):
        lhs_label = spread_row(lhs_label)
        spread = []
        for label, weight in pairs:
            high, low = split(weight)
            spread.append((spread_row(label), spread_row(high), spread_row(low)))
        for q in range(8):
            xs[16 * q : 16 * q + 16, at : at + CZ] = jnp.where(lhs_label == numbers[q], one, zero)
            y_high = zero
            y_low = zero
            for label, high, low in spread:
                hit = label == numbers[q]
                y_high = jnp.where(hit, high, y_high)
                y_low = jnp.where(hit, low, y_low)
            ys[16 * q : 16 * q + 16, at : at + CZ] = y_high
            ys[AGG + 16 * q : AGG + 16 * q + 16, at : at + CZ] = y_low

    acc[...] = jnp.zeros((AGG, 2 * AGG), F32)

    def own_step(block, carry):
        for m in range(8):
            at = slice(4 * m, 4 * m + 1)
            pairs = [(el[n, block, at], ew[n, block, at]) for n in range(1, 4)]
            place(m * CZ, el[0, block, at], pairs)
        acc[...] += lax.dot_general(xs[...], ys[...], NT, preferred_element_type=F32)
        return carry

    lax.fori_loop(0, OWN_1, own_step, 0)
    load_b.wait()
    own_d = []
    own_b = []
    for half in range(2):
        packed_d = zero_tile
        packed_b = zero_tile
        for local in range(12):
            packed_d = pack_plane(packed_d, dg[12 * half + local], local)
            packed_b = pack_plane(packed_b, bv[12 * half + local], local)
        own_d.append(packed_d)
        own_b.append(packed_b)
    finish("k")

    gx[0] = harmonic(kp[1, cells], kxh[0])
    gx[1] = harmonic(kp[CX, cells], kxh[1])
    for half in range(2):
        face_z = safe_harmonic(own_k[half], joined(kzh, half))
        fze[half] = face_z
        diag = own_d[half] + face_z
        for local in range(12):
            x = 12 * half + local
            low = harmonic(kp[x + 1, TOP : TOP + 8], kyh[0, x])
            high = harmonic(kp[x + 1, END - 8 : END], kyh[1, x])
            gy[0, x] = low
            gy[1, x] = high
            diag = diag + lane_roll(jnp.where(rim, low, 0.0), 8 * local)
            diag = diag + lane_roll(jnp.where(rim, high, 0.0), 8 * local + 6)
        diag = pack_plane(diag, gx[half], 11 * half)
        first = OMEGA_FINE * own_b[half] / jnp.where(diag > 0.0, diag, 1.0)
        store_packed(zs.at[0], half, first)
    start("v", 0, (4, 5))

    def first_part(x, g):
        at = slice(8 * g, 8 * g + 8)
        wall = jnp.where(rim, lane_roll(fze[x // 12], -2 * (4 * (x % 12) + g)), 0.0)
        gz[x, at] = wall
        diag = dg[x, at] + wall
        if g == 0:
            diag = diag + gy[0, x]
        if g == 3:
            diag = diag + gy[1, x]
        if x == 0:
            diag = diag + gx[0, at]
        if x == CX - 1:
            diag = diag + gx[1, at]
        scale = OMEGA_FINE / diag
        first = scale * bv[x, at]
        dg[x, at] = diag
        sc[x, at] = scale
        c0[x, at] = first
        v[0, x + 1, TOP + 8 * g : TOP + 8 * g + 8] = first

    for x in range(CX):
        for g in (range(4) if x in (0, CX - 1) else (0, 3)):
            first_part(x, g)
    start("v", 0, (2, 3, 0, 1))
    for x in range(1, CX - 1):
        for g in (1, 2):
            first_part(x, g)

    def face_rows(block, carry):
        x = 2 * block
        low = (gy[0, x] + gy[0, x + 1])[0:1]
        high = (gy[1, x] + gy[1, x + 1])[7:8]
        wyf[0, pl.ds(block, 1)] = low + lane_roll(low, -1)
        wyf[1, pl.ds(block, 1)] = high + lane_roll(high, -1)
        return carry

    lax.fori_loop(0, BX, face_rows, 0, unroll=True)
    wxf = [quad_sum(gx[side]) for side in range(2)]

    def scale_step(turn, carry):
        for local in range(4):
            x = 4 * turn + local
            scale = sc[x]
            gw[0, x] = scale * fx[x]
            gw[1, x] = scale * fx[x + 1]
            gw[2, x] = scale * fy[x, 0:CY]
            gw[3, x] = scale * fy[x, 1 : CY + 1]
            gw[4, x] = scale * fz[0, x]
            gw[5, x] = scale * fz[1, x]
            gz[x] = scale * gz[x]
            gy[0, x] = scale[0:8] * gy[0, x]
            gy[1, x] = scale[CY - 8 :] * gy[1, x]
        return carry

    lax.fori_loop(0, CX // 4, scale_step, 0)
    gx[0] = sc[0] * gx[0]
    gx[1] = sc[CX - 1] * gx[1]

    def pack_scale(half, carry):
        packed = zero_tile
        for local in range(12):
            packed = pack_plane(packed, gz[12 * half + local], local)
        gzp[half] = packed
        return carry

    lax.fori_loop(0, 2, pack_scale, 0)

    def inner(slot):
        def step(half, carry):
            packed = zero_tile
            for local in range(12):
                x = 12 * half + local
                centre = v[slot, x + 1, cells]
                total = c0[x] + (1.0 - OMEGA_FINE) * centre
                total = total + gw[0, x] * v[slot, x, cells] + gw[1, x] * v[slot, x + 2, cells]
                total = total + gw[2, x] * v[slot, x + 1, TOP - 1 : END - 1]
                total = total + gw[3, x] * v[slot, x + 1, TOP + 1 : END + 1]
                total = total + gw[4, x] * lane_roll(centre, 1) + gw[5, x] * lane_roll(centre, -1)
                tp[x] = total
                packed = pack_plane(packed, total, local)
            zp[half] = packed
            return carry

        lax.fori_loop(0, 2, step, 0)

    def outer_faces(slot, other):
        for half in range(2):
            halo_z = joined(zh.at[slot], half)
            hz[half] = halo_z
            packed = zp[half] + gzp[half] * halo_z
            for local in range(12):
                x = 12 * half + local
                low = jnp.where(rim, gy[0, x] * yh[slot, 0, x], 0.0)
                high = jnp.where(rim, gy[1, x] * yh[slot, 1, x], 0.0)
                packed = packed + lane_roll(low, 8 * local) + lane_roll(high, 8 * local + 6)
            if half == 0:
                packed = pack_plane(packed, gx[0] * xh[slot, 0], 0)
            else:
                packed = pack_plane(packed, gx[1] * xh[slot, 1], 11)
            store_packed(zs.at[other], half, packed)

    def finished(slot, x, g):
        at = slice(8 * g, 8 * g + 8)
        wall = lane_roll(hz[x // 12], -2 * (4 * (x % 12) + g))
        new = tp[x, at] + gz[x, at] * wall
        if g == 0:
            new = new + gy[0, x] * yh[slot, 0, x]
        if g == 3:
            new = new + gy[1, x] * yh[slot, 1, x]
        if x == 0:
            new = new + gx[0, at] * xh[slot, 0, at]
        if x == CX - 1:
            new = new + gx[1, at] * xh[slot, 1, at]
        return new

    def outer_edges(slot, other):
        for x in range(CX):
            for g in (range(4) if x in (0, CX - 1) else (0, 3)):
                v[other, x + 1, TOP + 8 * g : TOP + 8 * g + 8] = finished(slot, x, g)

    def outer_middle(other):
        for x in range(1, CX - 1):
            for g in (1, 2):
                v[other, x + 1, TOP + 8 * g : TOP + 8 * g + 8] = finished(None, x, g)

    wanted = rows_of((AGG, CZ)).astype(F32)

    def gather_row(sums, label, value):
        label = jnp.broadcast_to(label, (AGG, CZ))
        return sums + jnp.where(label == wanted, jnp.broadcast_to(value, (AGG, CZ)), 0.0)

    def restrict_step(block, sums):
        for m in range(8):
            at = slice(4 * m, 4 * m + 1)
            sums = gather_row(sums, el[0, block, at], ew[0, block, at])
        return sums

    def aggregate_row(sums):
        high, low = split(sums)
        ones = jnp.ones((16, CZ), BF16)
        out = lax.dot_general(ones, high.astype(BF16), NT, preferred_element_type=F32)
        return (out + lax.dot_general(ones, low.astype(BF16), NT, preferred_element_type=F32))[0:8]

    inner(0)
    lax.fori_loop(OWN_1, OWN_2, own_step, 0)

    finish("v", 0)
    outer_faces(0, 1)
    start("v", 1, (4, 5))
    outer_edges(0, 1)
    start("v", 1, (2, 3, 0, 1))
    outer_middle(1)

    diag_sums = lax.fori_loop(0, BX, restrict_step, jnp.zeros((AGG, CZ), F32))
    finish("l")

    def pair_rows(values):
        return jnp.where((lanes_of(values.shape) & 1) == 0, values, lane_roll(row_roll(values, -1), 1))

    def face_blocks(halves, side, summed):
        out = []
        for values in halves:
            if side:
                values = lane_roll(values, 1)
            if summed:
                values = values + lane_roll(values, -8)
                values = values + row_roll(values, -1)
            out.append(jnp.where((lane_8 & 8) == 0, values, lane_roll(row_roll(values, -2), 8)))
        out = jnp.where(odd, lane_roll(out[1], 1), out[0])
        return jnp.where(lane_8 < 96, out, 0.0) if summed else out

    faces_of = []
    for side in range(2):
        faces_of.append((side, squeeze_cells(lxh[side]), squeeze_cells(lc[side * (BX - 1), cells]),
                         squeeze_cells(wxf[side]), range(0, CY, 4)))
        faces_of.append((2 + side, pair_rows(lyh[side]), pair_rows(lys[side]), pair_rows(wyf[side]), range(0, BX, 2)))
        peers = [joined(lzh, half) for half in range(2)]
        faces_of.append((4 + side, face_blocks(peers, side, False), face_blocks(own_l, side, False),
                         face_blocks([fze[0], fze[1]], side, True), (0, 4)))

    for d, peer, own, weight, at_rows in faces_of:
        for n, r in enumerate(at_rows):
            at = slice(r, r + 1)
            place(n * CZ, peer[at], [(own[at], weight[at])])
        depth = len(at_rows) * CZ
        tile = lax.dot_general(xs[:, :depth], ys[:, :depth], NT, preferred_element_type=F32)
        mf[AGG * d : AGG * (d + 1)] = tile[:, :AGG] + tile[:, AGG:]
        for r in at_rows:
            diag_sums = gather_row(diag_sums, own[r : r + 1], weight[r : r + 1])

    coarse_scale = OMEGA_COARSE / aggregate_row(diag_sums)

    def store_tile(t, tile):
        high, low = split(tile * coarse_scale[0:1])
        mm[AGG * t : AGG * (t + 1), :AGG] = high.astype(BF16)
        mm[AGG * t : AGG * (t + 1), AGG:] = low.astype(BF16)

    for d in range(6):
        store_tile(d + 1, mf[AGG * d : AGG * (d + 1)])

    inner(1)

    def residual_step(turn, carry):
        for local in range(4):
            block = 4 * turn + local
            total = zero_plane
            for x in (2 * block, 2 * block + 1):
                total = total + dg[x] * (tp[x] - v[1, x + 1, cells])
            ew[0, block] = squeeze_cells(quad_sum(total * (1.0 / OMEGA_FINE)))
        return carry

    lax.fori_loop(0, BX // 4, residual_step, 0)
    sums = lax.fori_loop(0, BX, restrict_step, jnp.zeros((AGG, CZ), F32))

    finish("v", 1)
    halo_z = [fze[half] * joined(zh.at[1], half) for half in range(2)]
    inverse = 1.0 / OMEGA_FINE
    for block in range(BX):
        x = 2 * block
        low = sum(gy[0, n] * yh[1, 0, n] * dg[n, 0:8] for n in (x, x + 1))[0:1]
        high = sum(gy[1, n] * yh[1, 1, n] * dg[n, CY - 8 : CY] for n in (x, x + 1))[7:8]
        rows_y[0, block : block + 1] = inverse * (low + lane_roll(low, -1))
        rows_y[1, block : block + 1] = inverse * (high + lane_roll(high, -1))
    for side in range(2):
        plane = gx[side] * xh[1, side] * dg[side * (CX - 1)] * inverse
        values = (squeeze_cells(quad_sum(plane)), pair_rows(rows_y[side]), face_blocks(halo_z, side, True))
        for (d, peer, own, weight, at_rows), value in zip(faces_of[3 * side : 3 * side + 3], values):
            for r in at_rows:
                sums = gather_row(sums, own[r : r + 1], value[r : r + 1])
    first_correction = coarse_scale * aggregate_row(sums)

    def halves(values):
        high, low = split(values)
        return jnp.concatenate([high, low], axis=0).astype(BF16)

    def both(values):
        values = values[:, :AGG] + values[:, AGG:]
        return values[0:8] + values[8:16]

    def coarse_step(turn, correction, first=False):
        slot = turn % 2
        cs[slot] = correction
        start("c", slot)
        if first:
            lax.fori_loop(OWN_2, BX, own_step, 0)
            sum_own = acc[:, :AGG] + acc[:, AGG:]
            store_tile(0, sum_own + sum_own.T)
        image = jnp.dot(halves(correction), mm[0:AGG], preferred_element_type=F32)
        base = (1.0 - OMEGA_COARSE) * correction + first_correction
        base = base + both(image)
        finish("c", slot)
        beside = jnp.concatenate([jnp.broadcast_to(ch[slot, d, 0:1], (8, CZ)) for d in range(6)], axis=1)
        return base + both(jnp.dot(halves(beside), mm[AGG:], preferred_element_type=F32))

    correction = coarse_step(0, first_correction, True)
    for turn in range(1, KC - 1):
        correction = coarse_step(turn, correction)

    def lift_step(half, carry):
        packed = zero_tile
        for local in range(6):
            block = 6 * half + local
            index = lc[block, cells].astype(jnp.int32)
            lifted = jnp.concatenate(
                [jnp.take_along_axis(correction, index[8 * g : 8 * g + 8], axis=1, mode="promise_in_bounds")
                 for g in range(4)], axis=0)
            for n in range(2):
                x = 2 * block + n
                new = v[1, x + 1, cells] + lifted
                v[1, x + 1, cells] = new
                packed = pack_plane(packed, new, 2 * local + n)
        store_packed(zs.at[1], half, packed)
        return carry

    lax.fori_loop(0, 2, lift_step, 0)

    start("v", 1)
    for turn in range(POST):
        slot = 1 - turn % 2
        if turn:
            finish_send("v", 1 - slot)
        inner(slot)
        finish_recv("v", slot)
        if turn < POST - 1:
            outer_faces(slot, 1 - slot)
            start("v", 1 - slot, (4, 5))
            outer_edges(slot, 1 - slot)
            start("v", 1 - slot, (2, 3, 0, 1))
            outer_middle(1 - slot)
    finish_send("v", 0)
    for half in range(2):
        hz[half] = joined(zh.at[0], half)
    for x in range(CX):
        for g in range(4):
            out[x, 8 * g : 8 * g + 8] = finished(0, x, g)


def body(right_side, conductance, absorption, block_agg):
    field = (CX, CY, CZ)
    padded = (CX + 2, CY + 16, CZ)
    any_spec = pl.BlockSpec(memory_space=pl.ANY)

    def f32(*shape):
        return pltpu.VMEM(shape, F32)

    scratch = dict(
        bv=f32(*field), av=f32(*field), kp=f32(*padded), lv=pltpu.VMEM((BX, CY // 2, CZ // 2), jnp.int32),
        v=f32(2, *padded), gw=f32(6, *field), c0=f32(*field), dg=f32(*field), sc=f32(*field),
        fx=f32(CX + 1, CY, CZ), fy=f32(CX, CY + 8, CZ), fz=f32(2, *field),
        gz=f32(*field), gy=f32(2, CX, 8, CZ), gx=f32(2, CY, CZ),
        lc=f32(BX, CY + 16, CZ), el=f32(4, BX, CY, CZ), ew=f32(4, BX, CY, CZ),
        kxh=f32(2, CY, CZ), kyh=f32(2, CX, 8, CZ), kzs=f32(2, 2, 8, CZ), kzh=f32(2, 2, 8, CZ),
        lxh=f32(2, CY, CZ), lys=f32(2, 16, CZ), lyh=f32(2, 16, CZ), lzs=f32(2, 2, 8, CZ), lzh=f32(2, 2, 8, CZ),
        xh=f32(2, 2, CY, CZ), yh=f32(2, 2, CX, 8, CZ), zs=f32(2, 2, 2, 8, CZ), zh=f32(2, 2, 2, 8, CZ),
        fze=f32(2, 8, CZ), wyf=f32(2, 16, CZ), rows_y=f32(2, 16, CZ), zp=f32(2, 8, CZ), gzp=f32(2, 8, CZ), hz=f32(2, 8, CZ), tp=f32(*field),
        xs=pltpu.VMEM((AGG, 8 * CZ), BF16), ys=pltpu.VMEM((2 * AGG, 8 * CZ), BF16),
        acc=f32(AGG, 2 * AGG), mf=f32(6 * AGG, AGG), mm=pltpu.VMEM((7 * AGG, 2 * AGG), BF16),
        cs=f32(2, 8, CZ), ch=f32(2, 6, 8, CZ),
    )
    return pl.pallas_call(
        kernel,
        out_shape=pltpu.VMEM(field, F32),
        in_specs=[any_spec] * 4,
        out_specs=pl.BlockSpec(memory_space=pltpu.VMEM),
        scratch_shapes=list(scratch.values()) + [
            pltpu.SemaphoreType.DMA((4,)), pltpu.SemaphoreType.DMA((6, 6)), pltpu.SemaphoreType.DMA((6, 6)),
        ],
        compiler_params=pltpu.CompilerParams(collective_id=0, has_side_effects=True),
    )(right_side, conductance, absorption, block_agg)


def solution(mesh):
    spec = P("gx", "gy", "gz")
    return jax.shard_map(body, mesh=mesh, in_specs=(spec,) * 4, out_specs=spec, check_vma=False)
```
